32 devices in a mesh: layer: 2 (over x), expert: 4 (over y, core), col: 4 (over z).
Axes of the slice: x: 2, y: 2, z: 4, core: 2. Of those that a mesh axis runs over, the one named last changes fastest.
Arguments:
- target_weights: bfloat16 [8, 7168, 2048], P(('layer', 'expert'), None, 'col'), parts along dimension 0, may hold values from -36 to 36
- factors: float32 [8, 7168, 128], P(('layer', 'expert'), 'col'), parts along dimension 0, may hold values from -0.5 to 0.5
- bases: float32 [64, 128, 2048], P('layer', None, 'col'), parts along dimension 0, may hold values from -6 to 6
- coefficients: float32 [8, 32], P(('layer', 'expert')), parts along dimension 0, may hold values from -1 to 1
Outputs:
- new_factors: float32 [8, 7168, 128], P(('layer', 'expert'), 'col'), parts along dimension 0
- new_bases: float32 [64, 128, 2048], P('layer', None, 'col'), parts along dimension 0
- new_coefficients: float32 [8, 32], P(('layer', 'expert')), parts along dimension 0
- losses: float32 [4], P('layer'), parts along dimension 0
The draws below stay inside these ranges and needn't reach their ends.
There are 2 independent parts, one for each index of `layer`. The reference program is written for one: setup_inputs(seed, part) draws one part's arguments, and reference() takes and returns one part's arrays. A program takes and returns all parts, laid end to end along the dimension named above; each array names one. Nothing has to cross between parts.
All inputs are finite; a program needn't handle non-finite values.
Results may differ from the reference program's by a relative error of at most 0.0003.
Values sent between devices are 32-bit elements; how exact they have to be, the bound alone decides.
A program may use at most 128 MiB of HBM per device.

```python
import jax
import jax.numpy as jnp
from jax import lax

D = 7168
H = 2048
R = 128
K = 32
ITERS = 2
EXPERTS = 4


def draw_target_weights(key, part):
    keys = jax.random.split(key, 2)
    values = jnp.clip(jax.random.normal(keys[0], (EXPERTS, D, H), jnp.float32), -4.0, 4.0)
    expert_pos = jnp.arange(EXPERTS, dtype=jnp.float32) / (EXPERTS - 1)
    column_pos = jnp.arange(H, dtype=jnp.float32) / (H - 1)
    expert_scale = jnp.sqrt(1.0 + 2.0 * expert_pos)
    column_scale = jnp.sqrt(1.0 + 2.0 * column_pos) * jax.random.uniform(keys[1], (H,), jnp.float32, 0.7, 1.4)
    values = values * expert_scale[:, None, None] * column_scale[None, None, :]
    return values.astype(jnp.bfloat16)


def shard_levels(stream_key, shape, cuts, smallest, high):
    level = 1.0
    for dim, shards_of in cuts:
        heights = jax.random.uniform(jax.random.fold_in(jax.random.fold_in(stream_key, 6), dim), (shards_of,), jnp.float32, smallest / len(cuts), high / len(cuts))
        level = level * jnp.repeat(jnp.exp(heights), shape[dim] // shards_of).reshape((-1,) + (1,) * (len(shape) - 1 - dim))
    return level


def noise(key, dims, scale, reach, cuts=(), held_as=jnp.bfloat16):
    gain = shard_levels(key, dims, cuts, -0.22, 0.18) if cuts else 1.0
    result = jax.random.normal(key, dims, jnp.float32) * scale * gain
    return jnp.minimum(jnp.maximum(result, -reach), reach).astype(held_as)


def setup_inputs(seed: int = 0, part: int = 0) -> dict:
    key_list = jax.random.split(jax.random.key(seed), 5)
    part_keys = jax.random.split(jax.random.fold_in(key_list[4], part), 5)
    target_weights = draw_target_weights(jax.random.fold_in(jax.random.fold_in(key_list[4], part), 71), part)
    factors = noise(part_keys[1], (EXPERTS, D, R), R ** -0.5, 0.5, ((0, 4), (1, 4)), jnp.float32)
    bases = noise(part_keys[2], (K, R, H), 1.0, 6.0, ((2, 4),), jnp.float32)
    coefficients = noise(part_keys[3], (EXPERTS, K), K ** -0.5, 1.0, ((0, 4),), jnp.float32)
    return {"target_weights": target_weights, "factors": factors, "bases": bases, "coefficients": coefficients}


LEARN_RATE = 0.01
BETA_ONE = 0.9
BETA_TWO = 0.999
EPSILON = 0.0001
HIGHEST = lax.Precision.HIGHEST

def adam_update(parameter, gradient, moment_one, moment_two, iteration):
    moment_one = BETA_ONE * moment_one + (1.0 - BETA_ONE) * gradient
    moment_two = BETA_TWO * moment_two + (1.0 - BETA_TWO) * gradient * gradient
    first_hat = moment_one / (1.0 - BETA_ONE ** (iteration + 1))
    second_hat = moment_two / (1.0 - BETA_TWO ** (iteration + 1))
    parameter = parameter - LEARN_RATE * first_hat / (jnp.sqrt(second_hat) + EPSILON)
    return (parameter, moment_one, moment_two)

def expert_terms(operands):
    factor, mixed, target = operands
    residual = jnp.dot(factor, mixed, precision=HIGHEST) - target.astype(jnp.float32)
    loss_part = jnp.sum(residual * residual)
    gradient = residual / H
    d_factor = jnp.dot(gradient, mixed.T, precision=HIGHEST)
    d_mixed = jnp.dot(factor.T, gradient, precision=HIGHEST)
    return (loss_part, d_factor, d_mixed)

def reference(target_weights, factors, bases, coefficients):
    factor_one = jnp.zeros_like(factors)
    factor_two = jnp.zeros_like(factors)
    basis_one = jnp.zeros_like(bases)
    basis_two = jnp.zeros_like(bases)
    coef_one = jnp.zeros_like(coefficients)
    coef_two = jnp.zeros_like(coefficients)
    loss_list = []
    for iteration in range(ITERS):
        mixed = jnp.tanh(jnp.einsum('ek,krh->erh', coefficients, bases, precision=HIGHEST))
        loss_parts, d_factors, d_mixed = lax.map(expert_terms, (factors, mixed, target_weights))
        loss_list.append(jnp.sum(loss_parts) * (1.0 / (2.0 * EXPERTS * D * H)))
        d_pre = d_mixed * (1.0 - mixed * mixed)
        d_bases = jnp.einsum('ek,erh->krh', coefficients, d_pre, precision=HIGHEST)
        d_coef = jnp.einsum('krh,erh->ek', bases, d_pre, precision=HIGHEST)
        factors, factor_one, factor_two = adam_update(factors, d_factors, factor_one, factor_two, iteration)
        bases, basis_one, basis_two = adam_update(bases, d_bases, basis_one, basis_two, iteration)
        coefficients, coef_one, coef_two = adam_update(coefficients, d_coef, coef_one, coef_two, iteration)
    return (factors, bases, coefficients, jnp.stack(loss_list))
```

```python
import functools

import jax
import jax.numpy as jnp
from jax import lax
from jax.experimental import pallas as pl
from jax.experimental.pallas import tpu as pltpu
from jax.sharding import PartitionSpec as P

LEARN_RATE = 0.01
BETA_ONE = 0.9
BETA_TWO = 0.999
EPSILON = 0.0001
HIGHEST = lax.Precision.HIGHEST
MESH = pl.DeviceIdType.MESH
F32 = jnp.float32
BF16 = jnp.bfloat16
LAG = 3
SEMS = 16
GROUPS = 4


def adam_first(parameter, g):
    return parameter - LEARN_RATE * g / (jnp.abs(g) + EPSILON)


def adam_second(parameter, g_one, g_two):
    first = (BETA_ONE * (1.0 - BETA_ONE) * g_one + (1.0 - BETA_ONE) * g_two) * (1.0 / (1.0 - BETA_ONE**2))
    second = (
        BETA_TWO * (1.0 - BETA_TWO) * g_one * g_one + (1.0 - BETA_TWO) * g_two * g_two
    ) * (1.0 / (1.0 - BETA_TWO**2))
    return parameter - LEARN_RATE * first / (jnp.sqrt(second) + EPSILON)


def pieces(x):
    upper = x.astype(BF16)
    return upper, (x - upper.astype(F32)).astype(BF16)


def contract(a, b, dims):
    return lax.dot_general(a, b, (dims, ((), ())), preferred_element_type=F32)


def diagonal(size):
    shape = (size, 128)
    return lax.broadcasted_iota(jnp.int32, shape, 0) == lax.broadcasted_iota(jnp.int32, shape, 1)


def to_lanes(column):
    return jnp.sum(jnp.where(diagonal(column.shape[0]), column, 0.0), axis=0, keepdims=True)


def to_rows(row, size):
    held = jnp.where(diagonal(size), jnp.broadcast_to(row, (size, 128)), 0.0)
    return jnp.broadcast_to(jnp.sum(held, axis=1, keepdims=True), (size, 128))


def chunk_count(rows):
    for count in (4, 2):
        if rows % (16 * count) == 0:
            return count
    return 1


def kernel(
    n, experts, loss_scale, t_hbm, f_hbm, b_hbm, c_in, f_out, b_out, misc_out,
    target, bases, b_grad, full, part, landed, d_pre, c_one, c_two, coef_acc, message, loss_in, g_one, gram_sum,
    mixed, tall, loss_sum, gram_own, gram_in, gram_go,
    load_sem, out_sem, z_send, z_recv, gram_send, gram_recv, ex_send, ex_recv, co_send, co_recv,
):
    me = lax.axis_index("col")
    mine = lax.axis_index("expert")
    rows, r = f_hbm.shape
    d, hl = target.shape
    k_count = bases.shape[0]
    scale = 1.0 / (hl * n)
    table = experts * k_count
    block = min(table, 128)
    blocks = table // block
    chunks = chunk_count(rows)
    ch = rows // chunks
    phase = n * chunks
    group = k_count // GROUPS

    loads = [
        pltpu.make_async_copy(f_hbm, full.at[0, pl.ds(pl.multiple_of(me * rows, 16), rows)], load_sem.at[0]),
        pltpu.make_async_copy(b_hbm, bases, load_sem.at[1]),
    ]
    for j in range(n):
        at = pl.ds(j * rows, rows)
        loads.append(pltpu.make_async_copy(t_hbm.at[at], target.at[at], load_sem.at[2 + j]))
    for load in loads:
        load.start()
    barrier = pltpu.get_barrier_semaphore()
    for off in range(1, n):
        pl.semaphore_signal(barrier, inc=1, device_id={"col": lax.rem(me + off, n)}, device_id_type=MESH)
    for off in range(1, experts):
        pl.semaphore_signal(barrier, inc=1, device_id={"expert": lax.rem(mine + off, experts)}, device_id_type=MESH)
    pl.semaphore_wait(barrier, n + experts - 2)

    def place_of(way):
        return me if way == 0 else n - 1 - me

    def shard_at(way, place):
        return place if way == 0 else n - 1 - place

    def split(s):
        it = s // phase
        u = s - it * phase
        b = u // chunks
        return it, b, u - b * chunks

    def z_copy(way, s, src, dst):
        return pltpu.make_async_remote_copy(
            src_ref=src, dst_ref=dst, send_sem=z_send.at[way, s % SEMS], recv_sem=z_recv.at[way, s % SEMS],
            device_id={"col": me + 1 - 2 * way}, device_id_type=MESH,
        )

    def rows_of(shard, c):
        return pl.ds(pl.multiple_of(shard * rows + c * ch, 16), ch)

    def chunk_of(c):
        return pl.ds(pl.multiple_of(c * ch, 16), ch)

    def gather_copy(way, s, shard):
        it, b, c = split(s)
        ref = full.at[it, rows_of(shard, c)]
        return z_copy(way, s, ref, ref)

    def scatter_copy(way, s, shard):
        it, b, c = split(s)
        return z_copy(way, s, part.at[shard, chunk_of(c)], landed.at[way, b - 1, chunk_of(c)])

    def on_send(way, s, act):
        it, b, c = split(s)
        p = place_of(way)

        @pl.when((p < n - 1) & (b <= p))
        def _():
            act(gather_copy(way, s, shard_at(way, p - b)))

        @pl.when((p < n - 1) & (b > p))
        def _():
            act(scatter_copy(way, s, shard_at(way, n + p - b)))

    def arrive(way, s):
        it, b, c = split(s)
        p = place_of(way)

        @pl.when((p > 0) & (b <= p - 1))
        def _():
            gather_copy(way, s, shard_at(way, p - 1 - b)).wait_recv()

        @pl.when((p > 0) & (b > p - 1))
        def _():
            shard = shard_at(way, n + p - 1 - b)
            scatter_copy(way, s, shard).wait_recv()
            at = chunk_of(c)
            part[shard, at, :] = part[shard, at, :] + landed[way, b - 1, at, :]

    def step(s, first=False, last=False):
        if not first:
            for way in range(2):
                on_send(way, s - LAG, lambda copy: copy.wait_send())
            for way in range(2):
                arrive(way, s - LAG)
        if not last:
            for way in range(2):
                on_send(way, s, lambda copy: copy.start())

    def gram_copy(it, way):
        return pltpu.make_async_remote_copy(
            src_ref=gram_go.at[it, way], dst_ref=gram_in.at[it, way], send_sem=gram_send.at[it, way],
            recv_sem=gram_recv.at[it, way], device_id={"col": me + 1 - 2 * way}, device_id_type=MESH,
        )

    def gram_hop(it, s, start):
        for way in range(2):
            p = place_of(way)
            now = s == start + p * LAG

            @pl.when(now & (p > 0))
            def _():
                gram_copy(it, way).wait_recv()

            @pl.when(now & (p == 0) & (p < n - 1))
            def _():
                gram_go[it, way] = gram_own[...]

            @pl.when(now & (p > 0) & (p < n - 1))
            def _():
                gram_go[it, way] = gram_own[...] + gram_in[it, way]

            @pl.when(now & (p < n - 1))
            def _():
                gram_copy(it, way).start()

    def gram_close(it):
        for way in range(2):
            p = place_of(way)

            @pl.when(p > 0)
            def _():
                gram_own[...] = gram_own[...] + gram_in[it, way]

            @pl.when(p < n - 1)
            def _():
                gram_copy(it, way).wait_send()

    def expert_copy(ref, kind, off):
        place = ref.at[mine]
        return pltpu.make_async_remote_copy(
            src_ref=place, dst_ref=place, send_sem=ex_send.at[kind, off - 1], recv_sem=ex_recv.at[kind, off - 1],
            device_id={"expert": lax.rem(mine + off, experts)}, device_id_type=MESH,
        )

    def expert_start(ref, kind):
        for off in range(1, experts):
            expert_copy(ref, kind, off).start()

    def expert_wait(ref, kind):
        for off in range(1, experts):
            expert_copy(ref, kind, off).wait()

    def coef_copy(it, off):
        place = message.at[it, me]
        return pltpu.make_async_remote_copy(
            src_ref=place, dst_ref=place, send_sem=co_send.at[it, off - 1], recv_sem=co_recv.at[it, off - 1],
            device_id={"col": lax.rem(me + off, n)}, device_id_type=MESH,
        )

    def mix(c_ref):
        for q in range(0, hl, 128):
            def add(k, total):
                return total + c_ref[mine, pl.ds(k, 1), :] * bases[k, :, q : q + 128]

            value = jnp.tanh(lax.fori_loop(0, k_count, add, jnp.zeros((r, 128), F32), unroll=4))
            mixed[:, q : q + 128] = value
            upper, lower = pieces(value)
            for i in range(2):
                tall[2 * i * r : (2 * i + 1) * r, q : q + 128] = upper
                tall[(2 * i + 1) * r : (2 * i + 2) * r, q : q + 128] = lower

    def gram_local():
        cut = tall[: 2 * r, :]
        both = contract(cut, cut, ((1,), (1,)))
        both = both[:r] + both[r:]
        gram_own[...] = both[:, :r] + both[:, r:]

    def project(j):
        def one(c, carry):
            value = contract(target[rows_of(j, c), :], tall[: 2 * r, :], ((1,), (1,)))
            part[j, chunk_of(c), :] = value[:, :r] + value[:, r:]
            return carry

        lax.fori_loop(0, chunks, one, 0)

    def absorb(it, shard, c):
        at = rows_of(shard, c)
        cut = jnp.concatenate(pieces(full[it, at, :]), axis=1)
        gram_sum[...] += contract(cut, jnp.concatenate([target[at, :], cut], axis=1), ((0,), (0,)))

    def loss_add(it, shard, c):
        at = rows_of(shard, c)
        one, two = pieces(full[it, at, :])
        wide = jnp.concatenate([one, one, two, two], axis=1)
        residual = contract(wide, tall[...], ((1,), (0,))) - target[at, :].astype(F32)
        loss_sum[...] += jnp.sum((residual * residual).reshape(ch // 8, 8, hl), axis=0)

    def arrived(way, s):
        it, b, c = split(s)
        p = place_of(way)
        return (p > 0) & (b <= p - 1), shard_at(way, p - 1 - b), c

    def for_arrived(act, it, s, own):
        first, first_shard, c = arrived(0, s)
        second, second_shard, _ = arrived(1, s)

        def one(i, carry):
            valid = jnp.where(i == 0, first, jnp.where(i == 1, second, own))
            shard = jnp.where(i == 0, first_shard, jnp.where(i == 1, second_shard, me))

            @pl.when(valid)
            def _():
                act(it, shard, c)

            return carry

        lax.fori_loop(0, 3, one, 0)

    def pre_gradient(it):
        total = gram_sum[:r, :] + gram_sum[r:, :]
        gram = total[:, hl : hl + r] + total[:, hl + r :]
        now = mixed[...]
        d_mixed = jnp.dot(gram, now, precision=HIGHEST, preferred_element_type=F32) - total[:, :hl]
        d_pre[it, mine] = d_mixed * scale * (1.0 - now * now)

    def loss_close(it):
        total = loss_sum[:, 0:128]
        for q in range(128, hl, 128):
            total = total + loss_sum[:, q : q + 128]
        loss_in[mine, it * 8 : it * 8 + 8, :] = total
        loss_sum[...] = jnp.zeros_like(loss_sum)

    def combine(c_ref, it, k, q):
        total = c_ref[0, pl.ds(k, 1), :] * d_pre[it, 0, :, q : q + 128]
        for e in range(1, experts):
            total = total + c_ref[e, pl.ds(k, 1), :] * d_pre[it, e, :, q : q + 128]
        return total

    def coef_pass(it):
        def one(k, carry):
            sums = [jnp.zeros((8, 128), F32)] * experts
            for q in range(0, hl, 128):
                values = bases[k, :, q : q + 128]
                for e in range(experts):
                    held = values * d_pre[it, e, :, q : q + 128]
                    sums[e] = sums[e] + jnp.sum(held.reshape(r // 8, 8, 128), axis=0)
            for e in range(experts):
                coef_acc[pl.ds(e * k_count + k, 1), :] = jnp.sum(sums[e], axis=0, keepdims=True)
            return carry

        lax.fori_loop(0, k_count, one, 0)

    def coef_send(it, losses=None):
        message[it, me] = jnp.zeros(message.shape[2:], F32)
        for i in range(blocks):
            column = jnp.sum(coef_acc[i * block : (i + 1) * block, :], axis=1, keepdims=True)
            message[it, me, i : i + 1, :] = to_lanes(jnp.broadcast_to(column, (block, 128)))
        if losses is not None:
            for i in range(2):
                message[it, me, blocks + i : blocks + i + 1, :] = jnp.sum(
                    losses[i * 8 : i * 8 + 8], axis=0, keepdims=True
                )
        for off in range(1, n):
            coef_copy(it, off).start()

    def coef_wait(it):
        for off in range(1, n):
            coef_copy(it, off).wait()

    def message_sum(it):
        total = message[it, 0]
        for c in range(1, n):
            total = total + message[it, c]
        return total

    def coef_table(total):
        held = [to_rows(total[i : i + 1, :], block) for i in range(blocks)]
        held = held[0] if blocks == 1 else jnp.concatenate(held, axis=0)
        return held.reshape(experts, k_count, 128)

    def bases_one(g):
        def one(k, carry):
            for q in range(0, hl, 128):
                gradient = combine(c_one, 0, k, q)
                b_grad[k, :, q : q + 128] = gradient
                bases[k, :, q : q + 128] = adam_first(bases[k, :, q : q + 128], gradient)
            return carry

        lax.fori_loop(g * group, (g + 1) * group, one, 0)

    def bases_copy(g):
        at = pl.ds(g * group, group)
        return pltpu.make_async_copy(bases.at[at], b_out.at[at], out_sem.at[g])

    def bases_two(g):
        def one(k, carry):
            for q in range(0, hl, 128):
                values = bases[k, :, q : q + 128]
                bases[k, :, q : q + 128] = adam_second(values, b_grad[k, :, q : q + 128], combine(c_two, 1, k, q))
            return carry

        lax.fori_loop(g * group, (g + 1) * group, one, 0)
        bases_copy(g).start()

    def factor_gradient(it, c):
        before = full[it, rows_of(me, c), :]
        product = jnp.dot(before, gram_own[...], precision=HIGHEST, preferred_element_type=F32)
        return before, (product - part[me, chunk_of(c), :]) * scale

    def factor_one(c):
        before, g = factor_gradient(0, c)
        g_one[chunk_of(c), :] = g
        full[1, rows_of(me, c), :] = adam_first(before, g)

    def factor_copy(c):
        at = chunk_of(c)
        return pltpu.make_async_copy(g_one.at[at], f_out.at[at], out_sem.at[GROUPS + c])

    def factor_two(c):
        before, g = factor_gradient(1, c)
        at = chunk_of(c)
        g_one[at, :] = adam_second(before, g_one[at, :], g)
        factor_copy(c).start()

    loads[0].wait()
    for s in range(LAG):
        step(s, first=True)
    c_one[mine] = to_rows(c_in[...], k_count)
    expert_start(c_one, 0)
    gram_sum[...] = jnp.zeros_like(gram_sum)
    loss_sum[...] = jnp.zeros_like(loss_sum)
    loads[1].wait()
    mix(c_one)
    gram_local()
    for j in range(n):
        loads[2 + j].wait()
        project(j)
    final = phase - chunks + LAG

    def early(s, carry):
        gram_hop(0, s, LAG)
        step(s)
        own = s - LAG < chunks
        for_arrived(absorb, 0, s - LAG, own)
        for_arrived(loss_add, 0, s - LAG, own)
        return carry

    lax.fori_loop(LAG, final, early, 0)
    pre_gradient(0)
    expert_wait(c_one, 0)
    expert_start(d_pre.at[0], 1)
    gram_close(0)
    loss_close(0)
    gram_sum[...] = jnp.zeros_like(gram_sum)

    def after_first(c):
        step(final + c)
        factor_one(c)
        absorb(1, me, c)

    def base_work(i):
        if i == 0:
            expert_wait(d_pre.at[0], 1)
            coef_pass(0)
            coef_send(0)
        elif i == 1:
            for g in range(GROUPS // 2):
                bases_one(g)
        elif i == 2:
            for g in range(GROUPS // 2, GROUPS):
                bases_one(g)

    done = 0
    for c in range(chunks):
        after_first(c)
        if c >= 1 or chunks == 1:
            base_work(done)
            done += 1
    for i in range(done, 3):
        base_work(i)

    begin = phase + chunks
    for s in range(final + chunks, begin):
        step(s)
        for_arrived(absorb, 1, s - LAG, False)
    coef_wait(0)
    c_two[...] = adam_first(c_one[...], coef_table(message_sum(0)))
    mix(c_two)
    gram_local()
    for j in range(n):
        project(j)

    behind = begin - phase - LAG + 0

    def late(s, carry):
        gram_hop(1, s, begin)
        step(s)
        for_arrived(absorb, 1, s - LAG, False)
        for_arrived(loss_add, 1, s - LAG - behind, False)

        @pl.when(s - begin < chunks)
        def _():
            loss_add(1, me, s - begin)

        return carry

    lax.fori_loop(begin, phase + final, late, 0)
    pre_gradient(1)
    expert_start(d_pre.at[1], 2)
    gram_close(1)
    for s in range(phase + final - LAG - behind, phase + final - LAG):
        for_arrived(loss_add, 1, s, False)
    loss_close(1)
    expert_start(loss_in, 3)

    def after_second(c):
        step(phase + final + c, last=phase + final + c >= 2 * phase)
        factor_two(c)

    after_second(0)
    expert_wait(d_pre.at[1], 2)
    coef_pass(1)
    expert_wait(loss_in, 3)
    losses = loss_in[0]
    for e in range(1, experts):
        losses = losses + loss_in[e]
    coef_send(1, losses)
    g = 0
    for c in range(1, chunks):
        after_second(c)
        if g < GROUPS:
            bases_two(g)
            g += 1
    for i in range(g, GROUPS):
        bases_two(i)
    coef_wait(1)
    total = message_sum(1)
    c_two[...] = adam_second(c_two[...], coef_table(message_sum(0)), coef_table(total))
    misc_out[...] = jnp.zeros_like(misc_out)
    misc_out[0:1, :] = to_lanes(c_two[mine])
    for i in range(2):
        value = jnp.sum(total[blocks + i : blocks + i + 1, :], axis=1, keepdims=True) * loss_scale
        misc_out[1 + i : 2 + i, :] = jnp.broadcast_to(value, (1, 128))
    for c in range(chunks):
        factor_copy(c).wait()
    for i in range(GROUPS):
        bases_copy(i).wait()


def hand_over(b_in, f_in, b_out, f_out, b_held, f_held, sem):
    parts = sem.shape[1] - 1
    size = b_in.shape[0] // parts
    pairs = []
    for i in range(parts):
        at = pl.ds(i * size, size)
        pairs.append((b_in.at[at], b_held.at[at], b_out.at[at]))
    pairs.append((f_in, f_held, f_out))
    ins = [pltpu.make_async_copy(a, b, sem.at[0, i]) for i, (a, b, _) in enumerate(pairs)]
    outs = [pltpu.make_async_copy(b, c, sem.at[1, i]) for i, (_, b, c) in enumerate(pairs)]
    for copy in ins:
        copy.start()
    for i, copy in enumerate(outs):
        ins[i].wait()
        copy.start()
    for copy in outs:
        copy.wait()


def shards(target_weights, factors, bases, coefficients):
    n, experts = lax.axis_size("col"), lax.axis_size("expert")
    _, d, hl = target_weights.shape
    _, rows, r = factors.shape
    k = bases.shape[0]
    chunks = chunk_count(rows)
    anywhere = pl.BlockSpec(memory_space=pl.ANY)
    local = pl.BlockSpec(memory_space=pltpu.VMEM)
    dma = pltpu.SemaphoreType.DMA
    loss_scale = 1.0 / (2.0 * experts * d * hl * n)
    new_factors, new_bases, misc = pl.pallas_call(
        functools.partial(kernel, n, experts, loss_scale),
        out_shape=(
            jax.ShapeDtypeStruct((rows, r), F32),
            jax.ShapeDtypeStruct(bases.shape, F32),
            jax.ShapeDtypeStruct((8, 128), F32),
        ),
        in_specs=[anywhere, anywhere, anywhere, local],
        out_specs=(anywhere, anywhere, local),
        scratch_shapes=[
            pltpu.VMEM((d, hl), BF16),
            pltpu.VMEM(bases.shape, F32),
            pltpu.VMEM(bases.shape, F32),
            pltpu.VMEM((2, d, r), F32),
            pltpu.VMEM((n, rows, r), F32),
            pltpu.VMEM((2, n - 1, rows, r), F32),
            pltpu.VMEM((2, experts, r, hl), F32),
            pltpu.VMEM((experts, k, 128), F32),
            pltpu.VMEM((experts, k, 128), F32),
            pltpu.VMEM((experts * k, 128), F32),
            pltpu.VMEM((2, n, 8, 128), F32),
            pltpu.VMEM((experts, 16, 128), F32),
            pltpu.VMEM((rows, r), F32),
            pltpu.VMEM((2 * r, hl + 2 * r), F32),
            pltpu.VMEM((r, hl), F32),
            pltpu.VMEM((4 * r, hl), BF16),
            pltpu.VMEM((8, hl), F32),
            pltpu.VMEM((r, r), F32),
            pltpu.VMEM((2, 2, r, r), F32),
            pltpu.VMEM((2, 2, r, r), F32),
            dma((2 + n,)),
            dma((GROUPS + chunks,)),
            dma((2, SEMS)),
            dma((2, SEMS)),
            dma((2, 2)),
            dma((2, 2)),
            dma((4, experts - 1)),
            dma((4, experts - 1)),
            dma((2, n - 1)),
            dma((2, n - 1)),
        ],
        compiler_params=pltpu.CompilerParams(
            collective_id=0, has_side_effects=True, vmem_limit_bytes=66000000
        ),
    )(target_weights[0], factors[0], bases, jnp.pad(coefficients, ((0, 0), (0, 128 - k))))
    new_bases, new_factors = pl.pallas_call(
        hand_over,
        out_shape=(
            jax.ShapeDtypeStruct(bases.shape, F32),
            jax.ShapeDtypeStruct((rows, r), F32),
        ),
        in_specs=[anywhere, anywhere],
        out_specs=(anywhere, anywhere),
        scratch_shapes=[pltpu.VMEM(bases.shape, F32), pltpu.VMEM((rows, r), F32), dma((2, 9))],
        compiler_params=pltpu.CompilerParams(vmem_limit_bytes=66000000),
    )(new_bases, new_factors)
    return (new_factors[None], new_bases, misc[0:1, :k], misc[1:3, 0])


def solution(mesh):
    return jax.shard_map(
        shards,
        mesh=mesh,
        in_specs=(
            P(("layer", "expert"), None, "col"),
            P(("layer", "expert"), "col", None),
            P("layer", None, "col"),
            P(("layer", "expert"), None),
        ),
        out_specs=(
            P(("layer", "expert"), "col", None),
            P("layer", None, "col"),
            P(("layer", "expert"), None),
            P("layer"),
        ),
        check_vma=False,
    )
```

```python
import functools

import jax
import jax.numpy as jnp
from jax import lax
from jax.experimental import pallas as pl
from jax.experimental.pallas import tpu as pltpu
from jax.sharding import PartitionSpec as P

LEARN_RATE = 0.01
BETA_ONE = 0.9
BETA_TWO = 0.999
EPSILON = 0.0001
HIGHEST = lax.Precision.HIGHEST
MESH = pl.DeviceIdType.MESH
F32 = jnp.float32
BF16 = jnp.bfloat16
CHUNKS = 4
LAG = 3
VMEM_MAIN = 57000000
VMEM_LAST = 4000000
SEMS = 16


def adam_first(parameter, g):
    return parameter - LEARN_RATE * g / (jnp.abs(g) + EPSILON)


def adam_second(parameter, g_one, g_two):
    first = (BETA_ONE * (1.0 - BETA_ONE) * g_one + (1.0 - BETA_ONE) * g_two) * (1.0 / (1.0 - BETA_ONE**2))
    second = (
        BETA_TWO * (1.0 - BETA_TWO) * g_one * g_one + (1.0 - BETA_TWO) * g_two * g_two
    ) * (1.0 / (1.0 - BETA_TWO**2))
    return parameter - LEARN_RATE * first / (jnp.sqrt(second) + EPSILON)


def pieces(x):
    upper = x.astype(BF16)
    return upper, (x - upper.astype(F32)).astype(BF16)


def contract(a, b, dims):
    return lax.dot_general(a, b, (dims, ((), ())), preferred_element_type=F32)


def diagonal(size):
    shape = (size, 128)
    return lax.broadcasted_iota(jnp.int32, shape, 0) == lax.broadcasted_iota(jnp.int32, shape, 1)


def to_lanes(column):
    return jnp.sum(jnp.where(diagonal(column.shape[0]), column, 0.0), axis=0, keepdims=True)


def to_rows(row, size):
    held = jnp.where(diagonal(size), jnp.broadcast_to(row, (size, 128)), 0.0)
    return jnp.broadcast_to(jnp.sum(held, axis=1, keepdims=True), (size, 128))


def kernel(
    n, experts, loss_scale, t_hbm, f_hbm, b_hbm, c_hbm, f_out, bases, misc,
    target, b_grad, full, part, landed, d_pre, c_one, c_two, coef_acc, message, loss_in, g_one, gram_sum,
    mixed, tall, loss_sum, gram_own, gram_in, gram_go, c_raw,
    load_sem, z_send, z_recv, gram_send, gram_recv, ex_send, ex_recv, pre_send, pre_recv, co_send, co_recv,
):
    me = lax.axis_index("col")
    mine = lax.axis_index("expert")
    rows, r = f_hbm.shape
    d, hl = target.shape
    k_count = bases.shape[0]
    scale = 1.0 / (hl * n)
    table = experts * k_count
    block = min(table, 128)
    blocks = table // block
    chunks = CHUNKS
    ch = rows // chunks
    phase = n * chunks
    quarters = hl // 128
    pairs = experts // 2
    mate = mine + 1 - 2 * lax.rem(mine, 2)

    loads = [
        pltpu.make_async_copy(f_hbm, full.at[0, pl.ds(pl.multiple_of(me * rows, 16), rows)], load_sem.at[0]),
        pltpu.make_async_copy(b_hbm, bases, load_sem.at[1]),
        pltpu.make_async_copy(c_hbm, c_raw, load_sem.at[2]),
    ]
    for j in range(n):
        at = pl.ds(j * rows, rows)
        loads.append(pltpu.make_async_copy(t_hbm.at[at], target.at[at], load_sem.at[3 + j]))
    for load in loads:
        load.start()
    barrier = pltpu.get_barrier_semaphore()
    for off in range(1, n):
        pl.semaphore_signal(barrier, inc=1, device_id={"col": lax.rem(me + off, n)}, device_id_type=MESH)
    for off in range(1, experts):
        pl.semaphore_signal(barrier, inc=1, device_id={"expert": lax.rem(mine + off, experts)}, device_id_type=MESH)
    pl.semaphore_wait(barrier, n + experts - 2)

    def place_of(way):
        return me if way == 0 else n - 1 - me

    def shard_at(way, place):
        return place if way == 0 else n - 1 - place

    def split(s):
        it = s // phase
        u = s - it * phase
        b = u // chunks
        return it, b, u - b * chunks

    def z_copy(way, s, src, dst):
        return pltpu.make_async_remote_copy(
            src_ref=src, dst_ref=dst, send_sem=z_send.at[way, s % SEMS], recv_sem=z_recv.at[way, s % SEMS],
            device_id={"col": me + 1 - 2 * way}, device_id_type=MESH,
        )

    def rows_of(shard, c):
        return pl.ds(pl.multiple_of(shard * rows + c * ch, 16), ch)

    def chunk_of(c):
        return pl.ds(pl.multiple_of(c * ch, 16), ch)

    def gather_copy(way, s, shard):
        it, b, c = split(s)
        ref = full.at[it, rows_of(shard, c)]
        return z_copy(way, s, ref, ref)

    def scatter_copy(way, s, shard):
        it, b, c = split(s)
        return z_copy(way, s, part.at[shard, chunk_of(c)], landed.at[way, b - 1, chunk_of(c)])

    def on_send(way, s, act):
        it, b, c = split(s)
        p = place_of(way)

        @pl.when((p < n - 1) & (b <= p))
        def _():
            act(gather_copy(way, s, shard_at(way, p - b)))

        @pl.when((p < n - 1) & (b > p))
        def _():
            act(scatter_copy(way, s, shard_at(way, n + p - b)))

    def arrive(way, s):
        it, b, c = split(s)
        p = place_of(way)

        @pl.when((p > 0) & (b <= p - 1))
        def _():
            gather_copy(way, s, shard_at(way, p - 1 - b)).wait_recv()

        @pl.when((p > 0) & (b > p - 1))
        def _():
            shard = shard_at(way, n + p - 1 - b)
            scatter_copy(way, s, shard).wait_recv()
            at = chunk_of(c)
            part[shard, at, :] = part[shard, at, :] + landed[way, b - 1, at, :]

    def take(s):
        for way in range(2):
            on_send(way, s - LAG, lambda copy: copy.wait_send())
        for way in range(2):
            arrive(way, s - LAG)

    def give(s):
        for way in range(2):
            on_send(way, s, lambda copy: copy.start())

    def step(s):
        take(s)
        give(s)

    def give_first(s):
        for way in range(2):
            @pl.when(place_of(way) < n - 1)
            def _():
                z_copy(way, s, f_hbm.at[chunk_of(s)], full.at[0, rows_of(me, s)]).start()

    def gram_copy(it, way):
        return pltpu.make_async_remote_copy(
            src_ref=gram_go.at[it, way], dst_ref=gram_in.at[it, way], send_sem=gram_send.at[it, way],
            recv_sem=gram_recv.at[it, way], device_id={"col": me + 1 - 2 * way}, device_id_type=MESH,
        )

    def gram_hop(it, s, start):
        for way in range(2):
            p = place_of(way)
            now = s == start + p * LAG

            @pl.when(now & (p > 0))
            def _():
                gram_copy(it, way).wait_recv()

            @pl.when(now & (p == 0) & (p < n - 1))
            def _():
                gram_go[it, way] = gram_own[...]

            @pl.when(now & (p > 0) & (p < n - 1))
            def _():
                gram_go[it, way] = gram_own[...] + gram_in[it, way]

            @pl.when(now & (p < n - 1))
            def _():
                gram_copy(it, way).start()

    def gram_close(it):
        for way in range(2):
            p = place_of(way)

            @pl.when(p > 0)
            def _():
                gram_own[...] = gram_own[...] + gram_in[it, way]

            @pl.when(p < n - 1)
            def _():
                gram_copy(it, way).wait_send()

    def expert_copy(ref, kind, off):
        place = ref.at[mine]
        return pltpu.make_async_remote_copy(
            src_ref=place, dst_ref=place, send_sem=ex_send.at[kind, off - 1], recv_sem=ex_recv.at[kind, off - 1],
            device_id={"expert": lax.rem(mine + off, experts)}, device_id_type=MESH,
        )

    def expert_start(ref, kind):
        for off in range(1, experts):
            expert_copy(ref, kind, off).start()

    def expert_wait(ref, kind):
        for off in range(1, experts):
            expert_copy(ref, kind, off).wait()

    def pre_copy(it, q, e, i, target):
        place = d_pre.at[it, e, q]
        return pltpu.make_async_remote_copy(
            src_ref=place, dst_ref=place, send_sem=pre_send.at[it, q, i], recv_sem=pre_recv.at[it, q, i],
            device_id={"expert": target}, device_id_type=MESH,
        )

    def across(i):
        return lax.rem(mine + 2 * i, experts)

    def pre_start(it):
        for q in range(quarters):
            for i in range(1, pairs):
                pre_copy(it, q, mine, i - 1, across(i)).start()
            pre_copy(it, q, mine, pairs - 1, mate).start()

    def pre_forward(it, q):
        for i in range(1, pairs):
            source = across(pairs - i)
            pre_copy(it, q, source, i - 1, mate).wait_recv()
            pre_copy(it, q, source, pairs - 1 + i, mate).start()

    def pre_wait(it, q):
        for i in range(1, pairs):
            pre_copy(it, q, mine, i - 1, across(i)).wait_send()
        pre_copy(it, q, mine, pairs - 1, mate).wait_send()
        pre_copy(it, q, mate, pairs - 1, mate).wait_recv()
        for i in range(1, pairs):
            pre_copy(it, q, across(pairs - i), pairs - 1 + i, mate).wait_send()
            pre_copy(it, q, lax.rem(mate + 2 * (pairs - i), experts), pairs - 1 + i, mate).wait_recv()

    def coef_copy(it, off):
        place = message.at[it, me]
        return pltpu.make_async_remote_copy(
            src_ref=place, dst_ref=place, send_sem=co_send.at[it, off - 1], recv_sem=co_recv.at[it, off - 1],
            device_id={"col": lax.rem(me + off, n)}, device_id_type=MESH,
        )

    def mix(c_ref):
        for q in range(0, hl, 128):
            def add(k, total):
                return total + c_ref[mine, pl.ds(k, 1), :] * bases[k, :, q : q + 128]

            value = jnp.tanh(lax.fori_loop(0, k_count, add, jnp.zeros((r, 128), F32), unroll=4))
            mixed[:, q : q + 128] = value
            upper, lower = pieces(value)
            for i in range(2):
                tall[2 * i * r : (2 * i + 1) * r, q : q + 128] = upper
                tall[(2 * i + 1) * r : (2 * i + 2) * r, q : q + 128] = lower

    def gram_local():
        cut = tall[: 2 * r, :]
        both = contract(cut, cut, ((1,), (1,)))
        both = both[:r] + both[r:]
        gram_own[...] = both[:, :r] + both[:, r:]

    def project(j):
        def one(c, carry):
            value = contract(target[rows_of(j, c), :], tall[: 2 * r, :], ((1,), (1,)))
            part[j, chunk_of(c), :] = value[:, :r] + value[:, r:]
            return carry

        lax.fori_loop(0, chunks, one, 0)

    def absorb(it, shard, c):
        at = rows_of(shard, c)
        cut = jnp.concatenate(pieces(full[it, at, :]), axis=1)
        gram_sum[...] += contract(cut, jnp.concatenate([target[at, :], cut], axis=1), ((0,), (0,)))

    def loss_add(it, shard, c):
        at = rows_of(shard, c)
        one, two = pieces(full[it, at, :])
        wide = jnp.concatenate([one, one, two, two], axis=1)
        residual = contract(wide, tall[...], ((1,), (0,))) - target[at, :].astype(F32)
        loss_sum[...] += jnp.sum((residual * residual).reshape(ch // 8, 8, hl), axis=0)

    def arrived(way, s):
        it, b, c = split(s)
        p = place_of(way)
        return (p > 0) & (b <= p - 1), shard_at(way, p - 1 - b), c

    def for_arrived(act, it, s, own):
        first, first_shard, c = arrived(0, s)
        second, second_shard, _ = arrived(1, s)

        def one(i, carry):
            valid = jnp.where(i == 0, first, jnp.where(i == 1, second, own))
            shard = jnp.where(i == 0, first_shard, jnp.where(i == 1, second_shard, me))

            @pl.when(valid)
            def _():
                act(it, shard, c)

            return carry

        lax.fori_loop(0, 3, one, 0)

    def pre_gradient(it):
        total = gram_sum[:r, :] + gram_sum[r:, :]
        gram = total[:, hl : hl + r] + total[:, hl + r :]
        now = mixed[...]
        d_mixed = jnp.dot(gram, now, precision=HIGHEST, preferred_element_type=F32) - total[:, :hl]
        value = d_mixed * scale * (1.0 - now * now)
        for q in range(quarters):
            d_pre[it, mine, q] = value[:, q * 128 : (q + 1) * 128]

    def loss_close(it):
        total = loss_sum[:, 0:128]
        for q in range(128, hl, 128):
            total = total + loss_sum[:, q : q + 128]
        loss_in[mine, it * 8 : it * 8 + 8, :] = total
        loss_sum[...] = jnp.zeros_like(loss_sum)

    def combine(c_ref, it, k, q):
        total = c_ref[0, pl.ds(k, 1), :] * d_pre[it, 0, q]
        for e in range(1, experts):
            total = total + c_ref[e, pl.ds(k, 1), :] * d_pre[it, e, q]
        return total

    def columns(q):
        return slice(q * 128, (q + 1) * 128)

    def coef_pass(it, which):
        def one(k, carry):
            sums = [jnp.zeros((8, 128), F32)] * experts
            for q in which:
                values = bases[k, :, columns(q)]
                for e in range(experts):
                    held = values * d_pre[it, e, q]
                    sums[e] = sums[e] + jnp.sum(held.reshape(r // 8, 8, 128), axis=0)
            for e in range(experts):
                at = pl.ds(e * k_count + k, 1)
                value = jnp.sum(sums[e], axis=0, keepdims=True)
                coef_acc[at, :] = value if 0 in which else coef_acc[at, :] + value
            return carry

        lax.fori_loop(0, k_count, one, 0)

    def coef_send(it, losses=None):
        message[it, me] = jnp.zeros(message.shape[2:], F32)
        for i in range(blocks):
            column = jnp.sum(coef_acc[i * block : (i + 1) * block, :], axis=1, keepdims=True)
            message[it, me, i : i + 1, :] = to_lanes(jnp.broadcast_to(column, (block, 128)))
        if losses is not None:
            for i in range(2):
                message[it, me, blocks + i : blocks + i + 1, :] = jnp.sum(
                    losses[i * 8 : i * 8 + 8], axis=0, keepdims=True
                )
        for off in range(1, n):
            coef_copy(it, off).start()

    def coef_wait(it):
        for off in range(1, n):
            coef_copy(it, off).wait()

    def message_sum(it):
        total = message[it, 0]
        for c in range(1, n):
            total = total + message[it, c]
        return total

    def coef_table(total):
        held = [to_rows(total[i : i + 1, :], block) for i in range(blocks)]
        held = held[0] if blocks == 1 else jnp.concatenate(held, axis=0)
        return held.reshape(experts, k_count, 128)

    def bases_one(low, high):
        def one(k, carry):
            for q in range(quarters):
                gradient = combine(c_one, 0, k, q)
                b_grad[k, :, columns(q)] = gradient
                bases[k, :, columns(q)] = adam_first(bases[k, :, columns(q)], gradient)
            return carry

        lax.fori_loop(low, high, one, 0)

    def bases_two(q):
        def one(k, carry):
            values = bases[k, :, columns(q)]
            bases[k, :, columns(q)] = adam_second(values, b_grad[k, :, columns(q)], combine(c_two, 1, k, q))
            return carry

        lax.fori_loop(0, k_count, one, 0, unroll=2)

    def factor_gradient(it, c):
        before = full[it, rows_of(me, c), :]
        product = jnp.dot(before, gram_own[...], precision=HIGHEST, preferred_element_type=F32)
        return before, (product - part[me, chunk_of(c), :]) * scale

    def factor_one(c):
        before, g = factor_gradient(0, c)
        g_one[chunk_of(c), :] = g
        full[1, rows_of(me, c), :] = adam_first(before, g)

    def factor_two(c):
        before, g = factor_gradient(1, c)
        at = chunk_of(c)
        f_out[at, :] = adam_second(before, g_one[at, :], g)

    scope = jax.named_scope
    for s in range(LAG):
        give_first(s)
    misc[...] = jnp.zeros_like(misc)
    loads[2].wait()
    misc[0:1, :k_count] = c_raw[...]
    c_one[mine] = to_rows(misc[0:1, :], k_count)
    expert_start(c_one, 0)
    gram_sum[...] = jnp.zeros_like(gram_sum)
    loss_sum[...] = jnp.zeros_like(loss_sum)
    with scope("load"):
        loads[1].wait()
    with scope("mix"):
        mix(c_one)
        gram_local()
    with scope("project"):
        for j in range(n):
            loads[3 + j].wait()
            project(j)
    loads[0].wait()
    final = phase - chunks + LAG

    def early(s, carry):
        gram_hop(0, s, LAG)
        with scope("step"):
            step(s)
        own = s - LAG < chunks
        for_arrived(absorb, 0, s - LAG, own)
        for_arrived(loss_add, 0, s - LAG, own)
        return carry

    lax.fori_loop(LAG, final, early, 0)
    with scope("pre"):
        pre_gradient(0)
        expert_wait(c_one, 0)
        pre_start(0)
        gram_close(0)
        loss_close(0)
        gram_sum[...] = jnp.zeros_like(gram_sum)

    def base_work(i):
        if i == 0:
            with scope("forward"):
                for q in range(quarters):
                    pre_forward(0, q)
        elif i == 1:
            with scope("wait"):
                for q in range(quarters):
                    pre_wait(0, q)
            with scope("coef"):
                coef_pass(0, range(quarters))
                coef_send(0)
        elif i == 2:
            with scope("bases"):
                bases_one(0, k_count // 2)
        else:
            with scope("bases"):
                bases_one(k_count // 2, k_count)

    for c in range(chunks):
        with scope("step"):
            step(final + c)
        factor_one(c)
        absorb(1, me, c)
        base_work(c)

    begin = phase + chunks
    behind = begin - phase - LAG
    for s in range(final + chunks, begin):
        with scope("step"):
            step(s)
        for_arrived(absorb, 1, s - LAG, False)
    with scope("await"):
        coef_wait(0)
    c_two[...] = adam_first(c_one[...], coef_table(message_sum(0)))
    with scope("mix"):
        mix(c_two)
        gram_local()
    with scope("project"):
        for j in range(n):
            project(j)

    def late(s, carry):
        gram_hop(1, s, begin)
        with scope("step"):
            step(s)
        for_arrived(absorb, 1, s - LAG, False)
        for_arrived(loss_add, 1, s - LAG - behind, False)

        @pl.when(s - begin < chunks)
        def _():
            loss_add(1, me, s - begin)

        return carry

    end = phase + final
    lax.fori_loop(begin, end, late, 0)
    with scope("pre"):
        pre_gradient(1)
        pre_start(1)
        gram_close(1)
    for s in range(end - LAG - behind, end - LAG):
        for_arrived(loss_add, 1, s, False)
    loss_close(1)
    expert_start(loss_in, 1)
    with scope("step"):
        take(end)
    factor_two(0)
    with scope("forward"):
        pre_forward(1, 0)
    with scope("wait"):
        pre_wait(1, 0)
    with scope("coef"):
        coef_pass(1, (0,))
    with scope("forward"):
        for q in range(1, quarters):
            pre_forward(1, q)
    with scope("bases"):
        bases_two(0)
    with scope("wait"):
        for q in range(1, quarters):
            pre_wait(1, q)
    with scope("coef"):
        if quarters > 1:
            coef_pass(1, range(1, quarters))
        expert_wait(loss_in, 1)
        losses = loss_in[0]
        for e in range(1, experts):
            losses = losses + loss_in[e]
        coef_send(1, losses)
    give(end)
    q = 1
    for c in range(1, chunks):
        if q < quarters:
            with scope("bases"):
                bases_two(q)
            q += 1
        with scope("step"):
            take(end + c)
            if end + c < 2 * phase:
                give(end + c)
        with scope("factor"):
            factor_two(c)
    for i in range(q, quarters):
        bases_two(i)
    with scope("await"):
        coef_wait(1)
    total = message_sum(1)
    c_two[...] = adam_second(c_two[...], coef_table(message_sum(0)), coef_table(total))
    misc[0:1, :] = to_lanes(c_two[mine])
    for i in range(2):
        value = jnp.sum(total[blocks + i : blocks + i + 1, :], axis=1, keepdims=True) * loss_scale
        misc[1 + i : 2 + i, :] = jnp.broadcast_to(value, (1, 128))


def hand_over(b_in, f_in, misc, b_out, f_out, c_out, l_out, sem):
    parts = 8
    size = b_in.shape[0] // parts
    copies = [pltpu.make_async_copy(f_in, f_out, sem.at[parts])]
    for i in range(parts):
        at = pl.ds(i * size, size)
        copies.append(pltpu.make_async_copy(b_in.at[at], b_out.at[at], sem.at[i]))
    for copy in copies:
        copy.start()
    c_out[...] = misc[0:1, : c_out.shape[1]]
    for i in range(2):
        l_out[i] = misc[1 + i, 0]
    for copy in copies:
        copy.wait()


def shards(target_weights, factors, bases, coefficients):
    n, experts = lax.axis_size("col"), lax.axis_size("expert")
    _, d, hl = target_weights.shape
    _, rows, r = factors.shape
    k = bases.shape[0]
    held = pl.BlockSpec(memory_space=pltpu.HBM)
    local = pl.BlockSpec(memory_space=pltpu.VMEM)
    dma = pltpu.SemaphoreType.DMA
    loss_scale = 1.0 / (2.0 * experts * d * hl * n)
    new_factors, new_bases, misc = pl.pallas_call(
        functools.partial(kernel, n, experts, loss_scale),
        out_shape=(
            pltpu.VMEM((rows, r), F32),
            pltpu.VMEM(bases.shape, F32),
            pltpu.VMEM((8, 128), F32),
        ),
        in_specs=[held, held, held, held],
        out_specs=(local, local, local),
        scratch_shapes=[
            pltpu.VMEM((d, hl), BF16),
            pltpu.VMEM(bases.shape, F32),
            pltpu.VMEM((2, d, r), F32),
            pltpu.VMEM((n, rows, r), F32),
            pltpu.VMEM((2, n - 1, rows, r), F32),
            pltpu.VMEM((2, experts, hl // 128, r, 128), F32),
            pltpu.VMEM((experts, k, 128), F32),
            pltpu.VMEM((experts, k, 128), F32),
            pltpu.VMEM((experts * k, 128), F32),
            pltpu.VMEM((2, n, 8, 128), F32),
            pltpu.VMEM((experts, 16, 128), F32),
            pltpu.VMEM((rows, r), F32),
            pltpu.VMEM((2 * r, hl + 2 * r), F32),
            pltpu.VMEM((r, hl), F32),
            pltpu.VMEM((4 * r, hl), BF16),
            pltpu.VMEM((8, hl), F32),
            pltpu.VMEM((r, r), F32),
            pltpu.VMEM((2, 2, r, r), F32),
            pltpu.VMEM((2, 2, r, r), F32),
            pltpu.VMEM((1, k), F32),
            dma((3 + n,)),
            dma((2, SEMS)),
            dma((2, SEMS)),
            dma((2, 2)),
            dma((2, 2)),
            dma((2, experts - 1)),
            dma((2, experts - 1)),
            dma((2, hl // 128, experts - 1)),
            dma((2, hl // 128, experts - 1)),
            dma((2, n - 1)),
            dma((2, n - 1)),
        ],
        compiler_params=pltpu.CompilerParams(
            collective_id=0, has_side_effects=True, vmem_limit_bytes=VMEM_MAIN
        ),
    )(target_weights[0], factors[0], bases, coefficients)
    new_bases, new_factors, new_coef, losses = pl.pallas_call(
        hand_over,
        out_shape=(
            jax.ShapeDtypeStruct(bases.shape, F32),
            jax.ShapeDtypeStruct((rows, r), F32),
            jax.ShapeDtypeStruct((1, k), F32),
            jax.ShapeDtypeStruct((2,), F32),
        ),
        in_specs=[local, local, local],
        out_specs=(held, held, local, pl.BlockSpec(memory_space=pltpu.SMEM)),
        scratch_shapes=[dma((9,))],
        compiler_params=pltpu.CompilerParams(vmem_limit_bytes=VMEM_LAST),
    )(new_bases, new_factors, misc)
    return (new_factors[None], new_bases, new_coef, losses)


def solution(mesh):
    return jax.shard_map(
        shards,
        mesh=mesh,
        in_specs=(
            P(("layer", "expert"), None, "col"),
            P(("layer", "expert"), "col", None),
            P("layer", None, "col"),
            P(("layer", "expert"), None),
        ),
        out_specs=(
            P(("layer", "expert"), "col", None),
            P("layer", None, "col"),
            P(("layer", "expert"), None),
            P("layer"),
        ),
        check_vma=False,
    )
```

```python
import functools

import jax
import jax.numpy as jnp
from jax import lax
from jax.experimental import pallas as pl
from jax.experimental.pallas import tpu as pltpu
from jax.sharding import PartitionSpec as P

LEARN_RATE = 0.01
BETA_ONE = 0.9
BETA_TWO = 0.999
EPSILON = 0.0001
HIGHEST = lax.Precision.HIGHEST
MESH = pl.DeviceIdType.MESH
F32 = jnp.float32
BF16 = jnp.bfloat16
CHUNKS = 4
LAG = 3
VMEM_MAIN = 57000000
VMEM_LAST = 4000000
SEMS = 16


def adam_first(parameter, g):
    return parameter - LEARN_RATE * g / (jnp.abs(g) + EPSILON)


ROOT_ONE = (BETA_TWO * (1.0 - BETA_TWO) / (1.0 - BETA_TWO**2)) ** 0.5
ROOT_TWO = ((1.0 - BETA_TWO) / (1.0 - BETA_TWO**2)) ** 0.5
RATE_ONE = LEARN_RATE * BETA_ONE * (1.0 - BETA_ONE) / (1.0 - BETA_ONE**2) / ROOT_ONE
RATE_TWO = LEARN_RATE * (1.0 - BETA_ONE) / (1.0 - BETA_ONE**2) / ROOT_TWO


def adam_second(parameter, h_one, h_two):
    second = h_one * h_one + h_two * h_two
    root = second * lax.rsqrt(jnp.maximum(second, 1e-30))
    return parameter - (RATE_ONE * h_one + RATE_TWO * h_two) / (root + EPSILON)


def pieces(x):
    upper = x.astype(BF16)
    return upper, (x - upper.astype(F32)).astype(BF16)


def contract(a, b, dims):
    return lax.dot_general(a, b, (dims, ((), ())), preferred_element_type=F32)


def diagonal(size):
    shape = (size, 128)
    return lax.broadcasted_iota(jnp.int32, shape, 0) == lax.broadcasted_iota(jnp.int32, shape, 1)


def to_lanes(column):
    return jnp.sum(jnp.where(diagonal(column.shape[0]), column, 0.0), axis=0, keepdims=True)


def to_rows(row, size):
    held = jnp.where(diagonal(size), jnp.broadcast_to(row, (size, 128)), 0.0)
    return jnp.broadcast_to(jnp.sum(held, axis=1, keepdims=True), (size, 128))


def kernel(
    n, experts, loss_scale, t_hbm, f_hbm, b_hbm, c_hbm, f_out, bases, misc,
    target, b_grad, full, part, landed, d_pre, c_one, c_two, c_root, c_grad, coef_acc, message, loss_in, g_one, gram_sum,
    mixed, tall, loss_sum, gram_own, gram_in, gram_go, c_raw,
    load_sem, z_send, z_recv, gram_send, gram_recv, ex_send, ex_recv, pre_send, pre_recv, co_send, co_recv,
):
    me = lax.axis_index("col")
    mine = lax.axis_index("expert")
    rows, r = f_hbm.shape
    d, hl = target.shape
    k_count = bases.shape[0]
    scale = 1.0 / (hl * n)
    table = experts * k_count
    block = min(table, 128)
    blocks = table // block
    chunks = CHUNKS
    ch = rows // chunks
    phase = n * chunks
    quarters = hl // 128
    pairs = experts // 2
    mate = mine + 1 - 2 * lax.rem(mine, 2)

    loads = [
        pltpu.make_async_copy(f_hbm, full.at[0, pl.ds(pl.multiple_of(me * rows, 16), rows)], load_sem.at[0]),
        pltpu.make_async_copy(b_hbm, bases, load_sem.at[1]),
        pltpu.make_async_copy(c_hbm, c_raw, load_sem.at[2]),
    ]
    for j in range(n):
        at = pl.ds(j * rows, rows)
        loads.append(pltpu.make_async_copy(t_hbm.at[at], target.at[at], load_sem.at[3 + j]))
    for load in loads:
        load.start()
    barrier = pltpu.get_barrier_semaphore()
    for way in range(2):
        @pl.when((me + 1 - 2 * way >= 0) & (me + 1 - 2 * way < n))
        def _():
            pl.semaphore_signal(barrier, inc=1, device_id={"col": me + 1 - 2 * way}, device_id_type=MESH)

    for off in range(1, experts):
        pl.semaphore_signal(barrier, inc=1, device_id={"expert": lax.rem(mine + off, experts)}, device_id_type=MESH)
    pl.semaphore_wait(barrier, experts - 1 + jnp.where(me > 0, 1, 0) + jnp.where(me < n - 1, 1, 0))

    def place_of(way):
        return me if way == 0 else n - 1 - me

    def shard_at(way, place):
        return place if way == 0 else n - 1 - place

    def split(s):
        it = s // phase
        u = s - it * phase
        b = u // chunks
        return it, b, u - b * chunks

    def z_copy(way, s, src, dst):
        return pltpu.make_async_remote_copy(
            src_ref=src, dst_ref=dst, send_sem=z_send.at[way, s % SEMS], recv_sem=z_recv.at[way, s % SEMS],
            device_id={"col": me + 1 - 2 * way}, device_id_type=MESH,
        )

    def rows_of(shard, c):
        return pl.ds(pl.multiple_of(shard * rows + c * ch, 16), ch)

    def chunk_of(c):
        return pl.ds(pl.multiple_of(c * ch, 16), ch)

    def gather_copy(way, s, shard):
        it, b, c = split(s)
        ref = full.at[it, rows_of(shard, c)]
        return z_copy(way, s, ref, ref)

    def scatter_copy(way, s, shard):
        it, b, c = split(s)
        return z_copy(way, s, part.at[shard, chunk_of(c)], landed.at[way, b - 1, chunk_of(c)])

    def on_send(way, s, act):
        it, b, c = split(s)
        p = place_of(way)

        @pl.when((p < n - 1) & (b <= p))
        def _():
            act(gather_copy(way, s, shard_at(way, p - b)))

        @pl.when((p < n - 1) & (b > p))
        def _():
            act(scatter_copy(way, s, shard_at(way, n + p - b)))

    def arrive(way, s):
        it, b, c = split(s)
        p = place_of(way)

        @pl.when((p > 0) & (b <= p - 1))
        def _():
            gather_copy(way, s, shard_at(way, p - 1 - b)).wait_recv()

        @pl.when((p > 0) & (b > p - 1))
        def _():
            shard = shard_at(way, n + p - 1 - b)
            scatter_copy(way, s, shard).wait_recv()
            at = chunk_of(c)
            part[shard, at, :] = part[shard, at, :] + landed[way, b - 1, at, :]

    def take(s):
        for way in range(2):
            on_send(way, s - LAG, lambda copy: copy.wait_send())
        for way in range(2):
            arrive(way, s - LAG)

    def give(s):
        for way in range(2):
            on_send(way, s, lambda copy: copy.start())

    def step(s):
        take(s)
        give(s)

    def give_first(s):
        for way in range(2):
            @pl.when(place_of(way) < n - 1)
            def _():
                z_copy(way, s, f_hbm.at[chunk_of(s)], full.at[0, rows_of(me, s)]).start()

    def gram_copy(it, way):
        return pltpu.make_async_remote_copy(
            src_ref=gram_go.at[it, way], dst_ref=gram_in.at[it, way], send_sem=gram_send.at[it, way],
            recv_sem=gram_recv.at[it, way], device_id={"col": me + 1 - 2 * way}, device_id_type=MESH,
        )

    def gram_hop(it, s, start):
        for way in range(2):
            p = place_of(way)
            now = s == start + p * LAG

            @pl.when(now & (p > 0))
            def _():
                gram_copy(it, way).wait_recv()

            @pl.when(now & (p == 0) & (p < n - 1))
            def _():
                gram_go[it, way] = gram_own[...]

            @pl.when(now & (p > 0) & (p < n - 1))
            def _():
                gram_go[it, way] = gram_own[...] + gram_in[it, way]

            @pl.when(now & (p < n - 1))
            def _():
                gram_copy(it, way).start()

    def gram_close(it):
        for way in range(2):
            p = place_of(way)

            @pl.when(p > 0)
            def _():
                gram_own[...] = gram_own[...] + gram_in[it, way]

            @pl.when(p < n - 1)
            def _():
                gram_copy(it, way).wait_send()

    def expert_copy(ref, kind, off):
        place = ref.at[mine]
        return pltpu.make_async_remote_copy(
            src_ref=place, dst_ref=place, send_sem=ex_send.at[kind, off - 1], recv_sem=ex_recv.at[kind, off - 1],
            device_id={"expert": lax.rem(mine + off, experts)}, device_id_type=MESH,
        )

    def expert_start(ref, kind):
        for off in range(1, experts):
            expert_copy(ref, kind, off).start()

    def expert_wait(ref, kind):
        for off in range(1, experts):
            expert_copy(ref, kind, off).wait()

    def pre_copy(it, q, e, i, target):
        place = d_pre.at[it, e, q]
        return pltpu.make_async_remote_copy(
            src_ref=place, dst_ref=place, send_sem=pre_send.at[it, q, i], recv_sem=pre_recv.at[it, q, i],
            device_id={"expert": target}, device_id_type=MESH,
        )

    def across(i):
        return lax.rem(mine + 2 * i, experts)

    def pre_start(it):
        for q in range(quarters):
            for i in range(1, pairs):
                pre_copy(it, q, mine, i - 1, across(i)).start()
            pre_copy(it, q, mine, pairs - 1, mate).start()

    def pre_forward(it, q):
        for i in range(1, pairs):
            source = across(pairs - i)
            pre_copy(it, q, source, i - 1, mate).wait_recv()
            pre_copy(it, q, source, pairs - 1 + i, mate).start()

    def pre_wait(it, q):
        for i in range(1, pairs):
            pre_copy(it, q, mine, i - 1, across(i)).wait_send()
        pre_copy(it, q, mine, pairs - 1, mate).wait_send()
        pre_copy(it, q, mate, pairs - 1, mate).wait_recv()
        for i in range(1, pairs):
            pre_copy(it, q, across(pairs - i), pairs - 1 + i, mate).wait_send()
            pre_copy(it, q, lax.rem(mate + 2 * (pairs - i), experts), pairs - 1 + i, mate).wait_recv()

    def coef_copy(it, off):
        place = message.at[it, me]
        return pltpu.make_async_remote_copy(
            src_ref=place, dst_ref=place, send_sem=co_send.at[it, off - 1], recv_sem=co_recv.at[it, off - 1],
            device_id={"col": lax.rem(me + off, n)}, device_id_type=MESH,
        )

    def mix(c_ref):
        for q in range(0, hl, 128):
            def add(k, total):
                return total + c_ref[mine, pl.ds(k, 1), :] * bases[k, :, q : q + 128]

            value = jnp.tanh(lax.fori_loop(0, k_count, add, jnp.zeros((r, 128), F32), unroll=4))
            mixed[:, q : q + 128] = value
            upper, lower = pieces(value)
            for i in range(2):
                tall[2 * i * r : (2 * i + 1) * r, q : q + 128] = upper
                tall[(2 * i + 1) * r : (2 * i + 2) * r, q : q + 128] = lower

    def gram_local():
        cut = tall[: 2 * r, :]
        both = contract(cut, cut, ((1,), (1,)))
        both = both[:r] + both[r:]
        gram_own[...] = both[:, :r] + both[:, r:]

    def project(j):
        def one(c, carry):
            value = contract(target[rows_of(j, c), :], tall[: 2 * r, :], ((1,), (1,)))
            part[j, chunk_of(c), :] = value[:, :r] + value[:, r:]
            return carry

        lax.fori_loop(0, chunks, one, 0)

    def absorb(it, shard, c):
        at = rows_of(shard, c)
        cut = jnp.concatenate(pieces(full[it, at, :]), axis=1)
        gram_sum[...] += contract(cut, jnp.concatenate([target[at, :], cut], axis=1), ((0,), (0,)))

    def loss_add(it, shard, c):
        at = rows_of(shard, c)
        one, two = pieces(full[it, at, :])
        wide = jnp.concatenate([one, one, two, two], axis=1)
        residual = contract(wide, tall[...], ((1,), (0,))) - target[at, :].astype(F32)
        loss_sum[...] += jnp.sum((residual * residual).reshape(ch // 8, 8, hl), axis=0)

    def arrived(way, s):
        it, b, c = split(s)
        p = place_of(way)
        return (p > 0) & (b <= p - 1), shard_at(way, p - 1 - b), c

    def for_arrived(act, it, s, own):
        first, first_shard, c = arrived(0, s)
        second, second_shard, _ = arrived(1, s)

        def one(i, carry):
            valid = jnp.where(i == 0, first, jnp.where(i == 1, second, own))
            shard = jnp.where(i == 0, first_shard, jnp.where(i == 1, second_shard, me))

            @pl.when(valid)
            def _():
                act(it, shard, c)

            return carry

        lax.fori_loop(0, 3, one, 0)

    def pre_gradient(it):
        total = gram_sum[:r, :] + gram_sum[r:, :]
        gram = total[:, hl : hl + r] + total[:, hl + r :]
        now = mixed[...]
        d_mixed = jnp.dot(gram, now, precision=HIGHEST, preferred_element_type=F32) - total[:, :hl]
        value = d_mixed * scale * (1.0 - now * now)
        for q in range(quarters):
            d_pre[it, mine, q] = value[:, q * 128 : (q + 1) * 128]

    def loss_close(it):
        total = loss_sum[:, 0:128]
        for q in range(128, hl, 128):
            total = total + loss_sum[:, q : q + 128]
        loss_in[mine, it * 8 : it * 8 + 8, :] = total
        loss_sum[...] = jnp.zeros_like(loss_sum)

    def combine(c_ref, it, k, q):
        total = c_ref[0, pl.ds(k, 1), :] * d_pre[it, 0, q]
        for e in range(1, experts):
            total = total + c_ref[e, pl.ds(k, 1), :] * d_pre[it, e, q]
        return total

    def columns(q):
        return slice(q * 128, (q + 1) * 128)

    def coef_pass(it, which):
        def one(k, carry):
            sums = [jnp.zeros((8, 128), F32)] * experts
            for q in which:
                values = bases[k, :, columns(q)]
                for e in range(experts):
                    held = values * d_pre[it, e, q]
                    sums[e] = sums[e] + jnp.sum(held.reshape(r // 8, 8, 128), axis=0)
            for e in range(experts):
                at = pl.ds(e * k_count + k, 1)
                value = jnp.sum(sums[e], axis=0, keepdims=True)
                coef_acc[at, :] = value if 0 in which else coef_acc[at, :] + value
            return carry

        lax.fori_loop(0, k_count, one, 0)

    def coef_send(it, losses=None):
        message[it, me] = jnp.zeros(message.shape[2:], F32)
        for i in range(blocks):
            column = jnp.sum(coef_acc[i * block : (i + 1) * block, :], axis=1, keepdims=True)
            message[it, me, i : i + 1, :] = to_lanes(jnp.broadcast_to(column, (block, 128)))
        if losses is not None:
            for i in range(2):
                message[it, me, blocks + i : blocks + i + 1, :] = jnp.sum(
                    losses[i * 8 : i * 8 + 8], axis=0, keepdims=True
                )
        for off in range(1, n):
            coef_copy(it, off).start()

    def coef_wait(it):
        for off in range(1, n):
            coef_copy(it, off).wait()

    def message_sum(it):
        total = message[it, 0]
        for c in range(1, n):
            total = total + message[it, c]
        return total

    def coef_table(total):
        held = [to_rows(total[i : i + 1, :], block) for i in range(blocks)]
        held = held[0] if blocks == 1 else jnp.concatenate(held, axis=0)
        return held.reshape(experts, k_count, 128)

    def bases_one(low, high):
        def one(k, carry):
            for q in range(quarters):
                gradient = combine(c_one, 0, k, q)
                b_grad[k, :, columns(q)] = ROOT_ONE * gradient
                bases[k, :, columns(q)] = adam_first(bases[k, :, columns(q)], gradient)
            return carry

        lax.fori_loop(low, high, one, 0)

    def bases_two(q):
        def one(k, carry):
            values = bases[k, :, columns(q)]
            bases[k, :, columns(q)] = adam_second(values, b_grad[k, :, columns(q)], combine(c_root, 1, k, q))
            return carry

        lax.fori_loop(0, k_count, one, 0, unroll=2)

    def factor_product(it, c):
        return jnp.dot(
            full[it, rows_of(me, c), :], gram_own[...], precision=HIGHEST, preferred_element_type=F32
        )

    def factor_one(c):
        at = chunk_of(c)
        g = (factor_product(0, c) - part[me, at, :]) * scale
        g_one[at, :] = ROOT_ONE * g
        full[1, rows_of(me, c), :] = adam_first(full[0, rows_of(me, c), :], g)

    def factor_two(c):
        at = chunk_of(c)
        g = (full[0, rows_of(me, c), :] - part[me, at, :]) * (ROOT_TWO * scale)
        f_out[at, :] = adam_second(full[1, rows_of(me, c), :], g_one[at, :], g)

    scope = jax.named_scope
    for s in range(LAG):
        give_first(s)
    misc[...] = jnp.zeros_like(misc)
    loads[2].wait()
    misc[0:1, :k_count] = c_raw[...]
    c_one[mine] = to_rows(misc[0:1, :], k_count)
    expert_start(c_one, 0)
    gram_sum[...] = jnp.zeros_like(gram_sum)
    loss_sum[...] = jnp.zeros_like(loss_sum)
    with scope("load"):
        loads[1].wait()
    with scope("mix"):
        mix(c_one)
        gram_local()
    with scope("project"):
        for j in range(n):
            loads[3 + j].wait()
            project(j)
    loads[0].wait()
    final = phase - chunks + LAG

    def early(s, carry):
        gram_hop(0, s, LAG)
        with scope("step"):
            step(s)
        own = s - LAG < chunks
        for_arrived(absorb, 0, s - LAG, own)
        for_arrived(loss_add, 0, s - LAG, own)
        return carry

    lax.fori_loop(LAG, final, early, 0)
    with scope("pre"):
        pre_gradient(0)
        expert_wait(c_one, 0)
        pre_start(0)
        gram_close(0)
        loss_close(0)
        gram_sum[...] = jnp.zeros_like(gram_sum)

    def base_work(i):
        if i == 0:
            with scope("forward"):
                for q in range(quarters):
                    pre_forward(0, q)
        elif i == 1:
            with scope("wait"):
                for q in range(quarters):
                    pre_wait(0, q)
            with scope("coef"):
                coef_pass(0, range(quarters))
                coef_send(0)
        elif i == 2:
            with scope("bases"):
                bases_one(0, k_count // 2)
        else:
            with scope("bases"):
                bases_one(k_count // 2, k_count)

    for c in range(chunks):
        with scope("step"):
            step(final + c)
        factor_one(c)
        absorb(1, me, c)
        base_work(c)

    begin = phase + chunks
    behind = begin - phase - LAG
    for s in range(final + chunks, begin):
        with scope("step"):
            step(s)
        for_arrived(absorb, 1, s - LAG, False)
    with scope("await"):
        coef_wait(0)
    c_grad[...] = coef_table(message_sum(0))
    c_two[...] = adam_first(c_one[...], c_grad[...])
    c_root[...] = ROOT_TWO * c_two[...]
    with scope("mix"):
        mix(c_two)
        gram_local()
    with scope("project"):
        for j in range(n):
            project(j)

    def late(s, carry):
        gram_hop(1, s, begin)
        with scope("step"):
            step(s)
        for_arrived(absorb, 1, s - LAG, False)
        for_arrived(loss_add, 1, s - LAG - behind, False)

        @pl.when(s - begin < chunks)
        def _():
            loss_add(1, me, s - begin)

        return carry

    end = phase + final
    lax.fori_loop(begin, end, late, 0)
    with scope("pre"):
        pre_gradient(1)
        pre_start(1)
        gram_close(1)
    with scope("product"):
        for c in range(chunks):
            full[0, rows_of(me, c), :] = factor_product(1, c)
    for s in range(end - LAG - behind, end - LAG):
        for_arrived(loss_add, 1, s, False)
    loss_close(1)
    expert_start(loss_in, 1)
    with scope("forward"):
        pre_forward(1, 0)
    with scope("step"):
        take(end)
    factor_two(0)
    with scope("wait"):
        pre_wait(1, 0)
    with scope("coef"):
        coef_pass(1, (0,))
    with scope("forward"):
        for q in range(1, quarters):
            pre_forward(1, q)
    with scope("bases"):
        bases_two(0)
    with scope("wait"):
        for q in range(1, quarters):
            pre_wait(1, q)
    with scope("coef"):
        if quarters > 1:
            coef_pass(1, range(1, quarters))
        expert_wait(loss_in, 1)
        losses = loss_in[0]
        for e in range(1, experts):
            losses = losses + loss_in[e]
        coef_send(1, losses)
    give(end)
    for q in range(1, quarters):
        with scope("bases"):
            bases_two(q)
        if q < chunks - 1:
            with scope("step"):
                take(end + q)
            factor_two(q)
    for c in range(max(quarters, 1), chunks - 1):
        take(end + c)
        factor_two(c)
    with scope("await"):
        coef_wait(1)
    with scope("coefs"):
        total = message_sum(1)
        own = pl.ds(mine * k_count, k_count)
        coef_acc[...] = coef_table(total).reshape(table, 128)
        misc[0:1, :] = to_lanes(adam_second(c_two[mine], ROOT_ONE * c_grad[mine], ROOT_TWO * coef_acc[own, :]))
        for i in range(2):
            value = jnp.sum(total[blocks + i : blocks + i + 1, :], axis=1, keepdims=True) * loss_scale
            misc[1 + i : 2 + i, :] = jnp.broadcast_to(value, (1, 128))
    with scope("step"):
        take(end + chunks - 1)
    with scope("factor"):
        factor_two(chunks - 1)


def hand_over(b_in, f_in, misc, b_out, f_out, c_out, l_out, sem):
    parts = 8
    size = b_in.shape[0] // parts
    copies = [pltpu.make_async_copy(f_in, f_out, sem.at[parts])]
    for i in range(parts):
        at = pl.ds(i * size, size)
        copies.append(pltpu.make_async_copy(b_in.at[at], b_out.at[at], sem.at[i]))
    for copy in copies:
        copy.start()
    c_out[...] = misc[0:1, : c_out.shape[1]]
    for i in range(2):
        l_out[i] = misc[1 + i, 0]
    for copy in copies:
        copy.wait()


def shards(target_weights, factors, bases, coefficients):
    n, experts = lax.axis_size("col"), lax.axis_size("expert")
    _, d, hl = target_weights.shape
    _, rows, r = factors.shape
    k = bases.shape[0]
    held = pl.BlockSpec(memory_space=pltpu.HBM)
    local = pl.BlockSpec(memory_space=pltpu.VMEM)
    dma = pltpu.SemaphoreType.DMA
    loss_scale = 1.0 / (2.0 * experts * d * hl * n)
    new_factors, new_bases, misc = pl.pallas_call(
        functools.partial(kernel, n, experts, loss_scale),
        out_shape=(
            pltpu.VMEM((rows, r), F32),
            pltpu.VMEM(bases.shape, F32),
            pltpu.VMEM((8, 128), F32),
        ),
        in_specs=[held, held, held, held],
        out_specs=(local, local, local),
        scratch_shapes=[
            pltpu.VMEM((d, hl), BF16),
            pltpu.VMEM(bases.shape, F32),
            pltpu.VMEM((2, d, r), F32),
            pltpu.VMEM((n, rows, r), F32),
            pltpu.VMEM((2, n - 1, rows, r), F32),
            pltpu.VMEM((2, experts, hl // 128, r, 128), F32),
            pltpu.VMEM((experts, k, 128), F32),
            pltpu.VMEM((experts, k, 128), F32),
            pltpu.VMEM((experts, k, 128), F32),
            pltpu.VMEM((experts, k, 128), F32),
            pltpu.VMEM((experts * k, 128), F32),
            pltpu.VMEM((2, n, 8, 128), F32),
            pltpu.VMEM((experts, 16, 128), F32),
            pltpu.VMEM((rows, r), F32),
            pltpu.VMEM((2 * r, hl + 2 * r), F32),
            pltpu.VMEM((r, hl), F32),
            pltpu.VMEM((4 * r, hl), BF16),
            pltpu.VMEM((8, hl), F32),
            pltpu.VMEM((r, r), F32),
            pltpu.VMEM((2, 2, r, r), F32),
            pltpu.VMEM((2, 2, r, r), F32),
            pltpu.VMEM((1, k), F32),
            dma((3 + n,)),
            dma((2, SEMS)),
            dma((2, SEMS)),
            dma((2, 2)),
            dma((2, 2)),
            dma((2, experts - 1)),
            dma((2, experts - 1)),
            dma((2, hl // 128, experts - 1)),
            dma((2, hl // 128, experts - 1)),
            dma((2, n - 1)),
            dma((2, n - 1)),
        ],
        compiler_params=pltpu.CompilerParams(
            collective_id=0, has_side_effects=True, vmem_limit_bytes=VMEM_MAIN
        ),
    )(target_weights[0], factors[0], bases, coefficients)
    new_bases, new_factors, new_coef, losses = pl.pallas_call(
        hand_over,
        out_shape=(
            jax.ShapeDtypeStruct(bases.shape, F32),
            jax.ShapeDtypeStruct((rows, r), F32),
            jax.ShapeDtypeStruct((1, k), F32),
            jax.ShapeDtypeStruct((2,), F32),
        ),
        in_specs=[local, local, local],
        out_specs=(held, held, local, pl.BlockSpec(memory_space=pltpu.SMEM)),
        scratch_shapes=[dma((9,))],
        compiler_params=pltpu.CompilerParams(vmem_limit_bytes=VMEM_LAST),
    )(new_bases, new_factors, misc)
    return (new_factors[None], new_bases, new_coef, losses)


def solution(mesh):
    return jax.shard_map(
        shards,
        mesh=mesh,
        in_specs=(
            P(("layer", "expert"), None, "col"),
            P(("layer", "expert"), "col", None),
            P("layer", None, "col"),
            P(("layer", "expert"), None),
        ),
        out_specs=(
            P(("layer", "expert"), "col", None),
            P("layer", None, "col"),
            P(("layer", "expert"), None),
            P("layer"),
        ),
        check_vma=False,
    )
```

```python
import functools

import jax
import jax.numpy as jnp
from jax import lax
from jax.experimental import pallas as pl
from jax.experimental.pallas import tpu as pltpu
from jax.sharding import PartitionSpec as P

LEARN_RATE = 0.01
BETA_ONE = 0.9
BETA_TWO = 0.999
EPSILON = 0.0001
HIGHEST = lax.Precision.HIGHEST
MESH = pl.DeviceIdType.MESH
F32 = jnp.float32
BF16 = jnp.bfloat16
CHUNKS = 4
LAG = 3
VMEM_MAIN = 57000000
VMEM_LAST = 4000000
SEMS = 16


def adam_first(parameter, g):
    return parameter - LEARN_RATE * g / (jnp.abs(g) + EPSILON)


ROOT_ONE = (BETA_TWO * (1.0 - BETA_TWO) / (1.0 - BETA_TWO**2)) ** 0.5
ROOT_TWO = ((1.0 - BETA_TWO) / (1.0 - BETA_TWO**2)) ** 0.5
RATE_ONE = LEARN_RATE * BETA_ONE * (1.0 - BETA_ONE) / (1.0 - BETA_ONE**2) / ROOT_ONE
RATE_TWO = LEARN_RATE * (1.0 - BETA_ONE) / (1.0 - BETA_ONE**2) / ROOT_TWO


def adam_second(parameter, h_one, h_two):
    second = h_one * h_one + h_two * h_two
    root = second * lax.rsqrt(jnp.maximum(second, 1e-30))
    return parameter - (RATE_ONE * h_one + RATE_TWO * h_two) / (root + EPSILON)


def pieces(x):
    upper = x.astype(BF16)
    return upper, (x - upper.astype(F32)).astype(BF16)


def contract(a, b, dims):
    return lax.dot_general(a, b, (dims, ((), ())), preferred_element_type=F32)


def diagonal(size):
    shape = (size, 128)
    return lax.broadcasted_iota(jnp.int32, shape, 0) == lax.broadcasted_iota(jnp.int32, shape, 1)


def to_lanes(column):
    return jnp.sum(jnp.where(diagonal(column.shape[0]), column, 0.0), axis=0, keepdims=True)


def places(shape):
    return lax.broadcasted_iota(jnp.int32, shape, 0), lax.broadcasted_iota(jnp.int32, shape, 1)


def pack_symmetric(g):
    half = g.shape[0] // 2
    row, lane = places((half, 2 * half))
    turned = pltpu.roll(g[half:], half, 1)
    top = jnp.where((lane > row) & (lane < half), turned, g[:half])
    diagonal_row = jnp.sum(jnp.where(lane == row, turned, 0.0), axis=0, keepdims=True)
    return jnp.concatenate([top, jnp.broadcast_to(diagonal_row, (8, 2 * half))], axis=0)


def unpack_symmetric(p):
    half = p.shape[1] // 2
    row, lane = places((half, 2 * half))
    top, diagonal_row = p[:half], jnp.broadcast_to(p[half : half + 1], (half, 2 * half))
    flipped = jnp.transpose(jnp.concatenate([top, top], axis=0))
    upper = jnp.where((lane > row) & (lane < half), flipped[:half], top)
    last = jnp.where(lane > row, top, jnp.where(lane < row, flipped[:half], diagonal_row))
    lower = jnp.where(lane < half, flipped[half:], pltpu.roll(last, half, 1))
    return jnp.concatenate([upper, lower], axis=0)


def lane_sums(x):
    total = jnp.sum(x, axis=(0, 1), keepdims=True)
    return jnp.where(lax.broadcasted_iota(jnp.int32, x.shape, 0) == 0, jnp.broadcast_to(total, x.shape), 0.0)


def to_rows(row, size):
    held = jnp.where(diagonal(size), jnp.broadcast_to(row, (size, 128)), 0.0)
    return jnp.broadcast_to(jnp.sum(held, axis=1, keepdims=True), (size, 128))


def kernel(
    n, experts, loss_scale, t_hbm, f_hbm, b_hbm, c_hbm, f_out, bases, misc,
    target, b_grad, full, part, landed, d_pre, c_one, c_two, c_root, c_grad, coef_acc, message, loss_in, g_one, gram_sum,
    mixed, tall, loss_sum, gram, gram_packed, gram_in, gram_go, c_raw,
    entered, load_sem, z_send, z_recv, gram_send, gram_recv, ex_send, ex_recv, pre_send, pre_recv, co_send, co_recv,
):
    me = lax.axis_index("col")
    mine = lax.axis_index("expert")
    rows, r = f_hbm.shape
    d, hl = target.shape
    k_count = bases.shape[0]
    scale = 1.0 / (hl * n)
    table = experts * k_count
    block = min(table, 128)
    blocks = table // block
    chunks = CHUNKS
    ch = rows // chunks
    phase = n * chunks
    quarters = hl // 128
    pairs = experts // 2
    mate = mine + 1 - 2 * lax.rem(mine, 2)

    barrier = pltpu.get_barrier_semaphore()

    @pl.when(me < n - 1)
    def _():
        pl.semaphore_signal(barrier, inc=1, device_id={"col": me + 1}, device_id_type=MESH)

    for off in range(1, experts):
        pl.semaphore_signal(barrier, inc=1, device_id={"expert": lax.rem(mine + off, experts)}, device_id_type=MESH)
    loads = [
        pltpu.make_async_copy(f_hbm, full.at[0, pl.ds(pl.multiple_of(me * rows, 16), rows)], load_sem.at[0]),
        pltpu.make_async_copy(b_hbm, bases, load_sem.at[1]),
        pltpu.make_async_copy(c_hbm, c_raw, load_sem.at[2]),
    ]
    for j in range(n):
        at = pl.ds(j * rows, rows)
        loads.append(pltpu.make_async_copy(t_hbm.at[at], target.at[at], load_sem.at[3 + j]))
    for load in loads:
        load.start()

    @pl.when(me > 0)
    def _():
        pl.semaphore_wait(barrier, experts)
        pl.semaphore_signal(entered, inc=1, device_id={"col": me - 1}, device_id_type=MESH)

    def place_of(way):
        return me if way == 0 else n - 1 - me

    def shard_at(way, place):
        return place if way == 0 else n - 1 - place

    def split(s):
        it = s // phase
        u = s - it * phase
        b = u // chunks
        return it, b, u - b * chunks

    def z_copy(way, s, src, dst):
        return pltpu.make_async_remote_copy(
            src_ref=src, dst_ref=dst, send_sem=z_send.at[way, s % SEMS], recv_sem=z_recv.at[way, s % SEMS],
            device_id={"col": me + 1 - 2 * way}, device_id_type=MESH,
        )

    def rows_of(shard, c):
        return pl.ds(pl.multiple_of(shard * rows + c * ch, 16), ch)

    def chunk_of(c):
        return pl.ds(pl.multiple_of(c * ch, 16), ch)

    def gather_copy(way, s, shard):
        it, b, c = split(s)
        ref = full.at[it, rows_of(shard, c)]
        return z_copy(way, s, ref, ref)

    def scatter_copy(way, s, shard):
        it, b, c = split(s)
        return z_copy(way, s, part.at[shard, chunk_of(c)], landed.at[way, b - 1, chunk_of(c)])

    def on_send(way, s, act):
        it, b, c = split(s)
        p = place_of(way)

        @pl.when((p < n - 1) & (b <= p))
        def _():
            act(gather_copy(way, s, shard_at(way, p - b)))

        @pl.when((p < n - 1) & (b > p))
        def _():
            act(scatter_copy(way, s, shard_at(way, n + p - b)))

    def arrive(way, s):
        it, b, c = split(s)
        p = place_of(way)

        @pl.when((p > 0) & (b <= p - 1))
        def _():
            gather_copy(way, s, shard_at(way, p - 1 - b)).wait_recv()

        @pl.when((p > 0) & (b > p - 1))
        def _():
            shard = shard_at(way, n + p - 1 - b)
            scatter_copy(way, s, shard).wait_recv()
            at = chunk_of(c)
            part[shard, at, :] = part[shard, at, :] + landed[way, b - 1, at, :]

    def take(s):
        for way in range(2):
            on_send(way, s - LAG, lambda copy: copy.wait_send())
        for way in range(2):
            arrive(way, s - LAG)

    def give(s):
        for way in range(2):
            on_send(way, s, lambda copy: copy.start())

    def step(s):
        take(s)
        give(s)

    def give_first(way):
        @pl.when(place_of(way) < n - 1)
        def _():
            if way == 0:
                pl.semaphore_wait(entered, 1)
            for s in range(LAG):
                z_copy(way, s, f_hbm.at[chunk_of(s)], full.at[0, rows_of(me, s)]).start()

    def gram_copy(it, way):
        return pltpu.make_async_remote_copy(
            src_ref=gram_go.at[it, way], dst_ref=gram_in.at[it, way], send_sem=gram_send.at[it, way],
            recv_sem=gram_recv.at[it, way], device_id={"col": me + 1 - 2 * way}, device_id_type=MESH,
        )

    def gram_hop(it, s, start):
        for way in range(2):
            p = place_of(way)
            now = s == start + p * LAG

            @pl.when(now & (p > 0))
            def _():
                gram_copy(it, way).wait_recv()

            @pl.when(now & (p == 0) & (p < n - 1))
            def _():
                gram_go[it, way] = gram_packed[...]

            @pl.when(now & (p > 0) & (p < n - 1))
            def _():
                gram_go[it, way] = gram_packed[...] + gram_in[it, way]

            @pl.when(now & (p < n - 1))
            def _():
                gram_copy(it, way).start()

    def gram_close(it):
        for way in range(2):
            p = place_of(way)

            @pl.when(p > 0)
            def _():
                gram_packed[...] = gram_packed[...] + gram_in[it, way]

            @pl.when(p < n - 1)
            def _():
                gram_copy(it, way).wait_send()

        gram[...] = unpack_symmetric(gram_packed[...])

    def expert_copy(ref, kind, off):
        place = ref.at[mine]
        return pltpu.make_async_remote_copy(
            src_ref=place, dst_ref=place, send_sem=ex_send.at[kind, off - 1], recv_sem=ex_recv.at[kind, off - 1],
            device_id={"expert": lax.rem(mine + off, experts)}, device_id_type=MESH,
        )

    def expert_start(ref, kind):
        for off in range(1, experts):
            expert_copy(ref, kind, off).start()

    def expert_wait(ref, kind):
        for off in range(1, experts):
            expert_copy(ref, kind, off).wait()

    def pre_copy(it, q, e, i, target):
        place = d_pre.at[it, e, q]
        return pltpu.make_async_remote_copy(
            src_ref=place, dst_ref=place, send_sem=pre_send.at[it, q, i], recv_sem=pre_recv.at[it, q, i],
            device_id={"expert": target}, device_id_type=MESH,
        )

    def across(i):
        return lax.rem(mine + 2 * i, experts)

    def pre_start(it):
        for q in range(quarters):
            for i in range(1, pairs):
                pre_copy(it, q, mine, i - 1, across(i)).start()
            pre_copy(it, q, mine, pairs - 1, mate).start()

    def pre_forward(it, q):
        for i in range(1, pairs):
            source = across(pairs - i)
            pre_copy(it, q, source, i - 1, mate).wait_recv()
            pre_copy(it, q, source, pairs - 1 + i, mate).start()

    def pre_wait(it, q):
        for i in range(1, pairs):
            pre_copy(it, q, mine, i - 1, across(i)).wait_send()
        pre_copy(it, q, mine, pairs - 1, mate).wait_send()
        pre_copy(it, q, mate, pairs - 1, mate).wait_recv()
        for i in range(1, pairs):
            pre_copy(it, q, across(pairs - i), pairs - 1 + i, mate).wait_send()
            pre_copy(it, q, lax.rem(mate + 2 * (pairs - i), experts), pairs - 1 + i, mate).wait_recv()

    def coef_copy(it, off):
        place = message.at[it, me]
        return pltpu.make_async_remote_copy(
            src_ref=place, dst_ref=place, send_sem=co_send.at[it, off - 1], recv_sem=co_recv.at[it, off - 1],
            device_id={"col": lax.rem(me + off, n)}, device_id_type=MESH,
        )

    def mix(c_ref):
        for q in range(0, hl, 128):
            def add(k, total):
                return total + c_ref[mine, pl.ds(k, 1), :] * bases[k, :, q : q + 128]

            value = jnp.tanh(lax.fori_loop(0, k_count, add, jnp.zeros((r, 128), F32), unroll=4))
            mixed[:, q : q + 128] = value
            upper, lower = pieces(value)
            for i in range(2):
                tall[2 * i * r : (2 * i + 1) * r, q : q + 128] = upper
                tall[(2 * i + 1) * r : (2 * i + 2) * r, q : q + 128] = lower

    def gram_local():
        cut = tall[: 2 * r, :]
        both = contract(cut, cut, ((1,), (1,)))
        both = both[:r] + both[r:]
        gram_packed[...] = pack_symmetric(both[:, :r] + both[:, r:])

    def project(j):
        def one(c, carry):
            value = contract(target[rows_of(j, c), :], tall[: 2 * r, :], ((1,), (1,)))
            part[j, chunk_of(c), :] = value[:, :r] + value[:, r:]
            return carry

        lax.fori_loop(0, chunks, one, 0)

    def absorb(it, shard, c):
        at = rows_of(shard, c)
        cut = jnp.concatenate(pieces(full[it, at, :]), axis=1)
        gram_sum[...] += contract(cut, jnp.concatenate([target[at, :], cut], axis=1), ((0,), (0,)))

    def loss_add(it, shard, c):
        at = rows_of(shard, c)
        one, two = pieces(full[it, at, :])
        wide = jnp.concatenate([one, one, two, two], axis=1)
        residual = contract(wide, tall[...], ((1,), (0,))) - target[at, :].astype(F32)
        loss_sum[...] += jnp.sum((residual * residual).reshape(ch // 8, 8, hl), axis=0)

    def arrived(way, s):
        it, b, c = split(s)
        p = place_of(way)
        return (p > 0) & (b <= p - 1), shard_at(way, p - 1 - b), c

    def for_arrived(act, it, s, own):
        first, first_shard, c = arrived(0, s)
        second, second_shard, _ = arrived(1, s)

        def one(i, carry):
            valid = jnp.where(i == 0, first, jnp.where(i == 1, second, own))
            shard = jnp.where(i == 0, first_shard, jnp.where(i == 1, second_shard, me))

            @pl.when(valid)
            def _():
                act(it, shard, c)

            return carry

        lax.fori_loop(0, 3, one, 0)

    def pre_gradient(it):
        total = gram_sum[:r, :] + gram_sum[r:, :]
        square = total[:, hl : hl + r] + total[:, hl + r :]
        now = mixed[...]
        d_mixed = jnp.dot(square, now, precision=HIGHEST, preferred_element_type=F32) - total[:, :hl]
        value = d_mixed * scale * (1.0 - now * now)
        for q in range(quarters):
            d_pre[it, mine, q] = value[:, q * 128 : (q + 1) * 128]

    def loss_close(it):
        total = loss_sum[:, 0:128]
        for q in range(128, hl, 128):
            total = total + loss_sum[:, q : q + 128]
        loss_in[mine, it * 8 : it * 8 + 8, :] = total
        loss_sum[...] = jnp.zeros_like(loss_sum)

    def combine(c_ref, it, k, q):
        total = c_ref[0, pl.ds(k, 1), :] * d_pre[it, 0, q]
        for e in range(1, experts):
            total = total + c_ref[e, pl.ds(k, 1), :] * d_pre[it, e, q]
        return total

    def columns(q):
        return slice(q * 128, (q + 1) * 128)

    def coef_pass(it, which):
        def one(k, carry):
            sums = [jnp.zeros((8, 128), F32)] * experts
            for q in which:
                values = bases[k, :, columns(q)]
                for e in range(experts):
                    held = values * d_pre[it, e, q]
                    sums[e] = sums[e] + jnp.sum(held.reshape(r // 8, 8, 128), axis=0)
            for e in range(experts):
                at = pl.ds(e * k_count + k, 1)
                value = jnp.sum(sums[e], axis=0, keepdims=True)
                coef_acc[at, :] = value if 0 in which else coef_acc[at, :] + value
            return carry

        lax.fori_loop(0, k_count, one, 0)

    def coef_send(it, losses=None):
        message[it, me] = jnp.zeros(message.shape[2:], F32)
        for i in range(blocks):
            column = jnp.sum(coef_acc[i * block : (i + 1) * block, :], axis=1, keepdims=True)
            message[it, me, i : i + 1, :] = to_lanes(jnp.broadcast_to(column, (block, 128)))
        if losses is not None:
            message[it, me, blocks : blocks + 1, :] = to_lanes(
                jnp.concatenate([lane_sums(losses[:8]), lane_sums(losses[8:])], axis=0)
            )
        for off in range(1, n):
            coef_copy(it, off).start()

    def coef_wait(it):
        for off in range(1, n):
            coef_copy(it, off).wait()

    def message_sum(it):
        total = message[it, 0]
        for c in range(1, n):
            total = total + message[it, c]
        return total

    def coef_table(total):
        held = [to_rows(total[i : i + 1, :], block) for i in range(blocks)]
        held = held[0] if blocks == 1 else jnp.concatenate(held, axis=0)
        return held.reshape(experts, k_count, 128)

    def bases_one(low, high):
        def one(k, carry):
            for q in range(quarters):
                gradient = combine(c_one, 0, k, q)
                b_grad[k, :, columns(q)] = ROOT_ONE * gradient
                bases[k, :, columns(q)] = adam_first(bases[k, :, columns(q)], gradient)
            return carry

        lax.fori_loop(low, high, one, 0)

    def bases_two(q):
        def one(k, carry):
            values = bases[k, :, columns(q)]
            bases[k, :, columns(q)] = adam_second(values, b_grad[k, :, columns(q)], combine(c_root, 1, k, q))
            return carry

        lax.fori_loop(0, k_count, one, 0, unroll=2)

    def factor_product(it, c):
        return jnp.dot(
            full[it, rows_of(me, c), :], gram[...], precision=HIGHEST, preferred_element_type=F32
        )

    def factor_one(c):
        at = chunk_of(c)
        g = (factor_product(0, c) - part[me, at, :]) * scale
        g_one[at, :] = ROOT_ONE * g
        full[1, rows_of(me, c), :] = adam_first(full[0, rows_of(me, c), :], g)

    def factor_two(c):
        at = chunk_of(c)
        g = (full[0, rows_of(me, c), :] - part[me, at, :]) * (ROOT_TWO * scale)
        f_out[at, :] = adam_second(full[1, rows_of(me, c), :], g_one[at, :], g)

    scope = jax.named_scope
    with scope("enter"):
        give_first(1)
        give_first(0)
    misc[...] = jnp.zeros_like(misc)
    loads[2].wait()
    misc[0:1, :k_count] = c_raw[...]
    c_one[mine] = to_rows(misc[0:1, :], k_count)
    gram_sum[...] = jnp.zeros_like(gram_sum)
    loss_sum[...] = jnp.zeros_like(loss_sum)
    with scope("load"):
        loads[1].wait()
    with scope("mix"):
        mix(c_one)
        gram_local()
    with scope("project"):
        for j in range(n):
            loads[3 + j].wait()
            project(j)

    @pl.when(me == 0)
    def _():
        pl.semaphore_wait(barrier, experts - 1)

    expert_start(c_one, 0)
    loads[0].wait()
    final = phase - chunks + LAG

    def early(s, carry):
        gram_hop(0, s, LAG)
        with scope("step"):
            step(s)
        own = s - LAG < chunks
        for_arrived(absorb, 0, s - LAG, own)
        for_arrived(loss_add, 0, s - LAG, own)
        return carry

    lax.fori_loop(LAG, final, early, 0)
    with scope("pre"):
        pre_gradient(0)
        expert_wait(c_one, 0)
        pre_start(0)
        gram_close(0)
        loss_close(0)
        gram_sum[...] = jnp.zeros_like(gram_sum)

    def base_work(i):
        if i == 0:
            with scope("forward"):
                for q in range(quarters):
                    pre_forward(0, q)
        elif i == 1:
            with scope("wait"):
                for q in range(quarters):
                    pre_wait(0, q)
            with scope("coef"):
                coef_pass(0, range(quarters))
                coef_send(0)
        elif i == 2:
            with scope("bases"):
                bases_one(0, k_count // 2)
        else:
            with scope("bases"):
                bases_one(k_count // 2, k_count)

    for c in range(chunks):
        with scope("step"):
            step(final + c)
        factor_one(c)
        absorb(1, me, c)
        base_work(c)

    begin = phase + chunks
    behind = begin - phase - LAG
    for s in range(final + chunks, begin):
        with scope("step"):
            step(s)
        for_arrived(absorb, 1, s - LAG, False)
    with scope("await"):
        coef_wait(0)
    c_grad[...] = coef_table(message_sum(0))
    c_two[...] = adam_first(c_one[...], c_grad[...])
    c_root[...] = ROOT_TWO * c_two[...]
    with scope("mix"):
        mix(c_two)
        gram_local()
    with scope("project"):
        for j in range(n):
            project(j)

    def late(s, carry):
        gram_hop(1, s, begin)
        with scope("step"):
            step(s)
        for_arrived(absorb, 1, s - LAG, False)
        for_arrived(loss_add, 1, s - LAG - behind, False)

        @pl.when(s - begin < chunks)
        def _():
            loss_add(1, me, s - begin)

        return carry

    end = phase + final
    lax.fori_loop(begin, end, late, 0)
    with scope("pre"):
        pre_gradient(1)
        pre_start(1)
        gram_close(1)
    with scope("product"):
        for c in range(chunks):
            full[0, rows_of(me, c), :] = factor_product(1, c)
    for s in range(end - LAG - behind, end - LAG):
        for_arrived(loss_add, 1, s, False)
    loss_close(1)
    expert_start(loss_in, 1)
    with scope("forward"):
        pre_forward(1, 0)
    with scope("step"):
        take(end)
    factor_two(0)
    with scope("wait"):
        pre_wait(1, 0)
    with scope("coef"):
        coef_pass(1, (0,))
    with scope("forward"):
        for q in range(1, quarters):
            pre_forward(1, q)
    with scope("bases"):
        bases_two(0)
    with scope("wait"):
        for q in range(1, quarters):
            pre_wait(1, q)
    with scope("coef"):
        if quarters > 1:
            coef_pass(1, range(1, quarters))
        expert_wait(loss_in, 1)
        losses = loss_in[0]
        for e in range(1, experts):
            losses = losses + loss_in[e]
        coef_send(1, losses)
    give(end)
    for q in range(1, quarters):
        with scope("bases"):
            bases_two(q)
        if q < chunks - 1:
            with scope("step"):
                take(end + q)
            factor_two(q)
    for c in range(max(quarters, 1), chunks - 1):
        take(end + c)
        factor_two(c)
    with scope("await"):
        coef_wait(1)
    with scope("coefs"):
        total = message_sum(1)
        own = pl.ds(mine * k_count, k_count)
        coef_acc[...] = coef_table(total).reshape(table, 128)
        misc[0:1, :] = to_lanes(adam_second(c_two[mine], ROOT_ONE * c_grad[mine], ROOT_TWO * coef_acc[own, :]))
        misc[1:2, :] = total[blocks : blocks + 1, :] * loss_scale
    with scope("step"):
        take(end + chunks - 1)
    with scope("factor"):
        factor_two(chunks - 1)


def hand_over(b_in, f_in, misc, b_out, f_out, c_out, l_out, sem):
    parts = 8
    size = b_in.shape[0] // parts
    copies = [pltpu.make_async_copy(f_in, f_out, sem.at[parts])]
    for i in range(parts):
        at = pl.ds(i * size, size)
        copies.append(pltpu.make_async_copy(b_in.at[at], b_out.at[at], sem.at[i]))
    for copy in copies:
        copy.start()
    c_out[...] = misc[0:1, : c_out.shape[1]]
    for i in range(2):
        l_out[i] = misc[1, 8 * i]
    for copy in copies:
        copy.wait()


def shards(target_weights, factors, bases, coefficients):
    n, experts = lax.axis_size("col"), lax.axis_size("expert")
    _, d, hl = target_weights.shape
    _, rows, r = factors.shape
    k = bases.shape[0]
    held = pl.BlockSpec(memory_space=pltpu.HBM)
    local = pl.BlockSpec(memory_space=pltpu.VMEM)
    dma = pltpu.SemaphoreType.DMA
    loss_scale = 1.0 / (2.0 * experts * d * hl * n)
    new_factors, new_bases, misc = pl.pallas_call(
        functools.partial(kernel, n, experts, loss_scale),
        out_shape=(
            pltpu.VMEM((rows, r), F32),
            pltpu.VMEM(bases.shape, F32),
            pltpu.VMEM((8, 128), F32),
        ),
        in_specs=[held, held, held, held],
        out_specs=(local, local, local),
        scratch_shapes=[
            pltpu.VMEM((d, hl), BF16),
            pltpu.VMEM(bases.shape, F32),
            pltpu.VMEM((2, d, r), F32),
            pltpu.VMEM((n, rows, r), F32),
            pltpu.VMEM((2, n - 1, rows, r), F32),
            pltpu.VMEM((2, experts, hl // 128, r, 128), F32),
            pltpu.VMEM((experts, k, 128), F32),
            pltpu.VMEM((experts, k, 128), F32),
            pltpu.VMEM((experts, k, 128), F32),
            pltpu.VMEM((experts, k, 128), F32),
            pltpu.VMEM((experts * k, 128), F32),
            pltpu.VMEM((2, n, experts * k // min(experts * k, 128) + 1, 128), F32),
            pltpu.VMEM((experts, 16, 128), F32),
            pltpu.VMEM((rows, r), F32),
            pltpu.VMEM((2 * r, hl + 2 * r), F32),
            pltpu.VMEM((r, hl), F32),
            pltpu.VMEM((4 * r, hl), BF16),
            pltpu.VMEM((8, hl), F32),
            pltpu.VMEM((r, r), F32),
            pltpu.VMEM((r // 2 + 8, r), F32),
            pltpu.VMEM((2, 2, r // 2 + 8, r), F32),
            pltpu.VMEM((2, 2, r // 2 + 8, r), F32),
            pltpu.VMEM((1, k), F32),
            pltpu.SemaphoreType.REGULAR,
            dma((3 + n,)),
            dma((2, SEMS)),
            dma((2, SEMS)),
            dma((2, 2)),
            dma((2, 2)),
            dma((2, experts - 1)),
            dma((2, experts - 1)),
            dma((2, hl // 128, experts - 1)),
            dma((2, hl // 128, experts - 1)),
            dma((2, n - 1)),
            dma((2, n - 1)),
        ],
        compiler_params=pltpu.CompilerParams(
            collective_id=0, has_side_effects=True, vmem_limit_bytes=VMEM_MAIN
        ),
    )(target_weights[0], factors[0], bases, coefficients)
    new_bases, new_factors, new_coef, losses = pl.pallas_call(
        hand_over,
        out_shape=(
            jax.ShapeDtypeStruct(bases.shape, F32),
            jax.ShapeDtypeStruct((rows, r), F32),
            jax.ShapeDtypeStruct((1, k), F32),
            jax.ShapeDtypeStruct((2,), F32),
        ),
        in_specs=[local, local, local],
        out_specs=(held, held, local, pl.BlockSpec(memory_space=pltpu.SMEM)),
        scratch_shapes=[dma((9,))],
        compiler_params=pltpu.CompilerParams(vmem_limit_bytes=VMEM_LAST),
    )(new_bases, new_factors, misc)
    return (new_factors[None], new_bases, new_coef, losses)


def solution(mesh):
    return jax.shard_map(
        shards,
        mesh=mesh,
        in_specs=(
            P(("layer", "expert"), None, "col"),
            P(("layer", "expert"), "col", None),
            P("layer", None, "col"),
            P(("layer", "expert"), None),
        ),
        out_specs=(
            P(("layer", "expert"), "col", None),
            P("layer", None, "col"),
            P(("layer", "expert"), None),
            P("layer"),
        ),
        check_vma=False,
    )
```

```python
import functools

import jax
import jax.numpy as jnp
from jax import lax
from jax.experimental import pallas as pl
from jax.experimental.pallas import tpu as pltpu
from jax.sharding import PartitionSpec as P

LEARN_RATE = 0.01
BETA_ONE = 0.9
BETA_TWO = 0.999
EPSILON = 0.0001
HIGHEST = lax.Precision.HIGHEST
MESH = pl.DeviceIdType.MESH
F32 = jnp.float32
BF16 = jnp.bfloat16
CHUNKS = 4
LAG = 3
VMEM_MAIN = 57000000
VMEM_LAST = 4000000


def adam_first(parameter, g):
    return parameter - LEARN_RATE * g / (jnp.abs(g) + EPSILON)


ROOT_ONE = (BETA_TWO * (1.0 - BETA_TWO) / (1.0 - BETA_TWO**2)) ** 0.5
ROOT_TWO = ((1.0 - BETA_TWO) / (1.0 - BETA_TWO**2)) ** 0.5
RATE_ONE = LEARN_RATE * BETA_ONE * (1.0 - BETA_ONE) / (1.0 - BETA_ONE**2) / ROOT_ONE
RATE_TWO = LEARN_RATE * (1.0 - BETA_ONE) / (1.0 - BETA_ONE**2) / ROOT_TWO


def adam_second(parameter, h_one, h_two):
    second = h_one * h_one + h_two * h_two
    root = second * lax.rsqrt(jnp.maximum(second, 1e-30))
    return parameter - (RATE_ONE * h_one + RATE_TWO * h_two) / (root + EPSILON)


def pieces(x):
    upper = x.astype(BF16)
    return upper, (x - upper.astype(F32)).astype(BF16)


def contract(a, b, dims):
    return lax.dot_general(a, b, (dims, ((), ())), preferred_element_type=F32)


def diagonal(size):
    shape = (size, 128)
    return lax.broadcasted_iota(jnp.int32, shape, 0) == lax.broadcasted_iota(jnp.int32, shape, 1)


def to_lanes(column):
    return jnp.sum(jnp.where(diagonal(column.shape[0]), column, 0.0), axis=0, keepdims=True)


def places(shape):
    return lax.broadcasted_iota(jnp.int32, shape, 0), lax.broadcasted_iota(jnp.int32, shape, 1)


def pack_symmetric(g):
    half = g.shape[0] // 2
    row, lane = places((half, 2 * half))
    turned = pltpu.roll(g[half:], half, 1)
    top = jnp.where((lane > row) & (lane < half), turned, g[:half])
    diagonal_row = jnp.sum(jnp.where(lane == row, turned, 0.0), axis=0, keepdims=True)
    return jnp.concatenate([top, jnp.broadcast_to(diagonal_row, (8, 2 * half))], axis=0)


def unpack_symmetric(p):
    half = p.shape[1] // 2
    row, lane = places((half, 2 * half))
    top, diagonal_row = p[:half], jnp.broadcast_to(p[half : half + 1], (half, 2 * half))
    flipped = jnp.transpose(jnp.concatenate([top, top], axis=0))
    upper = jnp.where((lane > row) & (lane < half), flipped[:half], top)
    last = jnp.where(lane > row, top, jnp.where(lane < row, flipped[:half], diagonal_row))
    lower = jnp.where(lane < half, flipped[half:], pltpu.roll(last, half, 1))
    return jnp.concatenate([upper, lower], axis=0)


def lane_sums(x):
    total = jnp.sum(x, axis=(0, 1), keepdims=True)
    return jnp.where(lax.broadcasted_iota(jnp.int32, x.shape, 0) == 0, jnp.broadcast_to(total, x.shape), 0.0)


def to_rows(row, size):
    held = jnp.where(diagonal(size), jnp.broadcast_to(row, (size, 128)), 0.0)
    return jnp.broadcast_to(jnp.sum(held, axis=1, keepdims=True), (size, 128))


def kernel(
    n, experts, loss_scale, t_hbm, f_hbm, b_hbm, c_hbm, f_out, bases, misc,
    target, b_grad, full, part, landed, d_pre, c_one, c_two, c_root, c_grad, coef_acc, message, loss_in, g_one, gram_sum,
    mixed, tall, loss_sum, gram, gram_packed, gram_in, gram_go, c_raw,
    entered, load_sem, z_send, z_recv, gram_send, gram_recv, ex_send, ex_recv, pre_send, pre_recv, co_send, co_recv,
):
    me = lax.axis_index("col")
    mine = lax.axis_index("expert")
    rows, r = f_hbm.shape
    d, hl = target.shape
    k_count = bases.shape[0]
    scale = 1.0 / (hl * n)
    table = experts * k_count
    block = min(table, 128)
    blocks = table // block
    chunks = CHUNKS
    ch = rows // chunks
    phase = n * chunks
    quarters = hl // 128
    pairs = experts // 2
    mate = mine + 1 - 2 * lax.rem(mine, 2)

    barrier = pltpu.get_barrier_semaphore()

    @pl.when(me < n - 1)
    def _():
        pl.semaphore_signal(barrier, inc=1, device_id={"col": me + 1}, device_id_type=MESH)

    for off in range(1, experts):
        pl.semaphore_signal(barrier, inc=1, device_id={"expert": lax.rem(mine + off, experts)}, device_id_type=MESH)
    loads = [
        pltpu.make_async_copy(f_hbm, full.at[0, pl.ds(pl.multiple_of(me * rows, 16), rows)], load_sem.at[0]),
        pltpu.make_async_copy(b_hbm, bases, load_sem.at[1]),
        pltpu.make_async_copy(c_hbm, c_raw, load_sem.at[2]),
    ]
    halves = 2 if n % 2 == 0 else 1
    for j in range(halves):
        at = pl.ds(j * (d // halves), d // halves)
        loads.append(pltpu.make_async_copy(t_hbm.at[at], target.at[at], load_sem.at[3 + j]))
    for load in loads:
        load.start()

    @pl.when(me > 0)
    def _():
        pl.semaphore_wait(barrier, experts)
        pl.semaphore_signal(entered, inc=1, device_id={"col": me - 1}, device_id_type=MESH)

    def place_of(way):
        return me if way == 0 else n - 1 - me

    def shard_at(way, place):
        return place if way == 0 else n - 1 - place

    def split(s):
        it = s // phase
        u = s - it * phase
        b = u // chunks
        return it, b, u - b * chunks

    def z_copy(way, s, src, dst):
        return pltpu.make_async_remote_copy(
            src_ref=src, dst_ref=dst, send_sem=z_send.at[way, s % LAG], recv_sem=z_recv.at[way, s % (2 * LAG)],
            device_id={"col": me + 1 - 2 * way}, device_id_type=MESH,
        )

    def rows_of(shard, c):
        return pl.ds(pl.multiple_of(shard * rows + c * ch, 16), ch)

    def chunk_of(c):
        return pl.ds(pl.multiple_of(c * ch, 16), ch)

    def gather_copy(way, s, shard):
        it, b, c = split(s)
        ref = full.at[it, rows_of(shard, c)]
        return z_copy(way, s, ref, ref)

    def scatter_copy(way, s, shard):
        it, b, c = split(s)
        return z_copy(way, s, part.at[shard, chunk_of(c)], landed.at[way, b - 1, chunk_of(c)])

    def on_send(way, s, act):
        it, b, c = split(s)
        p = place_of(way)

        @pl.when((p < n - 1) & (b <= p))
        def _():
            act(gather_copy(way, s, shard_at(way, p - b)))

        @pl.when((p < n - 1) & (b > p))
        def _():
            act(scatter_copy(way, s, shard_at(way, n + p - b)))

    def arrive(way, s):
        it, b, c = split(s)
        p = place_of(way)

        @pl.when((p > 0) & (b <= p - 1))
        def _():
            gather_copy(way, s, shard_at(way, p - 1 - b)).wait_recv()

        @pl.when((p > 0) & (b > p - 1))
        def _():
            shard = shard_at(way, n + p - 1 - b)
            scatter_copy(way, s, shard).wait_recv()
            at = chunk_of(c)
            part[shard, at, :] = part[shard, at, :] + landed[way, b - 1, at, :]

    def take(s):
        for way in range(2):
            on_send(way, s - LAG, lambda copy: copy.wait_send())
        for way in range(2):
            arrive(way, s - LAG)

    def give(s):
        for way in range(2):
            on_send(way, s, lambda copy: copy.start())

    def step(s):
        take(s)
        give(s)

    def give_first(way):
        @pl.when(place_of(way) < n - 1)
        def _():
            if way == 0:
                pl.semaphore_wait(entered, 1)
            for s in range(LAG):
                z_copy(way, s, f_hbm.at[chunk_of(s)], full.at[0, rows_of(me, s)]).start()

    def gram_copy(it, way):
        return pltpu.make_async_remote_copy(
            src_ref=gram_go.at[it, way], dst_ref=gram_in.at[it, way], send_sem=gram_send.at[it, way],
            recv_sem=gram_recv.at[it, way], device_id={"col": me + 1 - 2 * way}, device_id_type=MESH,
        )

    def gram_hop(it, s, start):
        for way in range(2):
            p = place_of(way)
            now = s == start + p * LAG

            @pl.when(now & (p > 0))
            def _():
                gram_copy(it, way).wait_recv()

            @pl.when(now & (p == 0) & (p < n - 1))
            def _():
                gram_go[it, way] = gram_packed[...]

            @pl.when(now & (p > 0) & (p < n - 1))
            def _():
                gram_go[it, way] = gram_packed[...] + gram_in[it, way]

            @pl.when(now & (p < n - 1))
            def _():
                gram_copy(it, way).start()

    def gram_close(it):
        for way in range(2):
            p = place_of(way)

            @pl.when(p > 0)
            def _():
                gram_packed[...] = gram_packed[...] + gram_in[it, way]

            @pl.when(p < n - 1)
            def _():
                gram_copy(it, way).wait_send()

        gram[...] = unpack_symmetric(gram_packed[...])

    def expert_copy(ref, kind, off):
        place = ref.at[mine]
        return pltpu.make_async_remote_copy(
            src_ref=place, dst_ref=place, send_sem=ex_send.at[kind, off - 1], recv_sem=ex_recv.at[kind, off - 1],
            device_id={"expert": lax.rem(mine + off, experts)}, device_id_type=MESH,
        )

    def expert_start(ref, kind):
        for off in range(1, experts):
            expert_copy(ref, kind, off).start()

    def expert_wait(ref, kind):
        for off in range(1, experts):
            expert_copy(ref, kind, off).wait()

    def pre_copy(it, q, e, i, target):
        place = d_pre.at[it, e] if it == 0 else d_pre.at[it, e, q]
        return pltpu.make_async_remote_copy(
            src_ref=place, dst_ref=place, send_sem=pre_send.at[it + q, i], recv_sem=pre_recv.at[it + q, i],
            device_id={"expert": target}, device_id_type=MESH,
        )

    def across(i):
        return lax.rem(mine + 2 * i, experts)

    def pre_start(it):
        for q in range(quarters if it else 1):
            for i in range(1, pairs):
                pre_copy(it, q, mine, i - 1, across(i)).start()
            pre_copy(it, q, mine, pairs - 1, mate).start()

    def pre_forward(it, q):
        for i in range(1, pairs):
            source = across(pairs - i)
            pre_copy(it, q, source, i - 1, mate).wait_recv()
            pre_copy(it, q, source, pairs - 1 + i, mate).start()

    def pre_wait(it, q):
        for i in range(1, pairs):
            pre_copy(it, q, mine, i - 1, across(i)).wait_send()
        pre_copy(it, q, mine, pairs - 1, mate).wait_send()
        pre_copy(it, q, mate, pairs - 1, mate).wait_recv()
        for i in range(1, pairs):
            pre_copy(it, q, across(pairs - i), pairs - 1 + i, mate).wait_send()
            pre_copy(it, q, lax.rem(mate + 2 * (pairs - i), experts), pairs - 1 + i, mate).wait_recv()

    def coef_copy(it, off):
        place = message.at[it, me]
        return pltpu.make_async_remote_copy(
            src_ref=place, dst_ref=place, send_sem=co_send.at[it, off - 1], recv_sem=co_recv.at[it, off - 1],
            device_id={"col": lax.rem(me + off, n)}, device_id_type=MESH,
        )

    def mix(c_ref):
        for q in range(0, hl, 128):
            def add(k, total):
                return total + c_ref[mine, pl.ds(k, 1), :] * bases[k, :, q : q + 128]

            value = jnp.tanh(lax.fori_loop(0, k_count, add, jnp.zeros((r, 128), F32), unroll=4))
            mixed[:, q : q + 128] = value
            upper, lower = pieces(value)
            for i in range(2):
                tall[2 * i * r : (2 * i + 1) * r, q : q + 128] = upper
                tall[(2 * i + 1) * r : (2 * i + 2) * r, q : q + 128] = lower

    def gram_local():
        cut = tall[: 2 * r, :]
        both = contract(cut, cut, ((1,), (1,)))
        both = both[:r] + both[r:]
        gram_packed[...] = pack_symmetric(both[:, :r] + both[:, r:])

    def project(j):
        def one(c, carry):
            value = contract(target[rows_of(j, c), :], tall[: 2 * r, :], ((1,), (1,)))
            part[j, chunk_of(c), :] = value[:, :r] + value[:, r:]
            return carry

        lax.fori_loop(0, chunks, one, 0)

    def absorb(it, shard, c):
        at = rows_of(shard, c)
        cut = jnp.concatenate(pieces(full[it, at, :]), axis=1)
        gram_sum[...] += contract(cut, jnp.concatenate([target[at, :], cut], axis=1), ((0,), (0,)))

    def loss_add(it, shard, c):
        at = rows_of(shard, c)
        one, two = pieces(full[it, at, :])
        wide = jnp.concatenate([one, one, two, two], axis=1)
        residual = contract(wide, tall[...], ((1,), (0,))) - target[at, :].astype(F32)
        loss_sum[...] += jnp.sum((residual * residual).reshape(ch // 8, 8, hl), axis=0)

    def arrived(way, s):
        it, b, c = split(s)
        p = place_of(way)
        return (p > 0) & (b <= p - 1), shard_at(way, p - 1 - b), c

    def for_arrived(act, it, s, own):
        first, first_shard, c = arrived(0, s)
        second, second_shard, _ = arrived(1, s)

        def one(i, carry):
            valid = jnp.where(i == 0, first, jnp.where(i == 1, second, own))
            shard = jnp.where(i == 0, first_shard, jnp.where(i == 1, second_shard, me))

            @pl.when(valid)
            def _():
                act(it, shard, c)

            return carry

        lax.fori_loop(0, 3, one, 0)

    def pre_gradient(it):
        total = gram_sum[:r, :] + gram_sum[r:, :]
        square = total[:, hl : hl + r] + total[:, hl + r :]
        now = mixed[...]
        d_mixed = jnp.dot(square, now, precision=HIGHEST, preferred_element_type=F32) - total[:, :hl]
        value = d_mixed * scale * (1.0 - now * now)
        for q in range(quarters):
            d_pre[it, mine, q] = value[:, q * 128 : (q + 1) * 128]

    def loss_close(it):
        total = loss_sum[:, 0:128]
        for q in range(128, hl, 128):
            total = total + loss_sum[:, q : q + 128]
        loss_in[mine, it * 8 : it * 8 + 8, :] = total
        loss_sum[...] = jnp.zeros_like(loss_sum)

    def combine(c_ref, it, k, q):
        total = c_ref[0, pl.ds(k, 1), :] * d_pre[it, 0, q]
        for e in range(1, experts):
            total = total + c_ref[e, pl.ds(k, 1), :] * d_pre[it, e, q]
        return total

    def columns(q):
        return slice(q * 128, (q + 1) * 128)

    def coef_pass(it, which):
        def one(k, carry):
            sums = [jnp.zeros((8, 128), F32)] * experts
            for q in which:
                values = bases[k, :, columns(q)]
                for e in range(experts):
                    held = values * d_pre[it, e, q]
                    sums[e] = sums[e] + jnp.sum(held.reshape(r // 8, 8, 128), axis=0)
            for e in range(experts):
                at = pl.ds(e * k_count + k, 1)
                value = jnp.sum(sums[e], axis=0, keepdims=True)
                coef_acc[at, :] = value if 0 in which else coef_acc[at, :] + value
            return carry

        lax.fori_loop(0, k_count, one, 0)

    def coef_send(it, losses=None):
        message[it, me] = jnp.zeros(message.shape[2:], F32)
        for i in range(blocks):
            column = jnp.sum(coef_acc[i * block : (i + 1) * block, :], axis=1, keepdims=True)
            message[it, me, i : i + 1, :] = to_lanes(jnp.broadcast_to(column, (block, 128)))
        if losses is not None:
            message[it, me, blocks : blocks + 1, :] = to_lanes(
                jnp.concatenate([lane_sums(losses[:8]), lane_sums(losses[8:])], axis=0)
            )
        for off in range(1, n):
            coef_copy(it, off).start()

    def coef_wait(it):
        for off in range(1, n):
            coef_copy(it, off).wait()

    def message_sum(it):
        total = message[it, 0]
        for c in range(1, n):
            total = total + message[it, c]
        return total

    def coef_table(total):
        held = [to_rows(total[i : i + 1, :], block) for i in range(blocks)]
        held = held[0] if blocks == 1 else jnp.concatenate(held, axis=0)
        return held.reshape(experts, k_count, 128)

    def bases_one(low, high):
        def one(k, carry):
            for q in range(quarters):
                gradient = combine(c_one, 0, k, q)
                b_grad[k, :, columns(q)] = ROOT_ONE * gradient
                bases[k, :, columns(q)] = adam_first(bases[k, :, columns(q)], gradient)
            return carry

        lax.fori_loop(low, high, one, 0)

    def bases_two(q):
        def one(k, carry):
            values = bases[k, :, columns(q)]
            bases[k, :, columns(q)] = adam_second(values, b_grad[k, :, columns(q)], combine(c_root, 1, k, q))
            return carry

        lax.fori_loop(0, k_count, one, 0, unroll=2)

    def factor_product(it, c):
        return jnp.dot(
            full[it, rows_of(me, c), :], gram[...], precision=HIGHEST, preferred_element_type=F32
        )

    def factor_one(c):
        at = chunk_of(c)
        g = (factor_product(0, c) - part[me, at, :]) * scale
        g_one[at, :] = ROOT_ONE * g
        full[1, rows_of(me, c), :] = adam_first(full[0, rows_of(me, c), :], g)

    def factor_two(c):
        at = chunk_of(c)
        g = (full[0, rows_of(me, c), :] - part[me, at, :]) * (ROOT_TWO * scale)
        f_out[at, :] = adam_second(full[1, rows_of(me, c), :], g_one[at, :], g)

    scope = jax.named_scope
    with scope("enter"):
        give_first(1)
        give_first(0)
    misc[...] = jnp.zeros_like(misc)
    loads[2].wait()
    misc[0:1, :k_count] = c_raw[...]
    c_one[mine] = to_rows(misc[0:1, :], k_count)
    gram_sum[...] = jnp.zeros_like(gram_sum)
    loss_sum[...] = jnp.zeros_like(loss_sum)
    with scope("load"):
        loads[1].wait()
    with scope("mix"):
        mix(c_one)
        gram_local()
    with scope("project"):
        for j in range(n):
            if j % (n // halves) == 0:
                loads[3 + j // (n // halves)].wait()
            project(j)

    @pl.when(me == 0)
    def _():
        pl.semaphore_wait(barrier, experts - 1)

    expert_start(c_one, 0)
    loads[0].wait()
    final = phase - chunks + LAG

    def early(s, carry):
        gram_hop(0, s, LAG)
        with scope("step"):
            step(s)
        own = s - LAG < chunks
        for_arrived(absorb, 0, s - LAG, own)
        for_arrived(loss_add, 0, s - LAG, own)
        return carry

    lax.fori_loop(LAG, final, early, 0)
    with scope("pre"):
        pre_gradient(0)
        expert_wait(c_one, 0)
        pre_start(0)
        gram_close(0)
        loss_close(0)
        gram_sum[...] = jnp.zeros_like(gram_sum)

    def base_work(i):
        if i == 0:
            with scope("forward"):
                pre_forward(0, 0)
        elif i == 1:
            with scope("wait"):
                pre_wait(0, 0)
            with scope("coef"):
                coef_pass(0, range(quarters))
                coef_send(0)
        elif i == 2:
            with scope("bases"):
                bases_one(0, k_count // 2)
        else:
            with scope("bases"):
                bases_one(k_count // 2, k_count)

    for c in range(chunks):
        with scope("step"):
            step(final + c)
        factor_one(c)
        absorb(1, me, c)
        base_work(c)

    begin = phase + chunks
    behind = begin - phase - LAG
    for s in range(final + chunks, begin):
        with scope("step"):
            step(s)
        for_arrived(absorb, 1, s - LAG, False)
    with scope("await"):
        coef_wait(0)
    c_grad[...] = coef_table(message_sum(0))
    c_two[...] = adam_first(c_one[...], c_grad[...])
    c_root[...] = ROOT_TWO * c_two[...]
    with scope("mix"):
        mix(c_two)
        gram_local()
    with scope("project"):
        for j in range(n):
            project(j)

    def late(s, carry):
        gram_hop(1, s, begin)
        with scope("step"):
            step(s)
        for_arrived(absorb, 1, s - LAG, False)
        for_arrived(loss_add, 1, s - LAG - behind, False)

        @pl.when(s - begin < chunks)
        def _():
            loss_add(1, me, s - begin)

        return carry

    end = phase + final
    lax.fori_loop(begin, end, late, 0)
    with scope("pre"):
        pre_gradient(1)
        pre_start(1)
        gram_close(1)
    with scope("product"):
        for c in range(chunks):
            full[0, rows_of(me, c), :] = factor_product(1, c)
    for s in range(end - LAG - behind, end - LAG):
        for_arrived(loss_add, 1, s, False)
    loss_close(1)
    expert_start(loss_in, 1)
    with scope("forward"):
        pre_forward(1, 0)
    with scope("step"):
        take(end)
    factor_two(0)
    with scope("wait"):
        pre_wait(1, 0)
    with scope("coef"):
        coef_pass(1, (0,))
    with scope("forward"):
        for q in range(1, quarters):
            pre_forward(1, q)
    with scope("bases"):
        bases_two(0)
    with scope("wait"):
        for q in range(1, quarters):
            pre_wait(1, q)
    with scope("coef"):
        if quarters > 1:
            coef_pass(1, range(1, quarters))
        expert_wait(loss_in, 1)
        losses = loss_in[0]
        for e in range(1, experts):
            losses = losses + loss_in[e]
        coef_send(1, losses)
    give(end)
    for q in range(1, quarters):
        with scope("bases"):
            bases_two(q)
        if q < chunks - 1:
            with scope("step"):
                take(end + q)
            factor_two(q)
    for c in range(max(quarters, 1), chunks - 1):
        take(end + c)
        factor_two(c)
    with scope("await"):
        coef_wait(1)
    with scope("coefs"):
        total = message_sum(1)
        own = pl.ds(mine * k_count, k_count)
        coef_acc[...] = coef_table(total).reshape(table, 128)
        misc[0:1, :] = to_lanes(adam_second(c_two[mine], ROOT_ONE * c_grad[mine], ROOT_TWO * coef_acc[own, :]))
        misc[1:2, :] = total[blocks : blocks + 1, :] * loss_scale
    with scope("step"):
        take(end + chunks - 1)
    with scope("factor"):
        factor_two(chunks - 1)


def hand_over(b_in, f_in, misc, b_out, f_out, c_out, l_out, sem):
    parts = 8
    size = b_in.shape[0] // parts
    copies = [pltpu.make_async_copy(f_in, f_out, sem.at[parts])]
    for i in range(parts):
        at = pl.ds(i * size, size)
        copies.append(pltpu.make_async_copy(b_in.at[at], b_out.at[at], sem.at[i]))
    for copy in copies:
        copy.start()
    c_out[...] = misc[0:1, : c_out.shape[1]]
    for i in range(2):
        l_out[i] = misc[1, 8 * i]
    for copy in copies:
        copy.wait()


def shards(target_weights, factors, bases, coefficients):
    n, experts = lax.axis_size("col"), lax.axis_size("expert")
    _, d, hl = target_weights.shape
    _, rows, r = factors.shape
    k = bases.shape[0]
    held = pl.BlockSpec(memory_space=pltpu.HBM)
    local = pl.BlockSpec(memory_space=pltpu.VMEM)
    dma = pltpu.SemaphoreType.DMA
    loss_scale = 1.0 / (2.0 * experts * d * hl * n)
    new_factors, new_bases, misc = pl.pallas_call(
        functools.partial(kernel, n, experts, loss_scale),
        out_shape=(
            pltpu.VMEM((rows, r), F32),
            pltpu.VMEM(bases.shape, F32),
            pltpu.VMEM((8, 128), F32),
        ),
        in_specs=[held, held, held, held],
        out_specs=(local, local, local),
        scratch_shapes=[
            pltpu.VMEM((d, hl), BF16),
            pltpu.VMEM(bases.shape, F32),
            pltpu.VMEM((2, d, r), F32),
            pltpu.VMEM((n, rows, r), F32),
            pltpu.VMEM((2, n - 1, rows, r), F32),
            pltpu.VMEM((2, experts, hl // 128, r, 128), F32),
            pltpu.VMEM((experts, k, 128), F32),
            pltpu.VMEM((experts, k, 128), F32),
            pltpu.VMEM((experts, k, 128), F32),
            pltpu.VMEM((experts, k, 128), F32),
            pltpu.VMEM((experts * k, 128), F32),
            pltpu.VMEM((2, n, experts * k // min(experts * k, 128) + 1, 128), F32),
            pltpu.VMEM((experts, 16, 128), F32),
            pltpu.VMEM((rows, r), F32),
            pltpu.VMEM((2 * r, hl + 2 * r), F32),
            pltpu.VMEM((r, hl), F32),
            pltpu.VMEM((4 * r, hl), BF16),
            pltpu.VMEM((8, hl), F32),
            pltpu.VMEM((r, r), F32),
            pltpu.VMEM((r // 2 + 8, r), F32),
            pltpu.VMEM((2, 2, r // 2 + 8, r), F32),
            pltpu.VMEM((2, 2, r // 2 + 8, r), F32),
            pltpu.VMEM((1, k), F32),
            pltpu.SemaphoreType.REGULAR,
            dma((5,)),
            dma((2, LAG)),
            dma((2, 2 * LAG)),
            dma((2, 2)),
            dma((2, 2)),
            dma((2, experts - 1)),
            dma((2, experts - 1)),
            dma((1 + hl // 128, experts - 1)),
            dma((1 + hl // 128, experts - 1)),
            dma((2, n - 1)),
            dma((2, n - 1)),
        ],
        compiler_params=pltpu.CompilerParams(
            collective_id=0, has_side_effects=True, vmem_limit_bytes=VMEM_MAIN
        ),
    )(target_weights[0], factors[0], bases, coefficients)
    new_bases, new_factors, new_coef, losses = pl.pallas_call(
        hand_over,
        out_shape=(
            jax.ShapeDtypeStruct(bases.shape, F32),
            jax.ShapeDtypeStruct((rows, r), F32),
            jax.ShapeDtypeStruct((1, k), F32),
            jax.ShapeDtypeStruct((2,), F32),
        ),
        in_specs=[local, local, local],
        out_specs=(held, held, local, pl.BlockSpec(memory_space=pltpu.SMEM)),
        scratch_shapes=[dma((9,))],
        compiler_params=pltpu.CompilerParams(vmem_limit_bytes=VMEM_LAST),
    )(new_bases, new_factors, misc)
    return (new_factors[None], new_bases, new_coef, losses)


def solution(mesh):
    return jax.shard_map(
        shards,
        mesh=mesh,
        in_specs=(
            P(("layer", "expert"), None, "col"),
            P(("layer", "expert"), "col", None),
            P("layer", None, "col"),
            P(("layer", "expert"), None),
        ),
        out_specs=(
            P(("layer", "expert"), "col", None),
            P("layer", None, "col"),
            P(("layer", "expert"), None),
            P("layer"),
        ),
        check_vma=False,
    )
```

```python
import functools

import jax
import jax.numpy as jnp
from jax import lax
from jax.experimental import pallas as pl
from jax.experimental.pallas import tpu as pltpu
from jax.sharding import PartitionSpec as P

LEARN_RATE = 0.01
BETA_ONE = 0.9
BETA_TWO = 0.999
EPSILON = 0.0001
HIGHEST = lax.Precision.HIGHEST
MESH = pl.DeviceIdType.MESH
F32 = jnp.float32
BF16 = jnp.bfloat16
CHUNKS = 4
LAG = 3
VMEM_MAIN = 57000000
VMEM_LAST = 4000000


def adam_first(parameter, g):
    return parameter - LEARN_RATE * g / (jnp.abs(g) + EPSILON)


ROOT_ONE = (BETA_TWO * (1.0 - BETA_TWO) / (1.0 - BETA_TWO**2)) ** 0.5
ROOT_TWO = ((1.0 - BETA_TWO) / (1.0 - BETA_TWO**2)) ** 0.5
RATE_ONE = LEARN_RATE * BETA_ONE * (1.0 - BETA_ONE) / (1.0 - BETA_ONE**2) / ROOT_ONE
RATE_TWO = LEARN_RATE * (1.0 - BETA_ONE) / (1.0 - BETA_ONE**2) / ROOT_TWO


def adam_second(parameter, h_one, h_two):
    second = h_one * h_one + h_two * h_two
    root = second * lax.rsqrt(jnp.maximum(second, 1e-30))
    return parameter - (RATE_ONE * h_one + RATE_TWO * h_two) / (root + EPSILON)


def pieces(x):
    upper = x.astype(BF16)
    return upper, (x - upper.astype(F32)).astype(BF16)


def contract(a, b, dims):
    return lax.dot_general(a, b, (dims, ((), ())), preferred_element_type=F32)


def diagonal(size):
    shape = (size, 128)
    return lax.broadcasted_iota(jnp.int32, shape, 0) == lax.broadcasted_iota(jnp.int32, shape, 1)


def to_lanes(column):
    return jnp.sum(jnp.where(diagonal(column.shape[0]), column, 0.0), axis=0, keepdims=True)


def places(shape):
    return lax.broadcasted_iota(jnp.int32, shape, 0), lax.broadcasted_iota(jnp.int32, shape, 1)


def pack_symmetric(g):
    half = g.shape[0] // 2
    row, lane = places((half, 2 * half))
    turned = pltpu.roll(g[half:], half, 1)
    top = jnp.where((lane > row) & (lane < half), turned, g[:half])
    diagonal_row = jnp.sum(jnp.where(lane == row, turned, 0.0), axis=0, keepdims=True)
    return jnp.concatenate([top, jnp.broadcast_to(diagonal_row, (8, 2 * half))], axis=0)


def unpack_symmetric(p):
    half = p.shape[1] // 2
    row, lane = places((half, 2 * half))
    top, diagonal_row = p[:half], jnp.broadcast_to(p[half : half + 1], (half, 2 * half))
    flipped = jnp.transpose(jnp.concatenate([top, top], axis=0))
    upper = jnp.where((lane > row) & (lane < half), flipped[:half], top)
    last = jnp.where(lane > row, top, jnp.where(lane < row, flipped[:half], diagonal_row))
    lower = jnp.where(lane < half, flipped[half:], pltpu.roll(last, half, 1))
    return jnp.concatenate([upper, lower], axis=0)


def lane_sums(x):
    total = jnp.sum(x, axis=(0, 1), keepdims=True)
    return jnp.where(lax.broadcasted_iota(jnp.int32, x.shape, 0) == 0, jnp.broadcast_to(total, x.shape), 0.0)


def to_rows(row, size):
    held = jnp.where(diagonal(size), jnp.broadcast_to(row, (size, 128)), 0.0)
    return jnp.broadcast_to(jnp.sum(held, axis=1, keepdims=True), (size, 128))


def kernel(
    n, experts, loss_scale, t_hbm, f_hbm, b_hbm, c_hbm, f_out, bases, misc,
    target, b_grad, full, part, landed, d_pre, c_one, c_two, c_root, c_grad, coef_acc, message, loss_in, g_one, gram_sum,
    mixed, tall, loss_sum, gram, gram_packed, gram_in, gram_go, c_raw,
    entered, above, known, load_sem, z_send, z_recv, gram_send, gram_recv, ex_send, ex_recv, pre_send, pre_recv, co_send, co_recv,
):
    me = lax.axis_index("col")
    mine = lax.axis_index("expert")
    rows, r = f_hbm.shape
    d, hl = target.shape
    k_count = bases.shape[0]
    scale = 1.0 / (hl * n)
    table = experts * k_count
    block = min(table, 128)
    blocks = table // block
    chunks = CHUNKS
    ch = rows // chunks
    phase = n * chunks
    quarters = hl // 128
    pairs = experts // 2
    mate = mine + 1 - 2 * lax.rem(mine, 2)

    barrier = pltpu.get_barrier_semaphore()

    @pl.when(me < n - 1)
    def _():
        pl.semaphore_signal(barrier, inc=1, device_id={"col": me + 1}, device_id_type=MESH)

    def greet_experts(semaphore):
        for off in range(1, experts):
            pl.semaphore_signal(
                semaphore, inc=1, device_id={"expert": lax.rem(mine + off, experts)}, device_id_type=MESH
            )

    @pl.when(me == 0)
    def _():
        greet_experts(barrier)

    loads = [
        pltpu.make_async_copy(f_hbm, full.at[0, pl.ds(pl.multiple_of(me * rows, 16), rows)], load_sem.at[0]),
        pltpu.make_async_copy(b_hbm, bases, load_sem.at[1]),
        pltpu.make_async_copy(c_hbm, c_raw, load_sem.at[2]),
    ]
    halves = 2 if n % 2 == 0 else 1
    for j in range(halves):
        at = pl.ds(j * (d // halves), d // halves)
        loads.append(pltpu.make_async_copy(t_hbm.at[at], target.at[at], load_sem.at[3 + j]))
    for load in loads:
        load.start()

    @pl.when(me > 0)
    def _():
        pl.semaphore_wait(barrier, 1)
        pl.semaphore_signal(entered, inc=1, device_id={"col": me - 1}, device_id_type=MESH)

    def place_of(way):
        return me if way == 0 else n - 1 - me

    def shard_at(way, place):
        return place if way == 0 else n - 1 - place

    def split(s):
        it = s // phase
        u = s - it * phase
        b = u // chunks
        return it, b, u - b * chunks

    def z_copy(way, s, src, dst):
        return pltpu.make_async_remote_copy(
            src_ref=src, dst_ref=dst, send_sem=z_send.at[way, s % LAG], recv_sem=z_recv.at[way, s % (2 * LAG)],
            device_id={"col": me + 1 - 2 * way}, device_id_type=MESH,
        )

    def rows_of(shard, c):
        return pl.ds(pl.multiple_of(shard * rows + c * ch, 16), ch)

    def chunk_of(c):
        return pl.ds(pl.multiple_of(c * ch, 16), ch)

    def gather_copy(way, s, shard):
        it, b, c = split(s)
        ref = full.at[it, rows_of(shard, c)]
        return z_copy(way, s, ref, ref)

    def scatter_copy(way, s, shard):
        it, b, c = split(s)
        return z_copy(way, s, part.at[shard, chunk_of(c)], landed.at[way, b - 1, chunk_of(c)])

    def on_send(way, s, act):
        it, b, c = split(s)
        p = place_of(way)

        @pl.when((p < n - 1) & (b <= p))
        def _():
            act(gather_copy(way, s, shard_at(way, p - b)))

        @pl.when((p < n - 1) & (b > p))
        def _():
            act(scatter_copy(way, s, shard_at(way, n + p - b)))

    def arrive(way, s):
        it, b, c = split(s)
        p = place_of(way)

        @pl.when((p > 0) & (b <= p - 1))
        def _():
            gather_copy(way, s, shard_at(way, p - 1 - b)).wait_recv()

        @pl.when((p > 0) & (b > p - 1))
        def _():
            shard = shard_at(way, n + p - 1 - b)
            scatter_copy(way, s, shard).wait_recv()
            at = chunk_of(c)
            part[shard, at, :] = part[shard, at, :] + landed[way, b - 1, at, :]

    def take(s):
        for way in range(2):
            on_send(way, s - LAG, lambda copy: copy.wait_send())
        for way in range(2):
            arrive(way, s - LAG)

    def give(s):
        for way in range(2):
            on_send(way, s, lambda copy: copy.start())

    def step(s):
        take(s)
        give(s)

    def give_first(way):
        @pl.when(place_of(way) < n - 1)
        def _():
            if way == 0:
                pl.semaphore_wait(entered, 1)
            for s in range(LAG):
                z_copy(way, s, f_hbm.at[chunk_of(s)], full.at[0, rows_of(me, s)]).start()

    def gram_copy(it, way):
        return pltpu.make_async_remote_copy(
            src_ref=gram_go.at[it, way], dst_ref=gram_in.at[it, way], send_sem=gram_send.at[it, way],
            recv_sem=gram_recv.at[it, way], device_id={"col": me + 1 - 2 * way}, device_id_type=MESH,
        )

    def gram_hop(it, s, start):
        for way in range(2):
            p = place_of(way)
            now = s == start + p * LAG

            @pl.when(now & (p > 0))
            def _():
                gram_copy(it, way).wait_recv()

            @pl.when(now & (p == 0) & (p < n - 1))
            def _():
                gram_go[it, way] = gram_packed[...]

            @pl.when(now & (p > 0) & (p < n - 1))
            def _():
                gram_go[it, way] = gram_packed[...] + gram_in[it, way]

            @pl.when(now & (p < n - 1))
            def _():
                gram_copy(it, way).start()

    def gram_close(it):
        for way in range(2):
            p = place_of(way)

            @pl.when(p > 0)
            def _():
                gram_packed[...] = gram_packed[...] + gram_in[it, way]

            @pl.when(p < n - 1)
            def _():
                gram_copy(it, way).wait_send()

        gram[...] = unpack_symmetric(gram_packed[...])

    def expert_copy(ref, kind, off):
        place = ref.at[mine]
        return pltpu.make_async_remote_copy(
            src_ref=place, dst_ref=place, send_sem=ex_send.at[kind, off - 1], recv_sem=ex_recv.at[kind, off - 1],
            device_id={"expert": lax.rem(mine + off, experts)}, device_id_type=MESH,
        )

    def expert_start(ref, kind):
        for off in range(1, experts):
            expert_copy(ref, kind, off).start()

    def expert_wait(ref, kind):
        for off in range(1, experts):
            expert_copy(ref, kind, off).wait()

    def pre_copy(it, q, e, i, target):
        place = d_pre.at[it, e] if it == 0 else d_pre.at[it, e, q]
        return pltpu.make_async_remote_copy(
            src_ref=place, dst_ref=place, send_sem=pre_send.at[it + q, i], recv_sem=pre_recv.at[it + q, i],
            device_id={"expert": target}, device_id_type=MESH,
        )

    def across(i):
        return lax.rem(mine + 2 * i, experts)

    def pre_start(it):
        for q in range(quarters if it else 1):
            for i in range(1, pairs):
                pre_copy(it, q, mine, i - 1, across(i)).start()
            pre_copy(it, q, mine, pairs - 1, mate).start()

    def pre_forward(it, q):
        for i in range(1, pairs):
            source = across(pairs - i)
            pre_copy(it, q, source, i - 1, mate).wait_recv()
            pre_copy(it, q, source, pairs - 1 + i, mate).start()

    def pre_wait(it, q):
        for i in range(1, pairs):
            pre_copy(it, q, mine, i - 1, across(i)).wait_send()
        pre_copy(it, q, mine, pairs - 1, mate).wait_send()
        pre_copy(it, q, mate, pairs - 1, mate).wait_recv()
        for i in range(1, pairs):
            pre_copy(it, q, across(pairs - i), pairs - 1 + i, mate).wait_send()
            pre_copy(it, q, lax.rem(mate + 2 * (pairs - i), experts), pairs - 1 + i, mate).wait_recv()

    def coef_copy(it, off):
        place = message.at[it, me]
        return pltpu.make_async_remote_copy(
            src_ref=place, dst_ref=place, send_sem=co_send.at[it, off - 1], recv_sem=co_recv.at[it, off - 1],
            device_id={"col": lax.rem(me + off, n)}, device_id_type=MESH,
        )

    def mix(c_ref):
        for q in range(0, hl, 128):
            def add(k, total):
                return total + c_ref[mine, pl.ds(k, 1), :] * bases[k, :, q : q + 128]

            value = jnp.tanh(lax.fori_loop(0, k_count, add, jnp.zeros((r, 128), F32), unroll=4))
            mixed[:, q : q + 128] = value
            upper, lower = pieces(value)
            for i in range(2):
                tall[2 * i * r : (2 * i + 1) * r, q : q + 128] = upper
                tall[(2 * i + 1) * r : (2 * i + 2) * r, q : q + 128] = lower

    def gram_local():
        cut = tall[: 2 * r, :]
        both = contract(cut, cut, ((1,), (1,)))
        both = both[:r] + both[r:]
        gram_packed[...] = pack_symmetric(both[:, :r] + both[:, r:])

    def project(j):
        def one(c, carry):
            value = contract(target[rows_of(j, c), :], tall[: 2 * r, :], ((1,), (1,)))
            part[j, chunk_of(c), :] = value[:, :r] + value[:, r:]
            return carry

        lax.fori_loop(0, chunks, one, 0)

    def absorb(it, shard, c):
        at = rows_of(shard, c)
        cut = jnp.concatenate(pieces(full[it, at, :]), axis=1)
        gram_sum[...] += contract(cut, jnp.concatenate([target[at, :], cut], axis=1), ((0,), (0,)))

    def loss_add(it, shard, c):
        at = rows_of(shard, c)
        one, two = pieces(full[it, at, :])
        wide = jnp.concatenate([one, one, two, two], axis=1)
        residual = contract(wide, tall[...], ((1,), (0,))) - target[at, :].astype(F32)
        loss_sum[...] += jnp.sum((residual * residual).reshape(ch // 8, 8, hl), axis=0)

    def arrived(way, s):
        it, b, c = split(s)
        p = place_of(way)
        return (p > 0) & (b <= p - 1), shard_at(way, p - 1 - b), c

    def for_arrived(act, it, s, own):
        first, first_shard, c = arrived(0, s)
        second, second_shard, _ = arrived(1, s)

        def one(i, carry):
            valid = jnp.where(i == 0, first, jnp.where(i == 1, second, own))
            shard = jnp.where(i == 0, first_shard, jnp.where(i == 1, second_shard, me))

            @pl.when(valid)
            def _():
                act(it, shard, c)

            return carry

        lax.fori_loop(0, 3, one, 0)

    def pre_gradient(it):
        total = gram_sum[:r, :] + gram_sum[r:, :]
        square = total[:, hl : hl + r] + total[:, hl + r :]
        now = mixed[...]
        d_mixed = jnp.dot(square, now, precision=HIGHEST, preferred_element_type=F32) - total[:, :hl]
        value = d_mixed * scale * (1.0 - now * now)
        for q in range(quarters):
            d_pre[it, mine, q] = value[:, q * 128 : (q + 1) * 128]

    def loss_close(it):
        total = loss_sum[:, 0:128]
        for q in range(128, hl, 128):
            total = total + loss_sum[:, q : q + 128]
        loss_in[mine, it * 8 : it * 8 + 8, :] = total
        loss_sum[...] = jnp.zeros_like(loss_sum)

    def combine(c_ref, it, k, q):
        total = c_ref[0, pl.ds(k, 1), :] * d_pre[it, 0, q]
        for e in range(1, experts):
            total = total + c_ref[e, pl.ds(k, 1), :] * d_pre[it, e, q]
        return total

    def columns(q):
        return slice(q * 128, (q + 1) * 128)

    def coef_pass(it, which):
        def one(k, carry):
            sums = [jnp.zeros((8, 128), F32)] * experts
            for q in which:
                values = bases[k, :, columns(q)]
                for e in range(experts):
                    held = values * d_pre[it, e, q]
                    sums[e] = sums[e] + jnp.sum(held.reshape(r // 8, 8, 128), axis=0)
            for e in range(experts):
                at = pl.ds(e * k_count + k, 1)
                value = jnp.sum(sums[e], axis=0, keepdims=True)
                coef_acc[at, :] = value if 0 in which else coef_acc[at, :] + value
            return carry

        lax.fori_loop(0, k_count, one, 0)

    def coef_send(it, losses=None):
        message[it, me] = jnp.zeros(message.shape[2:], F32)
        for i in range(blocks):
            column = jnp.sum(coef_acc[i * block : (i + 1) * block, :], axis=1, keepdims=True)
            message[it, me, i : i + 1, :] = to_lanes(jnp.broadcast_to(column, (block, 128)))
        if losses is not None:
            message[it, me, blocks : blocks + 1, :] = to_lanes(
                jnp.concatenate([lane_sums(losses[:8]), lane_sums(losses[8:])], axis=0)
            )
        for off in range(1, n):
            coef_copy(it, off).start()

    def coef_wait(it):
        for off in range(1, n):
            coef_copy(it, off).wait()

    def message_sum(it):
        total = message[it, 0]
        for c in range(1, n):
            total = total + message[it, c]
        return total

    def coef_table(total):
        held = [to_rows(total[i : i + 1, :], block) for i in range(blocks)]
        held = held[0] if blocks == 1 else jnp.concatenate(held, axis=0)
        return held.reshape(experts, k_count, 128)

    def bases_one(low, high):
        def one(k, carry):
            for q in range(quarters):
                gradient = combine(c_one, 0, k, q)
                b_grad[k, :, columns(q)] = ROOT_ONE * gradient
                bases[k, :, columns(q)] = adam_first(bases[k, :, columns(q)], gradient)
            return carry

        lax.fori_loop(low, high, one, 0)

    def bases_two(q):
        def one(k, carry):
            values = bases[k, :, columns(q)]
            bases[k, :, columns(q)] = adam_second(values, b_grad[k, :, columns(q)], combine(c_root, 1, k, q))
            return carry

        lax.fori_loop(0, k_count, one, 0, unroll=2)

    def factor_product(it, c):
        return jnp.dot(
            full[it, rows_of(me, c), :], gram[...], precision=HIGHEST, preferred_element_type=F32
        )

    def factor_one(c):
        at = chunk_of(c)
        g = (factor_product(0, c) - part[me, at, :]) * scale
        g_one[at, :] = ROOT_ONE * g
        full[1, rows_of(me, c), :] = adam_first(full[0, rows_of(me, c), :], g)

    def factor_two(c):
        at = chunk_of(c)
        g = (full[0, rows_of(me, c), :] - part[me, at, :]) * (ROOT_TWO * scale)
        f_out[at, :] = adam_second(full[1, rows_of(me, c), :], g_one[at, :], g)

    scope = jax.named_scope
    with scope("enter"):
        give_first(1)
        give_first(0)
    misc[...] = jnp.zeros_like(misc)
    loads[2].wait()
    misc[0:1, :k_count] = c_raw[...]
    c_one[mine] = to_rows(misc[0:1, :], k_count)
    gram_sum[...] = jnp.zeros_like(gram_sum)
    loss_sum[...] = jnp.zeros_like(loss_sum)
    with scope("load"):
        loads[1].wait()
    with scope("mix"):
        mix(c_one)
        gram_local()
    with scope("project"):
        for j in range(n):
            if j % (n // halves) == 0:
                loads[3 + j // (n // halves)].wait()
            project(j)

    with scope("greet"):
        @pl.when(me == 0)
        def _():
            pl.semaphore_wait(barrier, experts - 1)

        @pl.when(me > 0)
        def _():
            pl.semaphore_wait(known, 1)

        @pl.when(me < n - 1)
        def _():
            greet_experts(above)
            pl.semaphore_wait(above, experts - 1)
            pl.semaphore_signal(known, inc=1, device_id={"col": me + 1}, device_id_type=MESH)

    expert_start(c_one, 0)
    loads[0].wait()
    final = phase - chunks + LAG

    def early(s, carry):
        gram_hop(0, s, LAG)
        with scope("step"):
            step(s)
        own = s - LAG < chunks
        for_arrived(absorb, 0, s - LAG, own)
        for_arrived(loss_add, 0, s - LAG, own)
        return carry

    lax.fori_loop(LAG, final, early, 0)
    with scope("pre"):
        pre_gradient(0)
        expert_wait(c_one, 0)
        pre_start(0)
        gram_close(0)
        loss_close(0)
        gram_sum[...] = jnp.zeros_like(gram_sum)

    def base_work(i):
        if i == 0:
            with scope("forward"):
                pre_forward(0, 0)
        elif i == 1:
            with scope("wait"):
                pre_wait(0, 0)
            with scope("coef"):
                coef_pass(0, range(quarters))
                coef_send(0)
        elif i == 2:
            with scope("bases"):
                bases_one(0, k_count // 2)
        else:
            with scope("bases"):
                bases_one(k_count // 2, k_count)

    for c in range(chunks):
        with scope("step"):
            step(final + c)
        factor_one(c)
        absorb(1, me, c)
        base_work(c)

    begin = phase + chunks
    behind = begin - phase - LAG
    for s in range(final + chunks, begin):
        with scope("step"):
            step(s)
        for_arrived(absorb, 1, s - LAG, False)
    with scope("await"):
        coef_wait(0)
    c_grad[...] = coef_table(message_sum(0))
    c_two[...] = adam_first(c_one[...], c_grad[...])
    c_root[...] = ROOT_TWO * c_two[...]
    with scope("mix"):
        mix(c_two)
        gram_local()
    with scope("project"):
        for j in range(n):
            project(j)

    def late(s, carry):
        gram_hop(1, s, begin)
        with scope("step"):
            step(s)
        for_arrived(absorb, 1, s - LAG, False)
        for_arrived(loss_add, 1, s - LAG - behind, False)

        @pl.when(s - begin < chunks)
        def _():
            loss_add(1, me, s - begin)

        return carry

    end = phase + final
    lax.fori_loop(begin, end, late, 0)
    with scope("pre"):
        pre_gradient(1)
        pre_start(1)
        gram_close(1)
    with scope("product"):
        for c in range(chunks):
            full[0, rows_of(me, c), :] = factor_product(1, c)
    for s in range(end - LAG - behind, end - LAG):
        for_arrived(loss_add, 1, s, False)
    loss_close(1)
    expert_start(loss_in, 1)
    with scope("forward"):
        pre_forward(1, 0)
    with scope("step"):
        take(end)
    factor_two(0)
    with scope("wait"):
        pre_wait(1, 0)
    with scope("coef"):
        coef_pass(1, (0,))
    with scope("forward"):
        for q in range(1, quarters):
            pre_forward(1, q)
    with scope("bases"):
        bases_two(0)
    with scope("wait"):
        for q in range(1, quarters):
            pre_wait(1, q)
    with scope("coef"):
        if quarters > 1:
            coef_pass(1, range(1, quarters))
        expert_wait(loss_in, 1)
        losses = loss_in[0]
        for e in range(1, experts):
            losses = losses + loss_in[e]
        coef_send(1, losses)
    give(end)
    for q in range(1, quarters):
        with scope("bases"):
            bases_two(q)
        if q < chunks - 1:
            with scope("step"):
                take(end + q)
            factor_two(q)
    for c in range(max(quarters, 1), chunks - 1):
        take(end + c)
        factor_two(c)
    with scope("await"):
        coef_wait(1)
    with scope("coefs"):
        total = message_sum(1)
        own = pl.ds(mine * k_count, k_count)
        coef_acc[...] = coef_table(total).reshape(table, 128)
        misc[0:1, :] = to_lanes(adam_second(c_two[mine], ROOT_ONE * c_grad[mine], ROOT_TWO * coef_acc[own, :]))
        misc[1:2, :] = total[blocks : blocks + 1, :] * loss_scale
    with scope("step"):
        take(end + chunks - 1)
    with scope("factor"):
        factor_two(chunks - 1)


def hand_over(b_in, f_in, misc, b_out, f_out, c_out, l_out, c_held, l_held, sem):
    copies = [
        pltpu.make_async_copy(f_in, f_out, sem.at[0]),
        pltpu.make_async_copy(b_in, b_out, sem.at[1]),
        pltpu.make_async_copy(c_held, c_out, sem.at[2]),
        pltpu.make_async_copy(l_held, l_out, sem.at[3]),
    ]
    for copy in copies[:2]:
        copy.start()
    c_held[...] = misc[0:1, : c_out.shape[1]]
    for i in range(2):
        l_held[i] = misc[1, 8 * i]
    for copy in copies[2:]:
        copy.start()
    for copy in copies:
        copy.wait()


def shards(target_weights, factors, bases, coefficients):
    n, experts = lax.axis_size("col"), lax.axis_size("expert")
    _, d, hl = target_weights.shape
    _, rows, r = factors.shape
    k = bases.shape[0]
    held = pl.BlockSpec(memory_space=pltpu.HBM)
    local = pl.BlockSpec(memory_space=pltpu.VMEM)
    dma = pltpu.SemaphoreType.DMA
    loss_scale = 1.0 / (2.0 * experts * d * hl * n)
    new_factors, new_bases, misc = pl.pallas_call(
        functools.partial(kernel, n, experts, loss_scale),
        out_shape=(
            pltpu.VMEM((rows, r), F32),
            pltpu.VMEM(bases.shape, F32),
            pltpu.VMEM((8, 128), F32),
        ),
        in_specs=[held, held, held, held],
        out_specs=(local, local, local),
        scratch_shapes=[
            pltpu.VMEM((d, hl), BF16),
            pltpu.VMEM(bases.shape, F32),
            pltpu.VMEM((2, d, r), F32),
            pltpu.VMEM((n, rows, r), F32),
            pltpu.VMEM((2, n - 1, rows, r), F32),
            pltpu.VMEM((2, experts, hl // 128, r, 128), F32),
            pltpu.VMEM((experts, k, 128), F32),
            pltpu.VMEM((experts, k, 128), F32),
            pltpu.VMEM((experts, k, 128), F32),
            pltpu.VMEM((experts, k, 128), F32),
            pltpu.VMEM((experts * k, 128), F32),
            pltpu.VMEM((2, n, experts * k // min(experts * k, 128) + 1, 128), F32),
            pltpu.VMEM((experts, 16, 128), F32),
            pltpu.VMEM((rows, r), F32),
            pltpu.VMEM((2 * r, hl + 2 * r), F32),
            pltpu.VMEM((r, hl), F32),
            pltpu.VMEM((4 * r, hl), BF16),
            pltpu.VMEM((8, hl), F32),
            pltpu.VMEM((r, r), F32),
            pltpu.VMEM((r // 2 + 8, r), F32),
            pltpu.VMEM((2, 2, r // 2 + 8, r), F32),
            pltpu.VMEM((2, 2, r // 2 + 8, r), F32),
            pltpu.VMEM((1, k), F32),
            pltpu.SemaphoreType.REGULAR,
            pltpu.SemaphoreType.REGULAR,
            pltpu.SemaphoreType.REGULAR,
            dma((5,)),
            dma((2, LAG)),
            dma((2, 2 * LAG)),
            dma((2, 2)),
            dma((2, 2)),
            dma((2, experts - 1)),
            dma((2, experts - 1)),
            dma((1 + hl // 128, experts - 1)),
            dma((1 + hl // 128, experts - 1)),
            dma((2, n - 1)),
            dma((2, n - 1)),
        ],
        compiler_params=pltpu.CompilerParams(
            collective_id=0, has_side_effects=True, vmem_limit_bytes=VMEM_MAIN
        ),
    )(target_weights[0], factors[0], bases, coefficients)
    new_bases, new_factors, new_coef, losses = pl.pallas_call(
        hand_over,
        out_shape=(
            jax.ShapeDtypeStruct(bases.shape, F32),
            jax.ShapeDtypeStruct((rows, r), F32),
            jax.ShapeDtypeStruct((1, k), F32),
            jax.ShapeDtypeStruct((2,), F32),
        ),
        in_specs=[local, local, local],
        out_specs=(held, held, held, held),
        scratch_shapes=[pltpu.VMEM((1, k), F32), pltpu.SMEM((2,), F32), dma((4,))],
        compiler_params=pltpu.CompilerParams(vmem_limit_bytes=VMEM_LAST),
    )(new_bases, new_factors, misc)
    return (new_factors[None], new_bases, new_coef, losses)


def solution(mesh):
    return jax.shard_map(
        shards,
        mesh=mesh,
        in_specs=(
            P(("layer", "expert"), None, "col"),
            P(("layer", "expert"), "col", None),
            P("layer", None, "col"),
            P(("layer", "expert"), None),
        ),
        out_specs=(
            P(("layer", "expert"), "col", None),
            P("layer", None, "col"),
            P(("layer", "expert"), None),
            P("layer"),
        ),
        check_vma=False,
    )
```

```python
import functools

import jax
import jax.numpy as jnp
from jax import lax
from jax.experimental import pallas as pl
from jax.experimental.pallas import tpu as pltpu
from jax.sharding import PartitionSpec as P

LEARN_RATE = 0.01
BETA_ONE = 0.9
BETA_TWO = 0.999
EPSILON = 0.0001
HIGHEST = lax.Precision.HIGHEST
MESH = pl.DeviceIdType.MESH
F32 = jnp.float32
BF16 = jnp.bfloat16
CHUNKS = 4
LAG = 3
VMEM_MAIN = 57000000
VMEM_LAST = 4000000


def adam_first(parameter, g):
    return parameter - LEARN_RATE * g / (jnp.abs(g) + EPSILON)


ROOT_ONE = (BETA_TWO * (1.0 - BETA_TWO) / (1.0 - BETA_TWO**2)) ** 0.5
ROOT_TWO = ((1.0 - BETA_TWO) / (1.0 - BETA_TWO**2)) ** 0.5
RATE_ONE = LEARN_RATE * BETA_ONE * (1.0 - BETA_ONE) / (1.0 - BETA_ONE**2) / ROOT_ONE
RATE_TWO = LEARN_RATE * (1.0 - BETA_ONE) / (1.0 - BETA_ONE**2) / ROOT_TWO


def adam_second(parameter, h_one, h_two):
    second = h_one * h_one + h_two * h_two
    root = second * lax.rsqrt(jnp.maximum(second, 1e-30))
    return parameter - (RATE_ONE * h_one + RATE_TWO * h_two) / (root + EPSILON)


def pieces(x):
    upper = x.astype(BF16)
    return upper, (x - upper.astype(F32)).astype(BF16)


def contract(a, b, dims):
    return lax.dot_general(a, b, (dims, ((), ())), preferred_element_type=F32)


def diagonal(size):
    shape = (size, 128)
    return lax.broadcasted_iota(jnp.int32, shape, 0) == lax.broadcasted_iota(jnp.int32, shape, 1)


def to_lanes(column):
    return jnp.sum(jnp.where(diagonal(column.shape[0]), column, 0.0), axis=0, keepdims=True)


def places(shape):
    return lax.broadcasted_iota(jnp.int32, shape, 0), lax.broadcasted_iota(jnp.int32, shape, 1)


def pack_symmetric(g):
    half = g.shape[0] // 2
    row, lane = places((half, 2 * half))
    turned = pltpu.roll(g[half:], half, 1)
    top = jnp.where((lane > row) & (lane < half), turned, g[:half])
    diagonal_row = jnp.sum(jnp.where(lane == row, turned, 0.0), axis=0, keepdims=True)
    return jnp.concatenate([top, jnp.broadcast_to(diagonal_row, (8, 2 * half))], axis=0)


def unpack_symmetric(p):
    half = p.shape[1] // 2
    row, lane = places((half, 2 * half))
    top, diagonal_row = p[:half], jnp.broadcast_to(p[half : half + 1], (half, 2 * half))
    flipped = jnp.transpose(jnp.concatenate([top, top], axis=0))
    upper = jnp.where((lane > row) & (lane < half), flipped[:half], top)
    last = jnp.where(lane > row, top, jnp.where(lane < row, flipped[:half], diagonal_row))
    lower = jnp.where(lane < half, flipped[half:], pltpu.roll(last, half, 1))
    return jnp.concatenate([upper, lower], axis=0)


def lane_sums(x):
    total = jnp.sum(x, axis=(0, 1), keepdims=True)
    return jnp.where(lax.broadcasted_iota(jnp.int32, x.shape, 0) == 0, jnp.broadcast_to(total, x.shape), 0.0)


def to_rows(row, size):
    held = jnp.where(diagonal(size), jnp.broadcast_to(row, (size, 128)), 0.0)
    return jnp.broadcast_to(jnp.sum(held, axis=1, keepdims=True), (size, 128))


def kernel(
    n, experts, loss_scale, t_hbm, f_hbm, b_hbm, c_hbm, f_out, bases, misc,
    target, b_grad, full, part, landed, d_pre, c_one, c_two, c_root, c_grad, coef_acc, message, loss_in, g_one, gram_sum,
    mixed, tall, loss_sum, gram, gram_packed, gram_in, gram_go, c_raw,
    entered, above, known, load_sem, z_send, z_recv, gram_send, gram_recv, ex_send, ex_recv, pre_send, pre_recv, co_send, co_recv,
):
    me = lax.axis_index("col")
    mine = lax.axis_index("expert")
    rows, r = f_hbm.shape
    d, hl = target.shape
    k_count = bases.shape[0]
    scale = 1.0 / (hl * n)
    table = experts * k_count
    block = min(table, 128)
    blocks = table // block
    chunks = CHUNKS
    ch = rows // chunks
    phase = n * chunks
    quarters = hl // 128
    pairs = experts // 2
    mate = mine + 1 - 2 * lax.rem(mine, 2)

    barrier = pltpu.get_barrier_semaphore()

    @pl.when(me < n - 1)
    def _():
        pl.semaphore_signal(barrier, inc=1, device_id={"col": me + 1}, device_id_type=MESH)

    def greet_experts(semaphore):
        for off in range(1, experts):
            pl.semaphore_signal(
                semaphore, inc=1, device_id={"expert": lax.rem(mine + off, experts)}, device_id_type=MESH
            )

    @pl.when(me == 0)
    def _():
        greet_experts(barrier)

    loads = [
        pltpu.make_async_copy(f_hbm, full.at[0, pl.ds(pl.multiple_of(me * rows, 16), rows)], load_sem.at[0]),
        pltpu.make_async_copy(b_hbm, bases, load_sem.at[1]),
        pltpu.make_async_copy(c_hbm, c_raw, load_sem.at[2]),
    ]
    halves = 2 if n % 2 == 0 else 1
    for j in range(halves):
        at = pl.ds(j * (d // halves), d // halves)
        loads.append(pltpu.make_async_copy(t_hbm.at[at], target.at[at], load_sem.at[3 + j]))
    for load in loads:
        load.start()

    @pl.when(me > 0)
    def _():
        pl.semaphore_wait(barrier, 1)
        pl.semaphore_signal(entered, inc=1, device_id={"col": me - 1}, device_id_type=MESH)

    def place_of(way):
        return me if way == 0 else n - 1 - me

    def shard_at(way, place):
        return place if way == 0 else n - 1 - place

    def split(s):
        it = s // phase
        u = s - it * phase
        b = u // chunks
        return it, b, u - b * chunks

    def z_copy(way, s, src, dst):
        return pltpu.make_async_remote_copy(
            src_ref=src, dst_ref=dst, send_sem=z_send.at[way, s % LAG], recv_sem=z_recv.at[way, s % (2 * LAG)],
            device_id={"col": me + 1 - 2 * way}, device_id_type=MESH,
        )

    def rows_of(shard, c):
        return pl.ds(pl.multiple_of(shard * rows + c * ch, 16), ch)

    def chunk_of(c):
        return pl.ds(pl.multiple_of(c * ch, 16), ch)

    def gather_copy(way, s, shard):
        it, b, c = split(s)
        ref = full.at[it, rows_of(shard, c)]
        return z_copy(way, s, ref, ref)

    def scatter_copy(way, s, shard):
        it, b, c = split(s)
        return z_copy(way, s, part.at[shard, chunk_of(c)], landed.at[way, b - 1, chunk_of(c)])

    def on_send(way, s, act):
        it, b, c = split(s)
        p = place_of(way)

        @pl.when((p < n - 1) & (b <= p))
        def _():
            act(gather_copy(way, s, shard_at(way, p - b)))

        @pl.when((p < n - 1) & (b > p))
        def _():
            act(scatter_copy(way, s, shard_at(way, n + p - b)))

    def arrive(way, s):
        it, b, c = split(s)
        p = place_of(way)

        @pl.when((p > 0) & (b <= p - 1))
        def _():
            gather_copy(way, s, shard_at(way, p - 1 - b)).wait_recv()

        @pl.when((p > 0) & (b > p - 1))
        def _():
            shard = shard_at(way, n + p - 1 - b)
            scatter_copy(way, s, shard).wait_recv()
            at = chunk_of(c)
            part[shard, at, :] = part[shard, at, :] + landed[way, b - 1, at, :]

    def take(s):
        for way in range(2):
            on_send(way, s - LAG, lambda copy: copy.wait_send())
        for way in range(2):
            arrive(way, s - LAG)

    def give(s):
        for way in range(2):
            on_send(way, s, lambda copy: copy.start())

    def step(s):
        take(s)
        give(s)

    def give_first(way):
        @pl.when(place_of(way) < n - 1)
        def _():
            if way == 0:
                pl.semaphore_wait(entered, 1)
            for s in range(LAG):
                z_copy(way, s, f_hbm.at[chunk_of(s)], full.at[0, rows_of(me, s)]).start()

    def gram_copy(it, way):
        return pltpu.make_async_remote_copy(
            src_ref=gram_go.at[it, way], dst_ref=gram_in.at[it, way], send_sem=gram_send.at[way],
            recv_sem=gram_recv.at[way], device_id={"col": me + 1 - 2 * way}, device_id_type=MESH,
        )

    def gram_hop(it, s, start):
        for way in range(2):
            p = place_of(way)
            now = s == start + p * LAG

            @pl.when(now & (p > 0))
            def _():
                gram_copy(it, way).wait_recv()

            @pl.when(now & (p == 0) & (p < n - 1))
            def _():
                gram_go[it, way] = gram_packed[...]

            @pl.when(now & (p > 0) & (p < n - 1))
            def _():
                gram_go[it, way] = gram_packed[...] + gram_in[it, way]

            @pl.when(now & (p < n - 1))
            def _():
                gram_copy(it, way).start()

    def gram_close(it):
        for way in range(2):
            p = place_of(way)

            @pl.when(p > 0)
            def _():
                gram_packed[...] = gram_packed[...] + gram_in[it, way]

            @pl.when(p < n - 1)
            def _():
                gram_copy(it, way).wait_send()

        gram[...] = unpack_symmetric(gram_packed[...])

    def expert_copy(ref, off):
        place = ref.at[mine]
        return pltpu.make_async_remote_copy(
            src_ref=place, dst_ref=place, send_sem=ex_send.at[off - 1], recv_sem=ex_recv.at[off - 1],
            device_id={"expert": lax.rem(mine + off, experts)}, device_id_type=MESH,
        )

    def expert_start(ref):
        for off in range(1, experts):
            expert_copy(ref, off).start()

    def expert_wait(ref):
        for off in range(1, experts):
            expert_copy(ref, off).wait()

    def pre_copy(it, q, e, i, target):
        place = d_pre.at[it, e] if it == 0 else d_pre.at[it, e, q]
        return pltpu.make_async_remote_copy(
            src_ref=place, dst_ref=place, send_sem=pre_send.at[it + q, i], recv_sem=pre_recv.at[it + q, i],
            device_id={"expert": target}, device_id_type=MESH,
        )

    def across(i):
        return lax.rem(mine + 2 * i, experts)

    def pre_start(it):
        for q in range(quarters if it else 1):
            for i in range(1, pairs):
                pre_copy(it, q, mine, i - 1, across(i)).start()
            pre_copy(it, q, mine, pairs - 1, mate).start()

    def pre_forward(it, q):
        for i in range(1, pairs):
            source = across(pairs - i)
            pre_copy(it, q, source, i - 1, mate).wait_recv()
            pre_copy(it, q, source, pairs - 1 + i, mate).start()

    def pre_wait(it, q):
        for i in range(1, pairs):
            pre_copy(it, q, mine, i - 1, across(i)).wait_send()
        pre_copy(it, q, mine, pairs - 1, mate).wait_send()
        pre_copy(it, q, mate, pairs - 1, mate).wait_recv()
        for i in range(1, pairs):
            pre_copy(it, q, across(pairs - i), pairs - 1 + i, mate).wait_send()
            pre_copy(it, q, lax.rem(mate + 2 * (pairs - i), experts), pairs - 1 + i, mate).wait_recv()

    def coef_copy(it, off):
        place = message.at[it, me]
        return pltpu.make_async_remote_copy(
            src_ref=place, dst_ref=place, send_sem=co_send.at[off - 1], recv_sem=co_recv.at[off - 1],
            device_id={"col": lax.rem(me + off, n)}, device_id_type=MESH,
        )

    def mix(c_ref):
        for q in range(0, hl, 128):
            def add(k, total):
                return total + c_ref[mine, pl.ds(k, 1), :] * bases[k, :, q : q + 128]

            value = jnp.tanh(lax.fori_loop(0, k_count, add, jnp.zeros((r, 128), F32), unroll=4))
            mixed[:, q : q + 128] = value
            upper, lower = pieces(value)
            for i in range(2):
                tall[2 * i * r : (2 * i + 1) * r, q : q + 128] = upper
                tall[(2 * i + 1) * r : (2 * i + 2) * r, q : q + 128] = lower

    def gram_local():
        cut = tall[: 2 * r, :]
        both = contract(cut, cut, ((1,), (1,)))
        both = both[:r] + both[r:]
        gram_packed[...] = pack_symmetric(both[:, :r] + both[:, r:])

    def project(j):
        def one(c, carry):
            value = contract(target[rows_of(j, c), :], tall[: 2 * r, :], ((1,), (1,)))
            part[j, chunk_of(c), :] = value[:, :r] + value[:, r:]
            return carry

        lax.fori_loop(0, chunks, one, 0)

    def absorb(it, shard, c):
        at = rows_of(shard, c)
        cut = jnp.concatenate(pieces(full[it, at, :]), axis=1)
        gram_sum[...] += contract(cut, jnp.concatenate([target[at, :], cut], axis=1), ((0,), (0,)))

    def loss_add(it, shard, c):
        at = rows_of(shard, c)
        one, two = pieces(full[it, at, :])
        wide = jnp.concatenate([one, one, two, two], axis=1)
        residual = contract(wide, tall[...], ((1,), (0,))) - target[at, :].astype(F32)
        loss_sum[...] += jnp.sum((residual * residual).reshape(ch // 8, 8, hl), axis=0)

    def arrived(way, s):
        it, b, c = split(s)
        p = place_of(way)
        return (p > 0) & (b <= p - 1), shard_at(way, p - 1 - b), c

    def for_arrived(act, it, s, own):
        first, first_shard, c = arrived(0, s)
        second, second_shard, _ = arrived(1, s)

        def one(i, carry):
            valid = jnp.where(i == 0, first, jnp.where(i == 1, second, own))
            shard = jnp.where(i == 0, first_shard, jnp.where(i == 1, second_shard, me))

            @pl.when(valid)
            def _():
                act(it, shard, c)

            return carry

        lax.fori_loop(0, 3, one, 0)

    def pre_gradient(it):
        total = gram_sum[:r, :] + gram_sum[r:, :]
        square = total[:, hl : hl + r] + total[:, hl + r :]
        now = mixed[...]
        d_mixed = jnp.dot(square, now, precision=HIGHEST, preferred_element_type=F32) - total[:, :hl]
        value = d_mixed * scale * (1.0 - now * now)
        for q in range(quarters):
            d_pre[it, mine, q] = value[:, q * 128 : (q + 1) * 128]

    def loss_close(it):
        total = loss_sum[:, 0:128]
        for q in range(128, hl, 128):
            total = total + loss_sum[:, q : q + 128]
        loss_in[mine, it * 8 : it * 8 + 8, :] = total
        loss_sum[...] = jnp.zeros_like(loss_sum)

    def combine(c_ref, it, k, q):
        total = c_ref[0, pl.ds(k, 1), :] * d_pre[it, 0, q]
        for e in range(1, experts):
            total = total + c_ref[e, pl.ds(k, 1), :] * d_pre[it, e, q]
        return total

    def columns(q):
        return slice(q * 128, (q + 1) * 128)

    def coef_pass(it, which):
        def one(k, carry):
            sums = [jnp.zeros((8, 128), F32)] * experts
            for q in which:
                values = bases[k, :, columns(q)]
                for e in range(experts):
                    held = values * d_pre[it, e, q]
                    sums[e] = sums[e] + jnp.sum(held.reshape(r // 8, 8, 128), axis=0)
            for e in range(experts):
                at = pl.ds(e * k_count + k, 1)
                value = jnp.sum(sums[e], axis=0, keepdims=True)
                coef_acc[at, :] = value if 0 in which else coef_acc[at, :] + value
            return carry

        lax.fori_loop(0, k_count, one, 0)

    def coef_send(it, losses=None):
        message[it, me] = jnp.zeros(message.shape[2:], F32)
        for i in range(blocks):
            column = jnp.sum(coef_acc[i * block : (i + 1) * block, :], axis=1, keepdims=True)
            message[it, me, i : i + 1, :] = to_lanes(jnp.broadcast_to(column, (block, 128)))
        if losses is not None:
            message[it, me, blocks : blocks + 1, :] = to_lanes(
                jnp.concatenate([lane_sums(losses[:8]), lane_sums(losses[8:])], axis=0)
            )
        for off in range(1, n):
            coef_copy(it, off).start()

    def coef_wait(it):
        for off in range(1, n):
            coef_copy(it, off).wait()

    def message_sum(it):
        total = message[it, 0]
        for c in range(1, n):
            total = total + message[it, c]
        return total

    def coef_table(total):
        held = [to_rows(total[i : i + 1, :], block) for i in range(blocks)]
        held = held[0] if blocks == 1 else jnp.concatenate(held, axis=0)
        return held.reshape(experts, k_count, 128)

    def bases_one(low, high):
        def one(k, carry):
            for q in range(quarters):
                gradient = combine(c_one, 0, k, q)
                b_grad[k, :, columns(q)] = ROOT_ONE * gradient
                bases[k, :, columns(q)] = adam_first(bases[k, :, columns(q)], gradient)
            return carry

        lax.fori_loop(low, high, one, 0)

    def bases_two(q):
        def one(k, carry):
            values = bases[k, :, columns(q)]
            bases[k, :, columns(q)] = adam_second(values, b_grad[k, :, columns(q)], combine(c_root, 1, k, q))
            return carry

        lax.fori_loop(0, k_count, one, 0, unroll=2)

    def factor_product(it, c):
        return jnp.dot(
            full[it, rows_of(me, c), :], gram[...], precision=HIGHEST, preferred_element_type=F32
        )

    def factor_one(c):
        at = chunk_of(c)
        g = (factor_product(0, c) - part[me, at, :]) * scale
        g_one[at, :] = ROOT_ONE * g
        full[1, rows_of(me, c), :] = adam_first(full[0, rows_of(me, c), :], g)

    def factor_two(c):
        at = chunk_of(c)
        g = (full[0, rows_of(me, c), :] - part[me, at, :]) * (ROOT_TWO * scale)
        f_out[at, :] = adam_second(full[1, rows_of(me, c), :], g_one[at, :], g)

    scope = jax.named_scope
    with scope("enter"):
        give_first(1)
        give_first(0)
    misc[...] = jnp.zeros_like(misc)
    loads[2].wait()
    misc[0:1, :k_count] = c_raw[...]
    c_one[mine] = to_rows(misc[0:1, :], k_count)
    gram_sum[...] = jnp.zeros_like(gram_sum)
    loss_sum[...] = jnp.zeros_like(loss_sum)
    with scope("load"):
        loads[1].wait()
    with scope("mix"):
        mix(c_one)
        gram_local()
    with scope("project"):
        for j in range(n):
            if j % (n // halves) == 0:
                loads[3 + j // (n // halves)].wait()
            project(j)

    with scope("greet"):
        @pl.when(me == 0)
        def _():
            pl.semaphore_wait(barrier, experts - 1)

        @pl.when(me > 0)
        def _():
            pl.semaphore_wait(known, 1)

        @pl.when(me < n - 1)
        def _():
            greet_experts(above)
            pl.semaphore_wait(above, experts - 1)
            pl.semaphore_signal(known, inc=1, device_id={"col": me + 1}, device_id_type=MESH)

    expert_start(c_one)
    loads[0].wait()
    final = phase - chunks + LAG

    def early(s, carry):
        gram_hop(0, s, LAG)
        with scope("step"):
            step(s)
        own = s - LAG < chunks
        for_arrived(absorb, 0, s - LAG, own)
        for_arrived(loss_add, 0, s - LAG, own)
        return carry

    lax.fori_loop(LAG, final, early, 0)
    with scope("pre"):
        pre_gradient(0)
        expert_wait(c_one)
        pre_start(0)
        gram_close(0)
        loss_close(0)
        gram_sum[...] = jnp.zeros_like(gram_sum)

    def base_work(i):
        if i == 0:
            with scope("forward"):
                pre_forward(0, 0)
        elif i == 1:
            with scope("wait"):
                pre_wait(0, 0)
            with scope("coef"):
                coef_pass(0, range(quarters))
                coef_send(0)
        elif i == 2:
            with scope("bases"):
                bases_one(0, k_count // 2)
        else:
            with scope("bases"):
                bases_one(k_count // 2, k_count)

    for c in range(chunks):
        with scope("step"):
            step(final + c)
        factor_one(c)
        absorb(1, me, c)
        base_work(c)

    begin = phase + chunks
    behind = begin - phase - LAG
    for s in range(final + chunks, begin):
        with scope("step"):
            step(s)
        for_arrived(absorb, 1, s - LAG, False)
    with scope("await"):
        coef_wait(0)
    c_grad[...] = coef_table(message_sum(0))
    c_two[...] = adam_first(c_one[...], c_grad[...])
    c_root[...] = ROOT_TWO * c_two[...]
    with scope("mix"):
        mix(c_two)
        gram_local()
    with scope("project"):
        for j in range(n):
            project(j)

    def late(s, carry):
        gram_hop(1, s, begin)
        with scope("step"):
            step(s)
        for_arrived(absorb, 1, s - LAG, False)
        for_arrived(loss_add, 1, s - LAG - behind, False)

        @pl.when(s - begin < chunks)
        def _():
            loss_add(1, me, s - begin)

        return carry

    end = phase + final
    lax.fori_loop(begin, end, late, 0)
    with scope("pre"):
        pre_gradient(1)
        pre_start(1)
        gram_close(1)
    with scope("product"):
        for c in range(chunks):
            full[0, rows_of(me, c), :] = factor_product(1, c)
    for s in range(end - LAG - behind, end - LAG):
        for_arrived(loss_add, 1, s, False)
    loss_close(1)
    expert_start(loss_in)
    with scope("forward"):
        pre_forward(1, 0)
    with scope("step"):
        take(end)
    factor_two(0)
    with scope("wait"):
        pre_wait(1, 0)
    with scope("coef"):
        coef_pass(1, (0,))
    with scope("forward"):
        for q in range(1, quarters):
            pre_forward(1, q)
    with scope("bases"):
        bases_two(0)
    with scope("wait"):
        for q in range(1, quarters):
            pre_wait(1, q)
    with scope("coef"):
        if quarters > 1:
            coef_pass(1, range(1, quarters))
        expert_wait(loss_in)
        losses = loss_in[0]
        for e in range(1, experts):
            losses = losses + loss_in[e]
        coef_send(1, losses)
    give(end)
    for q in range(1, quarters):
        with scope("bases"):
            bases_two(q)
        if q < chunks - 1:
            with scope("step"):
                take(end + q)
            factor_two(q)
    for c in range(max(quarters, 1), chunks - 1):
        take(end + c)
        factor_two(c)
    with scope("await"):
        coef_wait(1)
    with scope("coefs"):
        total = message_sum(1)
        own = pl.ds(mine * k_count, k_count)
        coef_acc[...] = coef_table(total).reshape(table, 128)
        misc[0:1, :] = to_lanes(adam_second(c_two[mine], ROOT_ONE * c_grad[mine], ROOT_TWO * coef_acc[own, :]))
        misc[1:2, :] = total[blocks : blocks + 1, :] * loss_scale
    with scope("step"):
        take(end + chunks - 1)
    with scope("factor"):
        factor_two(chunks - 1)


def hand_over(b_in, f_in, misc, b_out, f_out, c_out, l_out, c_held, l_held, sem):
    copies = [
        pltpu.make_async_copy(f_in, f_out, sem.at[0]),
        pltpu.make_async_copy(b_in, b_out, sem.at[1]),
        pltpu.make_async_copy(c_held, c_out, sem.at[2]),
        pltpu.make_async_copy(l_held, l_out, sem.at[3]),
    ]
    for copy in copies[:2]:
        copy.start()
    c_held[...] = misc[0:1, : c_out.shape[1]]
    for i in range(2):
        l_held[i] = misc[1, 8 * i]
    for copy in copies[2:]:
        copy.start()
    for copy in copies:
        copy.wait()


def shards(target_weights, factors, bases, coefficients):
    n, experts = lax.axis_size("col"), lax.axis_size("expert")
    _, d, hl = target_weights.shape
    _, rows, r = factors.shape
    k = bases.shape[0]
    held = pl.BlockSpec(memory_space=pltpu.HBM)
    local = pl.BlockSpec(memory_space=pltpu.VMEM)
    dma = pltpu.SemaphoreType.DMA
    loss_scale = 1.0 / (2.0 * experts * d * hl * n)
    new_factors, new_bases, misc = pl.pallas_call(
        functools.partial(kernel, n, experts, loss_scale),
        out_shape=(
            pltpu.VMEM((rows, r), F32),
            pltpu.VMEM(bases.shape, F32),
            pltpu.VMEM((8, 128), F32),
        ),
        in_specs=[held, held, held, held],
        out_specs=(local, local, local),
        scratch_shapes=[
            pltpu.VMEM((d, hl), BF16),
            pltpu.VMEM(bases.shape, F32),
            pltpu.VMEM((2, d, r), F32),
            pltpu.VMEM((n, rows, r), F32),
            pltpu.VMEM((2, n - 1, rows, r), F32),
            pltpu.VMEM((2, experts, hl // 128, r, 128), F32),
            pltpu.VMEM((experts, k, 128), F32),
            pltpu.VMEM((experts, k, 128), F32),
            pltpu.VMEM((experts, k, 128), F32),
            pltpu.VMEM((experts, k, 128), F32),
            pltpu.VMEM((experts * k, 128), F32),
            pltpu.VMEM((2, n, experts * k // min(experts * k, 128) + 1, 128), F32),
            pltpu.VMEM((experts, 16, 128), F32),
            pltpu.VMEM((rows, r), F32),
            pltpu.VMEM((2 * r, hl + 2 * r), F32),
            pltpu.VMEM((r, hl), F32),
            pltpu.VMEM((4 * r, hl), BF16),
            pltpu.VMEM((8, hl), F32),
            pltpu.VMEM((r, r), F32),
            pltpu.VMEM((r // 2 + 8, r), F32),
            pltpu.VMEM((2, 2, r // 2 + 8, r), F32),
            pltpu.VMEM((2, 2, r // 2 + 8, r), F32),
            pltpu.VMEM((1, k), F32),
            pltpu.SemaphoreType.REGULAR,
            pltpu.SemaphoreType.REGULAR,
            pltpu.SemaphoreType.REGULAR,
            dma((5,)),
            dma((2, LAG)),
            dma((2, 2 * LAG)),
            dma((2,)),
            dma((2,)),
            dma((experts - 1,)),
            dma((experts - 1,)),
            dma((1 + hl // 128, experts - 1)),
            dma((1 + hl // 128, experts - 1)),
            dma((n - 1,)),
            dma((n - 1,)),
        ],
        compiler_params=pltpu.CompilerParams(
            collective_id=0, has_side_effects=True, vmem_limit_bytes=VMEM_MAIN
        ),
    )(target_weights[0], factors[0], bases, coefficients)
    new_bases, new_factors, new_coef, losses = pl.pallas_call(
        hand_over,
        out_shape=(
            jax.ShapeDtypeStruct(bases.shape, F32),
            jax.ShapeDtypeStruct((rows, r), F32),
            jax.ShapeDtypeStruct((1, k), F32),
            jax.ShapeDtypeStruct((2,), F32),
        ),
        in_specs=[local, local, local],
        out_specs=(held, held, held, held),
        scratch_shapes=[pltpu.VMEM((1, k), F32), pltpu.SMEM((2,), F32), dma((4,))],
        compiler_params=pltpu.CompilerParams(vmem_limit_bytes=VMEM_LAST),
    )(new_bases, new_factors, misc)
    return (new_factors[None], new_bases, new_coef, losses)


def solution(mesh):
    return jax.shard_map(
        shards,
        mesh=mesh,
        in_specs=(
            P(("layer", "expert"), None, "col"),
            P(("layer", "expert"), "col", None),
            P("layer", None, "col"),
            P(("layer", "expert"), None),
        ),
        out_specs=(
            P(("layer", "expert"), "col", None),
            P("layer", None, "col"),
            P(("layer", "expert"), None),
            P("layer"),
        ),
        check_vma=False,
    )
```

```python
import functools

import jax
import jax.numpy as jnp
from jax import lax
from jax.experimental import pallas as pl
from jax.experimental.pallas import tpu as pltpu
from jax.sharding import PartitionSpec as P

LEARN_RATE = 0.01
BETA_ONE = 0.9
BETA_TWO = 0.999
EPSILON = 0.0001
HIGHEST = lax.Precision.HIGHEST
MESH = pl.DeviceIdType.MESH
F32 = jnp.float32
BF16 = jnp.bfloat16
CHUNKS = 4
LAG = 3
VMEM_MAIN = 57000000
VMEM_LAST = 4000000


def adam_first(parameter, g):
    return parameter - LEARN_RATE * g / (jnp.abs(g) + EPSILON)


ROOT_ONE = (BETA_TWO * (1.0 - BETA_TWO) / (1.0 - BETA_TWO**2)) ** 0.5
ROOT_TWO = ((1.0 - BETA_TWO) / (1.0 - BETA_TWO**2)) ** 0.5
RATE_ONE = LEARN_RATE * BETA_ONE * (1.0 - BETA_ONE) / (1.0 - BETA_ONE**2) / ROOT_ONE
RATE_TWO = LEARN_RATE * (1.0 - BETA_ONE) / (1.0 - BETA_ONE**2) / ROOT_TWO


def adam_second(parameter, h_one, h_two):
    second = h_one * h_one + h_two * h_two
    root = second * lax.rsqrt(jnp.maximum(second, 1e-30))
    return parameter - (RATE_ONE * h_one + RATE_TWO * h_two) / (root + EPSILON)


def pieces(x):
    upper = x.astype(BF16)
    return upper, (x - upper.astype(F32)).astype(BF16)


def contract(a, b, dims):
    return lax.dot_general(a, b, (dims, ((), ())), preferred_element_type=F32)


def diagonal(size):
    shape = (size, 128)
    return lax.broadcasted_iota(jnp.int32, shape, 0) == lax.broadcasted_iota(jnp.int32, shape, 1)


def to_lanes(column):
    return jnp.sum(jnp.where(diagonal(column.shape[0]), column, 0.0), axis=0, keepdims=True)


def places(shape):
    return lax.broadcasted_iota(jnp.int32, shape, 0), lax.broadcasted_iota(jnp.int32, shape, 1)


def pack_symmetric(g):
    half = g.shape[0] // 2
    row, lane = places((half, 2 * half))
    turned = pltpu.roll(g[half:], half, 1)
    top = jnp.where((lane > row) & (lane < half), turned, g[:half])
    diagonal_row = jnp.sum(jnp.where(lane == row, turned, 0.0), axis=0, keepdims=True)
    return jnp.concatenate([top, jnp.broadcast_to(diagonal_row, (8, 2 * half))], axis=0)


def unpack_symmetric(p):
    half = p.shape[1] // 2
    row, lane = places((half, 2 * half))
    top, diagonal_row = p[:half], jnp.broadcast_to(p[half : half + 1], (half, 2 * half))
    flipped = jnp.transpose(jnp.concatenate([top, top], axis=0))
    upper = jnp.where((lane > row) & (lane < half), flipped[:half], top)
    last = jnp.where(lane > row, top, jnp.where(lane < row, flipped[:half], diagonal_row))
    lower = jnp.where(lane < half, flipped[half:], pltpu.roll(last, half, 1))
    return jnp.concatenate([upper, lower], axis=0)


def lane_sums(x):
    total = jnp.sum(x, axis=(0, 1), keepdims=True)
    return jnp.where(lax.broadcasted_iota(jnp.int32, x.shape, 0) == 0, jnp.broadcast_to(total, x.shape), 0.0)


def to_rows(row, size):
    held = jnp.where(diagonal(size), jnp.broadcast_to(row, (size, 128)), 0.0)
    return jnp.broadcast_to(jnp.sum(held, axis=1, keepdims=True), (size, 128))


def kernel(
    n, experts, loss_scale, t_hbm, f_hbm, b_hbm, c_hbm, f_out, bases, misc,
    target, b_grad, full, part, landed, d_pre, c_one, c_two, c_root, c_grad, coef_acc, message, loss_in, g_one, gram_sum,
    mixed, tall, loss_sum, gram, gram_packed, gram_in, gram_go, c_raw,
    entered, above, known, load_sem, z_send, z_recv, gram_send, gram_recv, ex_send, ex_recv, pre_send, pre_recv, co_send, co_recv,
):
    me = lax.axis_index("col")
    mine = lax.axis_index("expert")
    rows, r = f_hbm.shape
    d, hl = target.shape
    k_count = bases.shape[0]
    scale = 1.0 / (hl * n)
    table = experts * k_count
    block = min(table, 128)
    blocks = table // block
    chunks = CHUNKS
    ch = rows // chunks
    phase = n * chunks
    quarters = hl // 128
    pairs = experts // 2
    mate = mine + 1 - 2 * lax.rem(mine, 2)

    barrier = pltpu.get_barrier_semaphore()

    @pl.when(me < n - 1)
    def _():
        pl.semaphore_signal(barrier, inc=1, device_id={"col": me + 1}, device_id_type=MESH)

    @pl.when(me > 0)
    def _():
        pl.semaphore_wait(barrier, 1)
        pl.semaphore_signal(entered, inc=1, device_id={"col": me - 1}, device_id_type=MESH)

    def greet_experts(semaphore):
        for off in range(1, experts):
            pl.semaphore_signal(
                semaphore, inc=1, device_id={"expert": lax.rem(mine + off, experts)}, device_id_type=MESH
            )

    @pl.when(me == 0)
    def _():
        greet_experts(barrier)

    loads = [
        pltpu.make_async_copy(f_hbm, full.at[0, pl.ds(pl.multiple_of(me * rows, 16), rows)], load_sem.at[0]),
        pltpu.make_async_copy(b_hbm, bases, load_sem.at[1]),
        pltpu.make_async_copy(c_hbm, c_raw, load_sem.at[2]),
    ]
    halves = 2 if n % 2 == 0 else 1
    for j in range(halves):
        at = pl.ds(j * (d // halves), d // halves)
        loads.append(pltpu.make_async_copy(t_hbm.at[at], target.at[at], load_sem.at[3 + j]))

    def place_of(way):
        return me if way == 0 else n - 1 - me

    def shard_at(way, place):
        return place if way == 0 else n - 1 - place

    def split(s):
        it = s // phase
        u = s - it * phase
        b = u // chunks
        return it, b, u - b * chunks

    def z_copy(way, s, src, dst):
        return pltpu.make_async_remote_copy(
            src_ref=src, dst_ref=dst, send_sem=z_send.at[way, s % LAG], recv_sem=z_recv.at[way, s % (2 * LAG)],
            device_id={"col": me + 1 - 2 * way}, device_id_type=MESH,
        )

    def rows_of(shard, c):
        return pl.ds(pl.multiple_of(shard * rows + c * ch, 16), ch)

    def chunk_of(c):
        return pl.ds(pl.multiple_of(c * ch, 16), ch)

    def gather_copy(way, s, shard):
        it, b, c = split(s)
        ref = full.at[it, rows_of(shard, c)]
        return z_copy(way, s, ref, ref)

    def scatter_copy(way, s, shard):
        it, b, c = split(s)
        return z_copy(way, s, part.at[shard, chunk_of(c)], landed.at[way, b - 1, chunk_of(c)])

    def on_send(way, s, act):
        it, b, c = split(s)
        p = place_of(way)

        @pl.when((p < n - 1) & (b <= p))
        def _():
            act(gather_copy(way, s, shard_at(way, p - b)))

        @pl.when((p < n - 1) & (b > p))
        def _():
            act(scatter_copy(way, s, shard_at(way, n + p - b)))

    def arrive(way, s):
        it, b, c = split(s)
        p = place_of(way)

        @pl.when((p > 0) & (b <= p - 1))
        def _():
            gather_copy(way, s, shard_at(way, p - 1 - b)).wait_recv()

        @pl.when((p > 0) & (b > p - 1))
        def _():
            shard = shard_at(way, n + p - 1 - b)
            scatter_copy(way, s, shard).wait_recv()
            at = chunk_of(c)
            part[shard, at, :] = part[shard, at, :] + landed[way, b - 1, at, :]

    def take(s):
        for way in range(2):
            on_send(way, s - LAG, lambda copy: copy.wait_send())
        for way in range(2):
            arrive(way, s - LAG)

    def give(s):
        for way in range(2):
            on_send(way, s, lambda copy: copy.start())

    def step(s):
        take(s)
        give(s)

    def give_first(way):
        @pl.when(place_of(way) < n - 1)
        def _():
            if way == 0:
                pl.semaphore_wait(entered, 1)
            for s in range(LAG):
                z_copy(way, s, f_hbm.at[chunk_of(s)], full.at[0, rows_of(me, s)]).start()

    def gram_copy(it, way):
        return pltpu.make_async_remote_copy(
            src_ref=gram_go.at[it, way], dst_ref=gram_in.at[it, way], send_sem=gram_send.at[way],
            recv_sem=gram_recv.at[way], device_id={"col": me + 1 - 2 * way}, device_id_type=MESH,
        )

    def gram_hop(it, s, start):
        for way in range(2):
            p = place_of(way)
            now = s == start + p * LAG

            @pl.when(now & (p > 0))
            def _():
                gram_copy(it, way).wait_recv()

            @pl.when(now & (p == 0) & (p < n - 1))
            def _():
                gram_go[it, way] = gram_packed[...]

            @pl.when(now & (p > 0) & (p < n - 1))
            def _():
                gram_go[it, way] = gram_packed[...] + gram_in[it, way]

            @pl.when(now & (p < n - 1))
            def _():
                gram_copy(it, way).start()

    def gram_close(it):
        for way in range(2):
            p = place_of(way)

            @pl.when(p > 0)
            def _():
                gram_packed[...] = gram_packed[...] + gram_in[it, way]

            @pl.when(p < n - 1)
            def _():
                gram_copy(it, way).wait_send()

        gram[...] = unpack_symmetric(gram_packed[...])

    def expert_copy(ref, off):
        place = ref.at[mine]
        return pltpu.make_async_remote_copy(
            src_ref=place, dst_ref=place, send_sem=ex_send.at[off - 1], recv_sem=ex_recv.at[off - 1],
            device_id={"expert": lax.rem(mine + off, experts)}, device_id_type=MESH,
        )

    def expert_start(ref):
        for off in range(1, experts):
            expert_copy(ref, off).start()

    def expert_wait(ref):
        for off in range(1, experts):
            expert_copy(ref, off).wait()

    def pre_copy(it, q, e, i, target):
        place = d_pre.at[it, e] if it == 0 else d_pre.at[it, e, q]
        return pltpu.make_async_remote_copy(
            src_ref=place, dst_ref=place, send_sem=pre_send.at[it + q, i], recv_sem=pre_recv.at[it + q, i],
            device_id={"expert": target}, device_id_type=MESH,
        )

    def across(i):
        return lax.rem(mine + 2 * i, experts)

    def pre_start(it):
        for q in range(quarters if it else 1):
            for i in range(1, pairs):
                pre_copy(it, q, mine, i - 1, across(i)).start()
            pre_copy(it, q, mine, pairs - 1, mate).start()

    def pre_forward(it, q):
        for i in range(1, pairs):
            source = across(pairs - i)
            pre_copy(it, q, source, i - 1, mate).wait_recv()
            pre_copy(it, q, source, pairs - 1 + i, mate).start()

    def pre_wait(it, q):
        for i in range(1, pairs):
            pre_copy(it, q, mine, i - 1, across(i)).wait_send()
        pre_copy(it, q, mine, pairs - 1, mate).wait_send()
        pre_copy(it, q, mate, pairs - 1, mate).wait_recv()
        for i in range(1, pairs):
            pre_copy(it, q, across(pairs - i), pairs - 1 + i, mate).wait_send()
            pre_copy(it, q, lax.rem(mate + 2 * (pairs - i), experts), pairs - 1 + i, mate).wait_recv()

    def coef_copy(it, off):
        place = message.at[it, me]
        return pltpu.make_async_remote_copy(
            src_ref=place, dst_ref=place, send_sem=co_send.at[off - 1], recv_sem=co_recv.at[off - 1],
            device_id={"col": lax.rem(me + off, n)}, device_id_type=MESH,
        )

    def mix(c_ref):
        for q in range(0, hl, 128):
            def add(k, total):
                return total + c_ref[mine, pl.ds(k, 1), :] * bases[k, :, q : q + 128]

            value = jnp.tanh(lax.fori_loop(0, k_count, add, jnp.zeros((r, 128), F32), unroll=4))
            mixed[:, q : q + 128] = value
            upper, lower = pieces(value)
            for i in range(2):
                tall[2 * i * r : (2 * i + 1) * r, q : q + 128] = upper
                tall[(2 * i + 1) * r : (2 * i + 2) * r, q : q + 128] = lower

    def gram_local():
        cut = tall[: 2 * r, :]
        both = contract(cut, cut, ((1,), (1,)))
        both = both[:r] + both[r:]
        gram_packed[...] = pack_symmetric(both[:, :r] + both[:, r:])

    def project(j):
        def one(c, carry):
            value = contract(target[rows_of(j, c), :], tall[: 2 * r, :], ((1,), (1,)))
            part[j, chunk_of(c), :] = value[:, :r] + value[:, r:]
            return carry

        lax.fori_loop(0, chunks, one, 0)

    def absorb(it, shard, c):
        at = rows_of(shard, c)
        cut = jnp.concatenate(pieces(full[it, at, :]), axis=1)
        gram_sum[...] += contract(cut, jnp.concatenate([target[at, :], cut], axis=1), ((0,), (0,)))

    def loss_add(it, shard, c):
        at = rows_of(shard, c)
        one, two = pieces(full[it, at, :])
        wide = jnp.concatenate([one, one, two, two], axis=1)
        residual = contract(wide, tall[...], ((1,), (0,))) - target[at, :].astype(F32)
        loss_sum[...] += jnp.sum((residual * residual).reshape(ch // 8, 8, hl), axis=0)

    def arrived(way, s):
        it, b, c = split(s)
        p = place_of(way)
        return (p > 0) & (b <= p - 1), shard_at(way, p - 1 - b), c

    def for_arrived(act, it, s, own):
        first, first_shard, c = arrived(0, s)
        second, second_shard, _ = arrived(1, s)

        def one(i, carry):
            valid = jnp.where(i == 0, first, jnp.where(i == 1, second, own))
            shard = jnp.where(i == 0, first_shard, jnp.where(i == 1, second_shard, me))

            @pl.when(valid)
            def _():
                act(it, shard, c)

            return carry

        lax.fori_loop(0, 3, one, 0)

    def pre_gradient(it):
        total = gram_sum[:r, :] + gram_sum[r:, :]
        square = total[:, hl : hl + r] + total[:, hl + r :]
        now = mixed[...]
        d_mixed = jnp.dot(square, now, precision=HIGHEST, preferred_element_type=F32) - total[:, :hl]
        value = d_mixed * scale * (1.0 - now * now)
        for q in range(quarters):
            d_pre[it, mine, q] = value[:, q * 128 : (q + 1) * 128]

    def loss_close(it):
        total = loss_sum[:, 0:128]
        for q in range(128, hl, 128):
            total = total + loss_sum[:, q : q + 128]
        loss_in[mine, it * 8 : it * 8 + 8, :] = total
        loss_sum[...] = jnp.zeros_like(loss_sum)

    def combine(c_ref, it, k, q):
        total = c_ref[0, pl.ds(k, 1), :] * d_pre[it, 0, q]
        for e in range(1, experts):
            total = total + c_ref[e, pl.ds(k, 1), :] * d_pre[it, e, q]
        return total

    def columns(q):
        return slice(q * 128, (q + 1) * 128)

    def coef_pass(it, which):
        def one(k, carry):
            sums = [jnp.zeros((8, 128), F32)] * experts
            for q in which:
                values = bases[k, :, columns(q)]
                for e in range(experts):
                    held = values * d_pre[it, e, q]
                    sums[e] = sums[e] + jnp.sum(held.reshape(r // 8, 8, 128), axis=0)
            for e in range(experts):
                at = pl.ds(e * k_count + k, 1)
                value = jnp.sum(sums[e], axis=0, keepdims=True)
                coef_acc[at, :] = value if 0 in which else coef_acc[at, :] + value
            return carry

        lax.fori_loop(0, k_count, one, 0)

    def coef_send(it, losses=None):
        message[it, me] = jnp.zeros(message.shape[2:], F32)
        for i in range(blocks):
            column = jnp.sum(coef_acc[i * block : (i + 1) * block, :], axis=1, keepdims=True)
            message[it, me, i : i + 1, :] = to_lanes(jnp.broadcast_to(column, (block, 128)))
        if losses is not None:
            message[it, me, blocks : blocks + 1, :] = to_lanes(
                jnp.concatenate([lane_sums(losses[:8]), lane_sums(losses[8:])], axis=0)
            )
        for off in range(1, n):
            coef_copy(it, off).start()

    def coef_wait(it):
        for off in range(1, n):
            coef_copy(it, off).wait()

    def message_sum(it):
        total = message[it, 0]
        for c in range(1, n):
            total = total + message[it, c]
        return total

    def coef_table(total):
        held = [to_rows(total[i : i + 1, :], block) for i in range(blocks)]
        held = held[0] if blocks == 1 else jnp.concatenate(held, axis=0)
        return held.reshape(experts, k_count, 128)

    def bases_one(low, high):
        def one(k, carry):
            for q in range(quarters):
                gradient = combine(c_one, 0, k, q)
                b_grad[k, :, columns(q)] = ROOT_ONE * gradient
                bases[k, :, columns(q)] = adam_first(bases[k, :, columns(q)], gradient)
            return carry

        lax.fori_loop(low, high, one, 0)

    def bases_two(q):
        def one(k, carry):
            values = bases[k, :, columns(q)]
            bases[k, :, columns(q)] = adam_second(values, b_grad[k, :, columns(q)], combine(c_root, 1, k, q))
            return carry

        lax.fori_loop(0, k_count, one, 0, unroll=2)

    def factor_product(it, c):
        return jnp.dot(
            full[it, rows_of(me, c), :], gram[...], precision=HIGHEST, preferred_element_type=F32
        )

    def factor_one(c):
        at = chunk_of(c)
        g = (factor_product(0, c) - part[me, at, :]) * scale
        g_one[at, :] = ROOT_ONE * g
        full[1, rows_of(me, c), :] = adam_first(full[0, rows_of(me, c), :], g)

    def factor_two(c):
        at = chunk_of(c)
        g = (full[0, rows_of(me, c), :] - part[me, at, :]) * (ROOT_TWO * scale)
        f_out[at, :] = adam_second(full[1, rows_of(me, c), :], g_one[at, :], g)

    scope = jax.named_scope
    with scope("enter"):
        give_first(1)
        for load in loads:
            load.start()
        give_first(0)
    misc[...] = jnp.zeros_like(misc)
    loads[2].wait()
    misc[0:1, :k_count] = c_raw[...]
    c_one[mine] = to_rows(misc[0:1, :], k_count)
    gram_sum[...] = jnp.zeros_like(gram_sum)
    loss_sum[...] = jnp.zeros_like(loss_sum)
    with scope("load"):
        loads[1].wait()
    with scope("mix"):
        mix(c_one)
        gram_local()
    with scope("project"):
        for j in range(n):
            if j % (n // halves) == 0:
                loads[3 + j // (n // halves)].wait()
            project(j)

    with scope("greet"):
        @pl.when(me == 0)
        def _():
            pl.semaphore_wait(barrier, experts - 1)

        @pl.when(me > 0)
        def _():
            pl.semaphore_wait(known, 1)

        @pl.when(me < n - 1)
        def _():
            greet_experts(above)
            pl.semaphore_wait(above, experts - 1)
            pl.semaphore_signal(known, inc=1, device_id={"col": me + 1}, device_id_type=MESH)

    expert_start(c_one)
    loads[0].wait()
    final = phase - chunks + LAG

    def early(s, carry):
        gram_hop(0, s, LAG)
        with scope("step"):
            step(s)
        own = s - LAG < chunks
        for_arrived(absorb, 0, s - LAG, own)
        for_arrived(loss_add, 0, s - LAG, own)
        return carry

    lax.fori_loop(LAG, final, early, 0)
    with scope("pre"):
        pre_gradient(0)
        expert_wait(c_one)
        pre_start(0)
        gram_close(0)
        loss_close(0)
        gram_sum[...] = jnp.zeros_like(gram_sum)

    def base_work(i):
        if i == 0:
            with scope("forward"):
                pre_forward(0, 0)
        elif i == 1:
            with scope("wait"):
                pre_wait(0, 0)
            with scope("coef"):
                coef_pass(0, range(quarters))
                coef_send(0)
        elif i == 2:
            with scope("bases"):
                bases_one(0, k_count // 2)
        else:
            with scope("bases"):
                bases_one(k_count // 2, k_count)

    for c in range(chunks):
        with scope("step"):
            step(final + c)
        factor_one(c)
        absorb(1, me, c)
        base_work(c)

    begin = phase + chunks
    behind = begin - phase - LAG
    for s in range(final + chunks, begin):
        with scope("step"):
            step(s)
        for_arrived(absorb, 1, s - LAG, False)
    with scope("await"):
        coef_wait(0)
    c_grad[...] = coef_table(message_sum(0))
    c_two[...] = adam_first(c_one[...], c_grad[...])
    c_root[...] = ROOT_TWO * c_two[...]
    with scope("mix"):
        mix(c_two)
        gram_local()
    with scope("project"):
        for j in range(n):
            project(j)

    def late(s, carry):
        gram_hop(1, s, begin)
        with scope("step"):
            step(s)
        for_arrived(absorb, 1, s - LAG, False)
        for_arrived(loss_add, 1, s - LAG - behind, False)

        @pl.when(s - begin < chunks)
        def _():
            loss_add(1, me, s - begin)

        return carry

    end = phase + final
    lax.fori_loop(begin, end, late, 0)
    with scope("pre"):
        pre_gradient(1)
        pre_start(1)
        gram_close(1)
    with scope("product"):
        for c in range(chunks):
            full[0, rows_of(me, c), :] = factor_product(1, c)
    for s in range(end - LAG - behind, end - LAG):
        for_arrived(loss_add, 1, s, False)
    loss_close(1)
    expert_start(loss_in)
    with scope("forward"):
        pre_forward(1, 0)
    with scope("step"):
        take(end)
    factor_two(0)
    with scope("wait"):
        pre_wait(1, 0)
    with scope("coef"):
        coef_pass(1, (0,))
    with scope("forward"):
        for q in range(1, quarters):
            pre_forward(1, q)
    with scope("bases"):
        bases_two(0)
    with scope("wait"):
        for q in range(1, quarters):
            pre_wait(1, q)
    with scope("coef"):
        if quarters > 1:
            coef_pass(1, range(1, quarters))
        expert_wait(loss_in)
        losses = loss_in[0]
        for e in range(1, experts):
            losses = losses + loss_in[e]
        coef_send(1, losses)
    give(end)
    for q in range(1, quarters):
        with scope("bases"):
            bases_two(q)
        if q < chunks - 1:
            with scope("step"):
                take(end + q)
            factor_two(q)
    for c in range(max(quarters, 1), chunks - 1):
        take(end + c)
        factor_two(c)
    with scope("await"):
        coef_wait(1)
    with scope("coefs"):
        total = message_sum(1)
        own = pl.ds(mine * k_count, k_count)
        coef_acc[...] = coef_table(total).reshape(table, 128)
        misc[0:1, :] = to_lanes(adam_second(c_two[mine], ROOT_ONE * c_grad[mine], ROOT_TWO * coef_acc[own, :]))
        misc[1:2, :] = total[blocks : blocks + 1, :] * loss_scale
    last = end + chunks - 1 - LAG
    with scope("step"):
        for way in range(2):
            arrive(way, last)
    with scope("factor"):
        factor_two(chunks - 1)
    for way in range(2):
        on_send(way, last, lambda copy: copy.wait_send())


def hand_over(b_in, f_in, misc, b_out, f_out, c_out, l_out, c_held, l_held, sem):
    copies = [
        pltpu.make_async_copy(f_in, f_out, sem.at[0]),
        pltpu.make_async_copy(b_in, b_out, sem.at[1]),
        pltpu.make_async_copy(c_held, c_out, sem.at[2]),
        pltpu.make_async_copy(l_held, l_out, sem.at[3]),
    ]
    for copy in copies[:2]:
        copy.start()
    c_held[...] = misc[0:1, : c_out.shape[1]]
    for i in range(2):
        l_held[i] = misc[1, 8 * i]
    for copy in copies[2:]:
        copy.start()
    for copy in copies:
        copy.wait()


def shards(target_weights, factors, bases, coefficients):
    n, experts = lax.axis_size("col"), lax.axis_size("expert")
    _, d, hl = target_weights.shape
    _, rows, r = factors.shape
    k = bases.shape[0]
    held = pl.BlockSpec(memory_space=pltpu.HBM)
    local = pl.BlockSpec(memory_space=pltpu.VMEM)
    dma = pltpu.SemaphoreType.DMA
    loss_scale = 1.0 / (2.0 * experts * d * hl * n)
    new_factors, new_bases, misc = pl.pallas_call(
        functools.partial(kernel, n, experts, loss_scale),
        out_shape=(
            pltpu.VMEM((rows, r), F32),
            pltpu.VMEM(bases.shape, F32),
            pltpu.VMEM((8, 128), F32),
        ),
        in_specs=[held, held, held, held],
        out_specs=(local, local, local),
        scratch_shapes=[
            pltpu.VMEM((d, hl), BF16),
            pltpu.VMEM(bases.shape, F32),
            pltpu.VMEM((2, d, r), F32),
            pltpu.VMEM((n, rows, r), F32),
            pltpu.VMEM((2, n - 1, rows, r), F32),
            pltpu.VMEM((2, experts, hl // 128, r, 128), F32),
            pltpu.VMEM((experts, k, 128), F32),
            pltpu.VMEM((experts, k, 128), F32),
            pltpu.VMEM((experts, k, 128), F32),
            pltpu.VMEM((experts, k, 128), F32),
            pltpu.VMEM((experts * k, 128), F32),
            pltpu.VMEM((2, n, experts * k // min(experts * k, 128) + 1, 128), F32),
            pltpu.VMEM((experts, 16, 128), F32),
            pltpu.VMEM((rows, r), F32),
            pltpu.VMEM((2 * r, hl + 2 * r), F32),
            pltpu.VMEM((r, hl), F32),
            pltpu.VMEM((4 * r, hl), BF16),
            pltpu.VMEM((8, hl), F32),
            pltpu.VMEM((r, r), F32),
            pltpu.VMEM((r // 2 + 8, r), F32),
            pltpu.VMEM((2, 2, r // 2 + 8, r), F32),
            pltpu.VMEM((2, 2, r // 2 + 8, r), F32),
            pltpu.VMEM((1, k), F32),
            pltpu.SemaphoreType.REGULAR,
            pltpu.SemaphoreType.REGULAR,
            pltpu.SemaphoreType.REGULAR,
            dma((5,)),
            dma((2, LAG)),
            dma((2, 2 * LAG)),
            dma((2,)),
            dma((2,)),
            dma((experts - 1,)),
            dma((experts - 1,)),
            dma((1 + hl // 128, experts - 1)),
            dma((1 + hl // 128, experts - 1)),
            dma((n - 1,)),
            dma((n - 1,)),
        ],
        compiler_params=pltpu.CompilerParams(
            collective_id=0, has_side_effects=True, vmem_limit_bytes=VMEM_MAIN
        ),
    )(target_weights[0], factors[0], bases, coefficients)
    new_bases, new_factors, new_coef, losses = pl.pallas_call(
        hand_over,
        out_shape=(
            jax.ShapeDtypeStruct(bases.shape, F32),
            jax.ShapeDtypeStruct((rows, r), F32),
            jax.ShapeDtypeStruct((1, k), F32),
            jax.ShapeDtypeStruct((2,), F32),
        ),
        in_specs=[local, local, local],
        out_specs=(held, held, held, held),
        scratch_shapes=[pltpu.VMEM((1, k), F32), pltpu.SMEM((2,), F32), dma((4,))],
        compiler_params=pltpu.CompilerParams(vmem_limit_bytes=VMEM_LAST),
    )(new_bases, new_factors, misc)
    return (new_factors[None], new_bases, new_coef, losses)


def solution(mesh):
    return jax.shard_map(
        shards,
        mesh=mesh,
        in_specs=(
            P(("layer", "expert"), None, "col"),
            P(("layer", "expert"), "col", None),
            P("layer", None, "col"),
            P(("layer", "expert"), None),
        ),
        out_specs=(
            P(("layer", "expert"), "col", None),
            P("layer", None, "col"),
            P(("layer", "expert"), None),
            P("layer"),
        ),
        check_vma=False,
    )
```

```python
import functools

import jax
import jax.numpy as jnp
from jax import lax
from jax.experimental import pallas as pl
from jax.experimental.pallas import tpu as pltpu
from jax.sharding import PartitionSpec as P

LEARN_RATE = 0.01
BETA_ONE = 0.9
BETA_TWO = 0.999
EPSILON = 0.0001
HIGHEST = lax.Precision.HIGHEST
MESH = pl.DeviceIdType.MESH
F32 = jnp.float32
BF16 = jnp.bfloat16
CHUNKS = 4
LAG = 3
VMEM_MAIN = 57000000
VMEM_LAST = 4000000


def adam_first(parameter, g):
    return parameter - LEARN_RATE * g / (jnp.abs(g) + EPSILON)


ROOT_ONE = (BETA_TWO * (1.0 - BETA_TWO) / (1.0 - BETA_TWO**2)) ** 0.5
ROOT_TWO = ((1.0 - BETA_TWO) / (1.0 - BETA_TWO**2)) ** 0.5
RATE_ONE = LEARN_RATE * BETA_ONE * (1.0 - BETA_ONE) / (1.0 - BETA_ONE**2) / ROOT_ONE
RATE_TWO = LEARN_RATE * (1.0 - BETA_ONE) / (1.0 - BETA_ONE**2) / ROOT_TWO


def adam_second(parameter, h_one, h_two):
    second = h_one * h_one + h_two * h_two
    root = second * lax.rsqrt(jnp.maximum(second, 1e-30))
    return parameter - (RATE_ONE * h_one + RATE_TWO * h_two) / (root + EPSILON)


def pieces(x):
    upper = x.astype(BF16)
    return upper, (x - upper.astype(F32)).astype(BF16)


def contract(a, b, dims):
    return lax.dot_general(a, b, (dims, ((), ())), preferred_element_type=F32)


def diagonal(size):
    shape = (size, 128)
    return lax.broadcasted_iota(jnp.int32, shape, 0) == lax.broadcasted_iota(jnp.int32, shape, 1)


def to_lanes(column):
    return jnp.sum(jnp.where(diagonal(column.shape[0]), column, 0.0), axis=0, keepdims=True)


def places(shape):
    return lax.broadcasted_iota(jnp.int32, shape, 0), lax.broadcasted_iota(jnp.int32, shape, 1)


def pack_symmetric(g):
    half = g.shape[0] // 2
    row, lane = places((half, 2 * half))
    turned = pltpu.roll(g[half:], half, 1)
    top = jnp.where((lane > row) & (lane < half), turned, g[:half])
    diagonal_row = jnp.sum(jnp.where(lane == row, turned, 0.0), axis=0, keepdims=True)
    return jnp.concatenate([top, jnp.broadcast_to(diagonal_row, (8, 2 * half))], axis=0)


def unpack_symmetric(p):
    half = p.shape[1] // 2
    row, lane = places((half, 2 * half))
    top, diagonal_row = p[:half], jnp.broadcast_to(p[half : half + 1], (half, 2 * half))
    flipped = jnp.transpose(jnp.concatenate([top, top], axis=0))
    upper = jnp.where((lane > row) & (lane < half), flipped[:half], top)
    last = jnp.where(lane > row, top, jnp.where(lane < row, flipped[:half], diagonal_row))
    lower = jnp.where(lane < half, flipped[half:], pltpu.roll(last, half, 1))
    return jnp.concatenate([upper, lower], axis=0)


def lane_sums(x):
    total = jnp.sum(x, axis=(0, 1), keepdims=True)
    return jnp.where(lax.broadcasted_iota(jnp.int32, x.shape, 0) == 0, jnp.broadcast_to(total, x.shape), 0.0)


def to_rows(row, size):
    held = jnp.where(diagonal(size), jnp.broadcast_to(row, (size, 128)), 0.0)
    return jnp.broadcast_to(jnp.sum(held, axis=1, keepdims=True), (size, 128))


def kernel(
    n, experts, loss_scale, t_hbm, f_hbm, b_hbm, c_hbm, f_out, bases, misc,
    target, b_grad, full, part, landed, d_pre, c_one, c_two, c_root, c_grad, coef_acc, message, loss_in, g_one, gram_sum,
    mixed, tall, loss_sum, gram, gram_packed, gram_in, gram_go, c_raw,
    entered, above, known, load_sem, z_send, z_recv, gram_send, gram_recv, ex_send, ex_recv, pre_send, pre_recv, co_send, co_recv,
):
    me = lax.axis_index("col")
    mine = lax.axis_index("expert")
    rows, r = f_hbm.shape
    d, hl = target.shape
    k_count = bases.shape[0]
    scale = 1.0 / (hl * n)
    table = experts * k_count
    block = min(table, 128)
    blocks = table // block
    chunks = CHUNKS
    ch = rows // chunks
    phase = n * chunks
    quarters = hl // 128
    width = 2 if quarters % 2 == 0 else 1
    pairs = experts // 2
    mate = mine + 1 - 2 * lax.rem(mine, 2)

    barrier = pltpu.get_barrier_semaphore()

    @pl.when(me < n - 1)
    def _():
        pl.semaphore_signal(barrier, inc=1, device_id={"col": me + 1}, device_id_type=MESH)

    def greet_experts(semaphore):
        for off in range(1, experts):
            pl.semaphore_signal(
                semaphore, inc=1, device_id={"expert": lax.rem(mine + off, experts)}, device_id_type=MESH
            )

    @pl.when(me == 0)
    def _():
        greet_experts(barrier)

    loads = [
        pltpu.make_async_copy(f_hbm, full.at[0, pl.ds(pl.multiple_of(me * rows, 16), rows)], load_sem.at[0]),
        pltpu.make_async_copy(b_hbm, bases, load_sem.at[1]),
        pltpu.make_async_copy(c_hbm, c_raw, load_sem.at[2]),
    ]
    halves = 2 if n % 2 == 0 else 1
    for j in range(halves):
        at = pl.ds(j * (d // halves), d // halves)
        loads.append(pltpu.make_async_copy(t_hbm.at[at], target.at[at], load_sem.at[3 + j]))
    for load in loads:
        load.start()

    @pl.when(me > 0)
    def _():
        pl.semaphore_wait(barrier, 1)
        pl.semaphore_signal(entered, inc=1, device_id={"col": me - 1}, device_id_type=MESH)

    def place_of(way):
        return me if way == 0 else n - 1 - me

    def shard_at(way, place):
        return place if way == 0 else n - 1 - place

    def split(s):
        it = s // phase
        u = s - it * phase
        b = u // chunks
        return it, b, u - b * chunks

    def z_copy(way, s, src, dst):
        return pltpu.make_async_remote_copy(
            src_ref=src, dst_ref=dst, send_sem=z_send.at[way, s % LAG], recv_sem=z_recv.at[way, s % (2 * LAG)],
            device_id={"col": me + 1 - 2 * way}, device_id_type=MESH,
        )

    def rows_of(shard, c):
        return pl.ds(pl.multiple_of(shard * rows + c * ch, 16), ch)

    def chunk_of(c):
        return pl.ds(pl.multiple_of(c * ch, 16), ch)

    def gather_copy(way, s, shard):
        it, b, c = split(s)
        ref = full.at[it, rows_of(shard, c)]
        return z_copy(way, s, ref, ref)

    def scatter_copy(way, s, shard):
        it, b, c = split(s)
        return z_copy(way, s, part.at[shard, chunk_of(c)], landed.at[way, b - 1, chunk_of(c)])

    def on_send(way, s, act):
        it, b, c = split(s)
        p = place_of(way)

        @pl.when((p < n - 1) & (b <= p))
        def _():
            act(gather_copy(way, s, shard_at(way, p - b)))

        @pl.when((p < n - 1) & (b > p))
        def _():
            act(scatter_copy(way, s, shard_at(way, n + p - b)))

    def arrive(way, s):
        it, b, c = split(s)
        p = place_of(way)

        @pl.when((p > 0) & (b <= p - 1))
        def _():
            gather_copy(way, s, shard_at(way, p - 1 - b)).wait_recv()

        @pl.when((p > 0) & (b > p - 1))
        def _():
            shard = shard_at(way, n + p - 1 - b)
            scatter_copy(way, s, shard).wait_recv()
            at = chunk_of(c)
            part[shard, at, :] = part[shard, at, :] + landed[way, b - 1, at, :]

    def take(s):
        for way in range(2):
            on_send(way, s - LAG, lambda copy: copy.wait_send())
        for way in range(2):
            arrive(way, s - LAG)

    def give(s):
        for way in range(2):
            on_send(way, s, lambda copy: copy.start())

    def step(s):
        take(s)
        give(s)

    def give_first(way):
        @pl.when(place_of(way) < n - 1)
        def _():
            if way == 0:
                pl.semaphore_wait(entered, 1)
            for s in range(LAG):
                z_copy(way, s, f_hbm.at[chunk_of(s)], full.at[0, rows_of(me, s)]).start()

    def gram_copy(it, way):
        return pltpu.make_async_remote_copy(
            src_ref=gram_go.at[it, way], dst_ref=gram_in.at[it, way], send_sem=gram_send.at[way],
            recv_sem=gram_recv.at[way], device_id={"col": me + 1 - 2 * way}, device_id_type=MESH,
        )

    def gram_hop(it, s, start):
        for way in range(2):
            p = place_of(way)
            now = s == start + p * LAG

            @pl.when(now & (p > 0))
            def _():
                gram_copy(it, way).wait_recv()

            @pl.when(now & (p == 0) & (p < n - 1))
            def _():
                gram_go[it, way] = gram_packed[...]

            @pl.when(now & (p > 0) & (p < n - 1))
            def _():
                gram_go[it, way] = gram_packed[...] + gram_in[it, way]

            @pl.when(now & (p < n - 1))
            def _():
                gram_copy(it, way).start()

    def gram_close(it):
        for way in range(2):
            p = place_of(way)

            @pl.when(p > 0)
            def _():
                gram_packed[...] = gram_packed[...] + gram_in[it, way]

            @pl.when(p < n - 1)
            def _():
                gram_copy(it, way).wait_send()

        gram[...] = unpack_symmetric(gram_packed[...])

    def expert_copy(ref, off):
        place = ref.at[mine]
        return pltpu.make_async_remote_copy(
            src_ref=place, dst_ref=place, send_sem=ex_send.at[off - 1], recv_sem=ex_recv.at[off - 1],
            device_id={"expert": lax.rem(mine + off, experts)}, device_id_type=MESH,
        )

    def expert_start(ref):
        for off in range(1, experts):
            expert_copy(ref, off).start()

    def expert_wait(ref):
        for off in range(1, experts):
            expert_copy(ref, off).wait()

    def pre_copy(it, q, e, i, target):
        place = d_pre.at[it, e] if it == 0 else d_pre.at[it, e, pl.ds(q * width, width)]
        return pltpu.make_async_remote_copy(
            src_ref=place, dst_ref=place, send_sem=pre_send.at[it + q, i], recv_sem=pre_recv.at[it + q, i],
            device_id={"expert": target}, device_id_type=MESH,
        )

    def across(i):
        return lax.rem(mine + 2 * i, experts)

    def pre_start(it):
        for q in range(quarters // width if it else 1):
            for i in range(1, pairs):
                pre_copy(it, q, mine, i - 1, across(i)).start()
            pre_copy(it, q, mine, pairs - 1, mate).start()

    def pre_forward(it, q):
        for i in range(1, pairs):
            source = across(pairs - i)
            pre_copy(it, q, source, i - 1, mate).wait_recv()
            pre_copy(it, q, source, pairs - 1 + i, mate).start()

    def pre_wait(it, q):
        for i in range(1, pairs):
            pre_copy(it, q, mine, i - 1, across(i)).wait_send()
        pre_copy(it, q, mine, pairs - 1, mate).wait_send()
        pre_copy(it, q, mate, pairs - 1, mate).wait_recv()
        for i in range(1, pairs):
            pre_copy(it, q, across(pairs - i), pairs - 1 + i, mate).wait_send()
            pre_copy(it, q, lax.rem(mate + 2 * (pairs - i), experts), pairs - 1 + i, mate).wait_recv()

    def coef_copy(it, off):
        place = message.at[it, me]
        return pltpu.make_async_remote_copy(
            src_ref=place, dst_ref=place, send_sem=co_send.at[off - 1], recv_sem=co_recv.at[off - 1],
            device_id={"col": lax.rem(me + off, n)}, device_id_type=MESH,
        )

    def mix(c_ref):
        for q in range(0, hl, 128):
            def add(k, total):
                return total + c_ref[mine, pl.ds(k, 1), :] * bases[k, :, q : q + 128]

            value = jnp.tanh(lax.fori_loop(0, k_count, add, jnp.zeros((r, 128), F32), unroll=4))
            mixed[:, q : q + 128] = value
            upper, lower = pieces(value)
            for i in range(2):
                tall[2 * i * r : (2 * i + 1) * r, q : q + 128] = upper
                tall[(2 * i + 1) * r : (2 * i + 2) * r, q : q + 128] = lower

    def gram_local():
        cut = tall[: 2 * r, :]
        both = contract(cut, cut, ((1,), (1,)))
        both = both[:r] + both[r:]
        gram_packed[...] = pack_symmetric(both[:, :r] + both[:, r:])

    def project(j):
        def one(c, carry):
            value = contract(target[rows_of(j, c), :], tall[: 2 * r, :], ((1,), (1,)))
            part[j, chunk_of(c), :] = value[:, :r] + value[:, r:]
            return carry

        lax.fori_loop(0, chunks, one, 0)

    def absorb(it, shard, c):
        at = rows_of(shard, c)
        cut = jnp.concatenate(pieces(full[it, at, :]), axis=1)
        gram_sum[...] += contract(cut, jnp.concatenate([target[at, :], cut], axis=1), ((0,), (0,)))

    def loss_add(it, shard, c):
        at = rows_of(shard, c)
        one, two = pieces(full[it, at, :])
        wide = jnp.concatenate([one, one, two, two], axis=1)
        residual = contract(wide, tall[...], ((1,), (0,))) - target[at, :].astype(F32)
        loss_sum[...] += jnp.sum((residual * residual).reshape(ch // 8, 8, hl), axis=0)

    def arrived(way, s):
        it, b, c = split(s)
        p = place_of(way)
        return (p > 0) & (b <= p - 1), shard_at(way, p - 1 - b), c

    def for_arrived(act, it, s, own):
        first, first_shard, c = arrived(0, s)
        second, second_shard, _ = arrived(1, s)

        def one(i, carry):
            valid = jnp.where(i == 0, first, jnp.where(i == 1, second, own))
            shard = jnp.where(i == 0, first_shard, jnp.where(i == 1, second_shard, me))

            @pl.when(valid)
            def _():
                act(it, shard, c)

            return carry

        lax.fori_loop(0, 3, one, 0)

    def pre_gradient(it):
        total = gram_sum[:r, :] + gram_sum[r:, :]
        square = total[:, hl : hl + r] + total[:, hl + r :]
        now = mixed[...]
        d_mixed = jnp.dot(square, now, precision=HIGHEST, preferred_element_type=F32) - total[:, :hl]
        value = d_mixed * scale * (1.0 - now * now)
        for q in range(quarters):
            d_pre[it, mine, q] = value[:, q * 128 : (q + 1) * 128]

    def loss_close(it):
        total = loss_sum[:, 0:128]
        for q in range(128, hl, 128):
            total = total + loss_sum[:, q : q + 128]
        loss_in[mine, it * 8 : it * 8 + 8, :] = total
        loss_sum[...] = jnp.zeros_like(loss_sum)

    def combine(c_ref, it, k, q):
        total = c_ref[0, pl.ds(k, 1), :] * d_pre[it, 0, q]
        for e in range(1, experts):
            total = total + c_ref[e, pl.ds(k, 1), :] * d_pre[it, e, q]
        return total

    def columns(q):
        return slice(q * 128, (q + 1) * 128)

    def coef_pass(it, which):
        def one(k, carry):
            sums = [jnp.zeros((8, 128), F32)] * experts
            for q in which:
                values = bases[k, :, columns(q)]
                for e in range(experts):
                    held = values * d_pre[it, e, q]
                    sums[e] = sums[e] + jnp.sum(held.reshape(r // 8, 8, 128), axis=0)
            for e in range(experts):
                at = pl.ds(e * k_count + k, 1)
                value = jnp.sum(sums[e], axis=0, keepdims=True)
                coef_acc[at, :] = value if 0 in which else coef_acc[at, :] + value
            return carry

        lax.fori_loop(0, k_count, one, 0)

    def coef_send(it, losses=None):
        message[it, me] = jnp.zeros(message.shape[2:], F32)
        for i in range(blocks):
            column = jnp.sum(coef_acc[i * block : (i + 1) * block, :], axis=1, keepdims=True)
            message[it, me, i : i + 1, :] = to_lanes(jnp.broadcast_to(column, (block, 128)))
        if losses is not None:
            message[it, me, blocks : blocks + 1, :] = to_lanes(
                jnp.concatenate([lane_sums(losses[:8]), lane_sums(losses[8:])], axis=0)
            )
        for off in range(1, n):
            coef_copy(it, off).start()

    def coef_wait(it):
        for off in range(1, n):
            coef_copy(it, off).wait()

    def message_sum(it):
        total = message[it, 0]
        for c in range(1, n):
            total = total + message[it, c]
        return total

    def coef_table(total):
        held = [to_rows(total[i : i + 1, :], block) for i in range(blocks)]
        held = held[0] if blocks == 1 else jnp.concatenate(held, axis=0)
        return held.reshape(experts, k_count, 128)

    def bases_one(low, high):
        def one(k, carry):
            for q in range(quarters):
                gradient = combine(c_one, 0, k, q)
                b_grad[k, :, columns(q)] = ROOT_ONE * gradient
                bases[k, :, columns(q)] = adam_first(bases[k, :, columns(q)], gradient)
            return carry

        lax.fori_loop(low, high, one, 0)

    def bases_two(q):
        def one(k, carry):
            values = bases[k, :, columns(q)]
            bases[k, :, columns(q)] = adam_second(values, b_grad[k, :, columns(q)], combine(c_root, 1, k, q))
            return carry

        lax.fori_loop(0, k_count, one, 0, unroll=2)

    def factor_product(it, c):
        return jnp.dot(
            full[it, rows_of(me, c), :], gram[...], precision=HIGHEST, preferred_element_type=F32
        )

    def factor_one(c):
        at = chunk_of(c)
        g = (factor_product(0, c) - part[me, at, :]) * scale
        g_one[at, :] = ROOT_ONE * g
        full[1, rows_of(me, c), :] = adam_first(full[0, rows_of(me, c), :], g)

    def factor_two(c):
        at = chunk_of(c)
        g = (full[0, rows_of(me, c), :] - part[me, at, :]) * (ROOT_TWO * scale)
        f_out[at, :] = adam_second(full[1, rows_of(me, c), :], g_one[at, :], g)

    scope = jax.named_scope
    with scope("enter"):
        give_first(1)
        give_first(0)
    misc[...] = jnp.zeros_like(misc)
    loads[2].wait()
    misc[0:1, :k_count] = c_raw[...]
    c_one[mine] = to_rows(misc[0:1, :], k_count)
    gram_sum[...] = jnp.zeros_like(gram_sum)
    loss_sum[...] = jnp.zeros_like(loss_sum)
    with scope("load"):
        loads[1].wait()
    with scope("mix"):
        mix(c_one)
        gram_local()
    with scope("project"):
        for j in range(n):
            if j % (n // halves) == 0:
                loads[3 + j // (n // halves)].wait()
            project(j)

    with scope("greet"):
        @pl.when(me == 0)
        def _():
            pl.semaphore_wait(barrier, experts - 1)

        @pl.when(me > 0)
        def _():
            pl.semaphore_wait(known, 1)

        @pl.when(me < n - 1)
        def _():
            greet_experts(above)
            pl.semaphore_wait(above, experts - 1)
            pl.semaphore_signal(known, inc=1, device_id={"col": me + 1}, device_id_type=MESH)

    expert_start(c_one)
    loads[0].wait()
    final = phase - chunks + LAG

    def early(s, carry):
        gram_hop(0, s, LAG)
        with scope("step"):
            step(s)
        own = s - LAG < chunks
        for_arrived(absorb, 0, s - LAG, own)
        for_arrived(loss_add, 0, s - LAG, own)
        return carry

    lax.fori_loop(LAG, final, early, 0)
    with scope("pre"):
        pre_gradient(0)
        expert_wait(c_one)
        pre_start(0)
        gram_close(0)
        loss_close(0)
        gram_sum[...] = jnp.zeros_like(gram_sum)

    def base_work(i):
        if i == 0:
            with scope("forward"):
                pre_forward(0, 0)
        elif i == 1:
            with scope("wait"):
                pre_wait(0, 0)
            with scope("coef"):
                coef_pass(0, range(quarters))
                coef_send(0)
        elif i == 2:
            with scope("bases"):
                bases_one(0, k_count // 2)
        else:
            with scope("bases"):
                bases_one(k_count // 2, k_count)

    for c in range(chunks):
        with scope("step"):
            step(final + c)
        factor_one(c)
        absorb(1, me, c)
        base_work(c)

    begin = phase + chunks
    behind = begin - phase - LAG
    for s in range(final + chunks, begin):
        with scope("step"):
            step(s)
        for_arrived(absorb, 1, s - LAG, False)
    with scope("await"):
        coef_wait(0)
    c_grad[...] = coef_table(message_sum(0))
    c_two[...] = adam_first(c_one[...], c_grad[...])
    c_root[...] = ROOT_TWO * c_two[...]
    with scope("mix"):
        mix(c_two)
        gram_local()
    with scope("project"):
        for j in range(n):
            project(j)

    def late(s, carry):
        gram_hop(1, s, begin)
        with scope("step"):
            step(s)
        for_arrived(absorb, 1, s - LAG, False)
        for_arrived(loss_add, 1, s - LAG - behind, False)

        @pl.when(s - begin < chunks)
        def _():
            loss_add(1, me, s - begin)

        return carry

    end = phase + final
    lax.fori_loop(begin, end, late, 0)
    with scope("pre"):
        pre_gradient(1)
        pre_start(1)
        gram_close(1)
    with scope("product"):
        for c in range(chunks):
            full[0, rows_of(me, c), :] = factor_product(1, c)
    for s in range(end - LAG - behind, end - LAG):
        for_arrived(loss_add, 1, s, False)
    loss_close(1)
    expert_start(loss_in)
    with scope("forward"):
        pre_forward(1, 0)
    with scope("step"):
        take(end)
    factor_two(0)
    with scope("wait"):
        pre_wait(1, 0)
    with scope("coef"):
        coef_pass(1, range(width))
    with scope("forward"):
        for q in range(1, quarters // width):
            pre_forward(1, q)
    with scope("bases"):
        bases_two(0)
    with scope("wait"):
        for q in range(1, quarters // width):
            pre_wait(1, q)
    with scope("coef"):
        if quarters > width:
            coef_pass(1, range(width, quarters))
        expert_wait(loss_in)
        losses = loss_in[0]
        for e in range(1, experts):
            losses = losses + loss_in[e]
        coef_send(1, losses)
    give(end)
    for q in range(1, quarters):
        with scope("bases"):
            bases_two(q)
        if q < chunks - 1:
            with scope("step"):
                take(end + q)
            factor_two(q)
    for c in range(max(quarters, 1), chunks - 1):
        take(end + c)
        factor_two(c)
    with scope("await"):
        coef_wait(1)
    with scope("coefs"):
        total = message_sum(1)
        own = pl.ds(mine * k_count, k_count)
        coef_acc[...] = coef_table(total).reshape(table, 128)
        misc[0:1, :] = to_lanes(adam_second(c_two[mine], ROOT_ONE * c_grad[mine], ROOT_TWO * coef_acc[own, :]))
        misc[1:2, :] = total[blocks : blocks + 1, :] * loss_scale
    with scope("step"):
        take(end + chunks - 1)
    with scope("factor"):
        factor_two(chunks - 1)


def hand_over(b_in, f_in, misc, b_out, f_out, c_out, l_out, c_held, l_held, sem):
    copies = [
        pltpu.make_async_copy(f_in, f_out, sem.at[0]),
        pltpu.make_async_copy(b_in, b_out, sem.at[1]),
        pltpu.make_async_copy(c_held, c_out, sem.at[2]),
        pltpu.make_async_copy(l_held, l_out, sem.at[3]),
    ]
    for copy in copies[:2]:
        copy.start()
    c_held[...] = misc[0:1, : c_out.shape[1]]
    for i in range(2):
        l_held[i] = misc[1, 8 * i]
    for copy in copies[2:]:
        copy.start()
    for copy in copies:
        copy.wait()


def shards(target_weights, factors, bases, coefficients):
    n, experts = lax.axis_size("col"), lax.axis_size("expert")
    _, d, hl = target_weights.shape
    _, rows, r = factors.shape
    k = bases.shape[0]
    held = pl.BlockSpec(memory_space=pltpu.HBM)
    local = pl.BlockSpec(memory_space=pltpu.VMEM)
    dma = pltpu.SemaphoreType.DMA
    loss_scale = 1.0 / (2.0 * experts * d * hl * n)
    new_factors, new_bases, misc = pl.pallas_call(
        functools.partial(kernel, n, experts, loss_scale),
        out_shape=(
            pltpu.VMEM((rows, r), F32),
            pltpu.VMEM(bases.shape, F32),
            pltpu.VMEM((8, 128), F32),
        ),
        in_specs=[held, held, held, held],
        out_specs=(local, local, local),
        scratch_shapes=[
            pltpu.VMEM((d, hl), BF16),
            pltpu.VMEM(bases.shape, F32),
            pltpu.VMEM((2, d, r), F32),
            pltpu.VMEM((n, rows, r), F32),
            pltpu.VMEM((2, n - 1, rows, r), F32),
            pltpu.VMEM((2, experts, hl // 128, r, 128), F32),
            pltpu.VMEM((experts, k, 128), F32),
            pltpu.VMEM((experts, k, 128), F32),
            pltpu.VMEM((experts, k, 128), F32),
            pltpu.VMEM((experts, k, 128), F32),
            pltpu.VMEM((experts * k, 128), F32),
            pltpu.VMEM((2, n, experts * k // min(experts * k, 128) + 1, 128), F32),
            pltpu.VMEM((experts, 16, 128), F32),
            pltpu.VMEM((rows, r), F32),
            pltpu.VMEM((2 * r, hl + 2 * r), F32),
            pltpu.VMEM((r, hl), F32),
            pltpu.VMEM((4 * r, hl), BF16),
            pltpu.VMEM((8, hl), F32),
            pltpu.VMEM((r, r), F32),
            pltpu.VMEM((r // 2 + 8, r), F32),
            pltpu.VMEM((2, 2, r // 2 + 8, r), F32),
            pltpu.VMEM((2, 2, r // 2 + 8, r), F32),
            pltpu.VMEM((1, k), F32),
            pltpu.SemaphoreType.REGULAR,
            pltpu.SemaphoreType.REGULAR,
            pltpu.SemaphoreType.REGULAR,
            dma((5,)),
            dma((2, LAG)),
            dma((2, 2 * LAG)),
            dma((2,)),
            dma((2,)),
            dma((experts - 1,)),
            dma((experts - 1,)),
            dma((1 + hl // 128 // (2 if hl % 256 == 0 else 1), experts - 1)),
            dma((1 + hl // 128 // (2 if hl % 256 == 0 else 1), experts - 1)),
            dma((n - 1,)),
            dma((n - 1,)),
        ],
        compiler_params=pltpu.CompilerParams(
            collective_id=0, has_side_effects=True, vmem_limit_bytes=VMEM_MAIN
        ),
    )(target_weights[0], factors[0], bases, coefficients)
    new_bases, new_factors, new_coef, losses = pl.pallas_call(
        hand_over,
        out_shape=(
            jax.ShapeDtypeStruct(bases.shape, F32),
            jax.ShapeDtypeStruct((rows, r), F32),
            jax.ShapeDtypeStruct((1, k), F32),
            jax.ShapeDtypeStruct((2,), F32),
        ),
        in_specs=[local, local, local],
        out_specs=(held, held, held, held),
        scratch_shapes=[pltpu.VMEM((1, k), F32), pltpu.SMEM((2,), F32), dma((4,))],
        compiler_params=pltpu.CompilerParams(vmem_limit_bytes=VMEM_LAST),
    )(new_bases, new_factors, misc)
    return (new_factors[None], new_bases, new_coef, losses)


def solution(mesh):
    return jax.shard_map(
        shards,
        mesh=mesh,
        in_specs=(
            P(("layer", "expert"), None, "col"),
            P(("layer", "expert"), "col", None),
            P("layer", None, "col"),
            P(("layer", "expert"), None),
        ),
        out_specs=(
            P(("layer", "expert"), "col", None),
            P("layer", None, "col"),
            P(("layer", "expert"), None),
            P("layer"),
        ),
        check_vma=False,
    )
```
